32 devices in a mesh: tile: 16 (over z, y, x), depth: 2 (over core).
Axes of the slice: x: 2, y: 2, z: 4, core: 2. Of those that a mesh axis runs over, the one named last changes fastest.
Arguments:
- density: float32 [64, 256, 256], P('depth', 'tile'), may hold values from -6 to 6
- absorption: float32 [256, 256], P('tile'), may hold values from 0.25 to 32
- view_dir: int32 [256], P('tile'), may hold values 0 or 1
- target_ids: int32 [256, 256], P('tile'), may hold values from 0 to 127
- palette: float32 [3, 128], replicated, may hold values from -3 to 3
- emission_coef: float32 [3, 4], replicated, may hold values from -3 to 3
- light: float32 [3], replicated, may hold values from -4 to 4
Outputs:
- image: float32 [3, 256, 256], P(None, ('tile', 'depth'))
- density_grad: float32 [64, 256, 256], P('depth', 'tile')
The draws below stay inside these ranges and needn't reach their ends.
All inputs are finite; a program needn't handle non-finite values. No bound on the sum of `view_dir` on one device may be relied on, other than what follows from the above.
Results may differ from the reference program's by a relative error of at most 0.00023.
Values sent between devices are 32-bit elements; how exact they have to be, the bound alone decides.
No kernel may reach another device: no remote copies, remote signals or barrier semaphores. Data moves between devices by JAX's collectives and lax.ppermute only.
A program may use at most 64 MiB of HBM per device.

```python
import math
import jax
import jax.numpy as jnp
import numpy as np
from jax import lax

COLS = 256
PALETTE = 128
NZ = 64
NY = 256


def set_ends(drawn, key, smallest, top_value):
    longest = drawn.shape.index(max(drawn.shape))
    spots = []
    for shift in (0, 1):
        where = [jax.random.randint(jax.random.fold_in(key, axis), (), 0, length) for axis, length in enumerate(drawn.shape)]
        where[longest] = (where[longest] + shift) % drawn.shape[longest]
        spots.append(tuple(where))
    return drawn.at[spots[0]].set(smallest).at[spots[1]].set(top_value)


def shard_levels(own_key, shape, shards, low, high):
    loudness = 1.0
    for dim, shards_of in shards:
        steps = jax.random.uniform(jax.random.fold_in(jax.random.fold_in(own_key, 6), dim), (shards_of,), jnp.float32, low / len(shards), high / len(shards))
        loudness = loudness * jnp.repeat(jnp.exp(steps), shape[dim] // shards_of).reshape((-1,) + (1,) * (len(shape) - 1 - dim))
    return loudness


def cumulative_ranks(number_of, skew):
    loads = [(1 << 20) // math.isqrt(standing ** skew) + 1 for standing in range(1, number_of + 1)]
    scale = 1 + sum(loads) // (1 << 30)
    return np.cumsum(np.array([max(1, weight // scale) for weight in loads]))


def skewed_ids(rng, dims, count, slope):
    grid = cumulative_ranks(count, slope)
    ticket = jax.random.randint(jax.random.fold_in(rng, 1), dims, 0, int(grid[count - 1]))
    standing = jnp.searchsorted(jnp.asarray(grid, jnp.int32), ticket, side="right")
    return jax.random.permutation(jax.random.fold_in(rng, 2), count)[standing].astype(jnp.int32)


def bell_draw(rng, extent, width, most, pieces=(), dtype=jnp.bfloat16):
    entries = width * jax.random.normal(rng, extent, jnp.float32)
    if pieces:
        entries = entries * shard_levels(rng, extent, pieces, -0.22, 0.18)
    return jnp.clip(entries, -most, most).astype(dtype)


def setup_inputs(seed: int = 0) -> dict:
    key_of = jax.random.split(jax.random.key(seed), 8)
    density = bell_draw(key_of[0], (NZ, NY, COLS), 1.0, 6.0, ((0, 2), (1, 16)), jnp.float32)
    absorption = jnp.clip(jnp.exp(math.log(32.0) - 4.8520303 * jax.random.uniform(key_of[1], (NY, COLS), jnp.float32) ** shard_levels(key_of[1], (NY, COLS), ((0, 16),), -0.2, 0.2)), 0.25, 32.0)
    view_dir = set_ends((jax.random.randint(key_of[2], (NY,), 0, 2) < 1).astype(jnp.int32), jax.random.fold_in(key_of[2], 1), 0, 1)
    target_ids = set_ends(skewed_ids(key_of[3], (NY, COLS), PALETTE, 2), jax.random.fold_in(key_of[3], 3), 0, PALETTE - 1).astype(jnp.int32)
    palette = bell_draw(key_of[4], (3, PALETTE), 0.5, 3.0, (), jnp.float32)
    emission_coef = bell_draw(key_of[5], (3, 4), 0.5, 3.0, (), jnp.float32)
    light = bell_draw(key_of[6], (3,), 1.0, 4.0, (), jnp.float32)
    return dict(density=density, absorption=absorption, view_dir=view_dir, target_ids=target_ids, palette=palette, emission_coef=emission_coef, light=light)


def smooth_field(ext):
    core = ext[1:-1, 1:-1]
    total = 2.0 * core + ext[2:, 1:-1] + ext[:-2, 1:-1] + ext[1:-1, 2:] + ext[1:-1, :-2]
    total = total + jnp.roll(core, -1, 2) + jnp.roll(core, 1, 2)
    return total / 8.0

def shade_parts(padded, absorption, emission_coef, light, depth_count):
    smoothed = smooth_field(padded)
    centre = smoothed[1:-1, 1:-1]
    grad_z = 0.5 * (smoothed[2:, 1:-1] - smoothed[:-2, 1:-1])
    grad_y = 0.5 * (smoothed[1:-1, 2:] - smoothed[1:-1, :-2])
    grad_x = 0.5 * (jnp.roll(centre, -1, 2) - jnp.roll(centre, 1, 2))
    facing = grad_z * light[0] + grad_y * light[1] + grad_x * light[2]
    shade = 0.5 + 0.5 * facing / jnp.sqrt(1.0 + grad_z * grad_z + grad_y * grad_y + grad_x * grad_x)
    value = emission_coef[:, 3][:, None, None, None] * centre[None] + emission_coef[:, 2][:, None, None, None]
    value = value * centre[None] + emission_coef[:, 1][:, None, None, None]
    value = value * centre[None] + emission_coef[:, 0][:, None, None, None]
    emission = value * shade[None]
    sigma = absorption[None] * jax.nn.softplus(centre) / depth_count
    return (emission, sigma)

def reference(density, absorption, view_dir, target_ids, palette, emission_coef, light):
    depth_count = density.shape[0]
    flipped = (view_dir == 1)[None, :, None]

    def render(field):
        padded = jnp.pad(field, ((2, 2), (2, 2), (0, 0)))
        emission, sigma = shade_parts(padded, absorption, emission_coef, light, depth_count)
        ascending = jnp.cumsum(sigma, 0) - sigma
        total = lax.optimization_barrier(jnp.sum(sigma, 0))
        descending = total[None] - ascending - sigma
        depth_before = jnp.where(flipped, descending, ascending)
        weight = jnp.exp(-depth_before) * (1.0 - jnp.exp(-sigma))
        return lax.optimization_barrier(jnp.sum(emission * weight[None], 1))
    image, pullback = jax.vjp(render, density)
    target = palette[:, target_ids]
    density_grad, = pullback((image - target) * depth_count)
    return (image, density_grad)
```

```python
import functools

import jax
import jax.numpy as jnp
from jax import lax
from jax.experimental import pallas as pl
from jax.experimental.pallas import tpu as pltpu
from jax.sharding import PartitionSpec as P

F32 = jnp.float32
HALO = 4
PIX = 3
VMEM = pl.BlockSpec(memory_space=pltpu.VMEM)
SMEM = pl.BlockSpec(memory_space=pltpu.SMEM)


def call(kernel, outs, args, specs, scratch=(), cost=None):
    args = [pltpu.with_memory_space_constraint(a, pltpu.VMEM) if s is VMEM else a for a, s in zip(args, specs)]
    return pl.pallas_call(
        kernel,
        out_shape=outs,
        in_specs=specs,
        out_specs=jax.tree.map(lambda _: VMEM, outs),
        scratch_shapes=scratch,
        cost_estimate=cost,
        compiler_params=pltpu.CompilerParams(vmem_limit_bytes=8 << 20),
    )(*args)


def resident(*shape):
    return pltpu.VMEM(shape, F32)


def where_am_i():
    return lax.axis_index("depth"), lax.rem(lax.axis_index("tile"), 2)


def local_plane(core, nz, z):
    return jnp.where(core == 0, z, nz - 1 - z)


def prep_kernel(dens, absorb, ids, view, zmsg, xmsg, lmsg, pix):
    nz, rows, cols = dens.shape
    core, odd = where_am_i()
    row = lax.broadcasted_iota(jnp.int32, (rows, cols), 0)
    seen = jnp.zeros((rows, cols), F32)
    for r in range(rows):
        seen = jnp.where(row == r, view[r].astype(F32), seen)
    pix[0] = absorb[...]
    pix[1] = ids[...].astype(F32)
    pix[2] = seen

    def edges(plane, x_to, l_to):
        head, tail = plane[:HALO], plane[rows - HALO :]
        xmsg[x_to] = jnp.where(odd == 1, head, tail)
        lmsg[l_to] = jnp.where(odd == 1, tail, head)

    for j in range(nz):
        plane = dens[local_plane(core, nz, nz - 1 - j)]
        edges(plane, j, j)
        if j < HALO:
            zmsg[j] = plane
    for j in range(PIX):
        edges(pix[j], nz + j, nz + j)


def corner_kernel(zrecv, early, lmsg):
    rows = zrecv.shape[1]
    _, odd = where_am_i()
    lmsg[HALO:] = early[...]
    for j in range(HALO):
        plane = zrecv[HALO - 1 - j]
        lmsg[j] = jnp.where(odd == 1, plane[rows - HALO :], plane[:HALO])


def lookup(palette, ids):
    rows, cols = ids.shape
    entries = palette.shape[1]
    index = ids.astype(jnp.int32)
    parts = []
    for c in range(3):
        strips = []
        for r in range(0, rows, 8):
            strip = []
            for x in range(0, cols, entries):
                table = jnp.broadcast_to(palette[c : c + 1, :], (8, entries))
                strip.append(jnp.take_along_axis(table, index[r : r + 8, x : x + entries], axis=1))
            strips.append(jnp.concatenate(strip, axis=1))
        parts.append(jnp.concatenate(strips, axis=0))
    return parts


def forward_block(band, depth, own, halo, shift, light, coef, out):
    core, _ = where_am_i()
    wide = band + 8
    smooth, dxs, dys, rnorm, phis, edge, sig, taus, mid, pixo = out

    def gather(o, h):
        return pltpu.roll(jnp.concatenate([o, h, h], axis=0), shift, axis=0)

    a, ids, view = [gather(own(-1 - j), halo(-1 - j))[:band] for j in range(PIX)]
    back = jnp.where(core == 0, view, 1.0 - view)
    sign = 1.0 - 2.0 * back
    scale = a * (1.0 / (2 * depth))
    pixo[0] = a
    pixo[1] = ids
    pixo[2] = back
    signed = scale * sign

    def smoothing(before, here, after):
        t = before + after + 2.0 * here
        t = t + pltpu.roll(here, 1, axis=0) + pltpu.roll(here, wide - 1, axis=0)
        cols = here.shape[1]
        t = t + pltpu.roll(here, 1, axis=1) + pltpu.roll(here, cols - 1, axis=1)
        return t * 0.125

    def optical(z, s):
        e = jnp.exp(s)
        soft = jnp.log(1.0 + e)
        sig[z] = 1.0 - jnp.exp(-soft)
        tau = signed * soft
        taus[z] = tau
        return tau

    first = gather(own(0), halo(0))
    zero = jnp.zeros_like(first)
    smooth[0] = first * 0.125

    def smooth_step(z, carry):
        before, here, total = carry
        after = gather(own(z + 1), halo(z + 1))
        s = smoothing(before, here, after)
        smooth[z + 1] = s
        return here, after, total + optical(z, s[:band])

    carry = (zero, first, jnp.zeros_like(a))
    carry = lax.fori_loop(0, depth - 1, smooth_step, carry)
    before, here, total = smooth_step_seam(depth - 1, carry, own, halo, gather, smoothing, smooth, optical, band)
    tot = total
    for z in range(depth, depth + 3):
        after = gather(own(z + 1), halo(z + 1))
        s = smoothing(before, here, after)
        smooth[z + 1] = s
        if z < depth + 2:
            optical(z, s[:band])
        before, here = here, after

    start = jnp.where(back == 1.0, tot, 0.0)
    lz = jnp.where(core == 0, light[0], -light[0])
    ly, lx = light[1], light[2]
    first_edge = jnp.exp(start)
    edge[0] = first_edge

    def shade_step(z, carry):
        run, seen, m0, m1, m2, m3 = carry
        wide_s = smooth[z + 1]
        cols = wide_s.shape[1]
        s = wide_s[:band]
        dz = smooth[z + 2, pl.ds(0, band)] - smooth[z, pl.ds(0, band)]
        dy = (pltpu.roll(wide_s, wide - 1, axis=0) - pltpu.roll(wide_s, 1, axis=0))[:band]
        dx = pltpu.roll(s, cols - 1, axis=1) - pltpu.roll(s, 1, axis=1)
        r = lax.rsqrt(4.0 + dz * dz + dy * dy + dx * dx)
        phi = (dz * lz + dy * ly + dx * lx) * r
        dxs[z] = dx
        dys[z] = dy
        rnorm[z] = r
        phis[z] = phi
        run = run - taus[z]
        nxt = jnp.exp(run)
        edge[z + 1] = nxt
        b = (seen - nxt) * (1.0 + phi)
        m0 = m0 + b
        b = b * s
        m1 = m1 + b
        b = b * s
        m2 = m2 + b
        b = b * s
        m3 = m3 + b
        return run, nxt, m0, m1, m2, m3

    nil = jnp.zeros_like(a)
    carry = (start, first_edge, nil, nil, nil, nil)
    carry = lax.fori_loop(0, depth, shade_step, carry)
    _, _, m0, m1, m2, m3 = carry
    half = 0.5 * sign
    mid[0] = sign * tot
    for c in range(3):
        mid[1 + c] = half * (m0 * coef[c, 0] + m1 * coef[c, 1] + m2 * coef[c, 2] + m3 * coef[c, 3])
    shade_step(depth, carry)
    shade_step(depth + 1, (carry[0] - taus[depth], *carry[1:]))


def smooth_step_seam(z, carry, own, halo, gather, smoothing, smooth, optical, band):
    before, here, total = carry
    after = gather(own(z + 1), halo(z + 1))
    s = smoothing(before, here, after)
    smooth[z + 1] = s
    return here, after, total + optical(z, s[:band])


def main_forward_kernel(dens, pix, zrecv, xrecv, xcorner, light, coef, *out):
    nz, rows, cols = dens.shape
    core, odd = where_am_i()

    def own(z):
        if isinstance(z, int):
            if z < 0:
                return pix[-1 - z]
            if z >= nz:
                return zrecv[z - nz]
        return dens[local_plane(core, nz, z)]

    def halo(z):
        if isinstance(z, int):
            if z < 0:
                return xrecv[nz - 1 - z]
            if z >= nz:
                return xcorner[z - nz]
        return xrecv[nz - 1 - z]

    shift = jnp.where(odd == 1, 2, rows + 8 - 2)
    forward_block(rows, nz, own, halo, shift, light, coef, out)


def far_forward_kernel(dens, pix, zrecv, lrecv, light, coef, *out):
    nz, rows, cols = dens.shape
    core, odd = where_am_i()
    at = pl.multiple_of(odd * (rows - 8), 8)

    def own(z):
        if isinstance(z, int):
            if z < 0:
                return pix[-1 - z, pl.ds(at, 8)]
            if z >= nz:
                return zrecv[z - nz, pl.ds(at, 8)]
        return dens[local_plane(core, nz, z), pl.ds(at, 8)]

    def halo(z):
        if isinstance(z, int) and z < 0:
            return lrecv[nz + HALO - 1 - z]
        return lrecv[nz + HALO - 1 - z]

    shift = jnp.where(odd == 1, 16 - 2, 2)
    forward_block(8, nz, own, halo, shift, light, coef, out)


def backward_block(band, depth, res, theirs, palette, light, coef, grads, image, emit):
    core, _ = where_am_i()
    smooth, dxs, dys, rnorm, phis, edge, sig, taus, mid, pixo = res
    back = pixo[2] == 1.0
    sign = jnp.where(back, -1.0, 1.0)
    mine_total, their_total = mid[0], theirs[0]
    through_me, through_them = jnp.exp(-mine_total), jnp.exp(-their_total)
    target = lookup(palette, pixo[1])
    g, flow = [], jnp.zeros_like(sign)
    for c in range(3):
        mine, other = mid[1 + c], theirs[1 + c]
        pic = jnp.where(back, other + through_them * mine, mine + through_me * other)
        image[c] = pic
        err = (pic - target[c]) * (2.0 * depth)
        g.append(err)
        flow = flow + err * pic
    kappa = jnp.where(back, 0.5 * through_them, 0.5)
    gam = [kappa * (g[0] * coef[0, k] + g[1] * coef[1, k] + g[2] * coef[2, k]) for k in range(4)]
    gam2, gam3 = 2.0 * gam[2], 3.0 * gam[3]
    queue = jnp.where(back, 0.0, -flow)
    weight = pixo[0] * (1.0 / (2 * depth))
    lz = jnp.where(core == 0, light[0], -light[0])
    ly, lx = light[1], light[2]

    def shade_back(z, carry):
        run, part, last = carry
        s = smooth[z + 1, pl.ds(0, band)]
        cols = s.shape[1]
        dz = smooth[z + 2, pl.ds(0, band)] - smooth[z, pl.ds(0, band)]
        phi, r, near, far = phis[z], rnorm[z], edge[z], edge[z + 1]
        shade = 1.0 + phi
        poly = gam[0] + s * (gam[1] + s * (gam[2] + s * gam[3]))
        slope = gam[1] + s * (gam2 + s * gam3)
        h = shade * poly
        lost = near - far
        w = sign * lost
        mine = (near * h + run) * (weight * sig[z]) + (w * shade) * slope
        run = run + lost * h
        t1 = w * poly * r
        t3 = t1 * phi * r
        az = t1 * lz - t3 * dz
        ay = t1 * ly - t3 * dys[z]
        ax = t1 * lx - t3 * dxs[z]
        grads[z] = part - az
        part = mine + last
        part = part + (pltpu.roll(ay, 1, axis=0) - pltpu.roll(ay, band - 1, axis=0))
        part = part + (pltpu.roll(ax, 1, axis=1) - pltpu.roll(ax, cols - 1, axis=1))
        return run, part, az

    nil = jnp.zeros_like(sign)
    lax.fori_loop(0, depth + 2, shade_back, (queue, nil, nil))

    def smooth_back(z, carry):
        here = grads[z + 1]
        cols = here.shape[1]
        t = grads[z] + grads[z + 2] + 2.0 * here
        t = t + pltpu.roll(here, 1, axis=0) + pltpu.roll(here, band - 1, axis=0)
        t = t + pltpu.roll(here, 1, axis=1) + pltpu.roll(here, cols - 1, axis=1)
        emit(z, t * 0.125)
        return carry

    lax.fori_loop(0, depth, smooth_back, 0)


def main_backward_kernel(*refs):
    res, (theirs, palette, light, coef, out, image, grads) = refs[:10], refs[10:]
    nz, rows, cols = out.shape
    core, odd = where_am_i()
    shift = jnp.where(odd == 1, rows - 2, 2)

    def emit(z, value):
        out[local_plane(core, nz, z)] = pltpu.roll(value, shift, axis=0)

    backward_block(rows, nz, res, theirs, palette, light, coef, grads, image, emit)


def far_backward_kernel(*refs):
    res = refs[:10]
    theirs, palette, light, coef, near_grad, near_image, picture, out, image, grads = refs[10:]
    nz, rows, cols = out.shape
    core, odd = where_am_i()
    shift = jnp.where(odd == 1, 2, rows - 2)
    unshift = jnp.where(odd == 1, rows - 2, 2)
    row = lax.broadcasted_iota(jnp.int32, (rows, cols), 0)
    low = odd * (rows - 4)
    mask = (row >= low) & (row < low + 4)

    def emit(z, value):
        at = local_plane(core, nz, z)
        both = pltpu.roll(jnp.concatenate([value, value], axis=0), shift, axis=0)
        out[at] = jnp.where(mask, both, near_grad[at])

    backward_block(8, nz, res, theirs, palette, light, coef, grads, image, emit)
    low = odd * (rows - 2)
    mask2 = (row >= low) & (row < low + 2)
    for c in range(3):
        both = pltpu.roll(jnp.concatenate([image[c], image[c]], axis=0), shift, axis=0)
        whole = jnp.where(mask2, both, pltpu.roll(near_image[c], unshift, axis=0))
        picture[c] = jnp.where(core == 0, whole[:8], whole[8:])


def shards(density, absorption, view_dir, target_ids, palette, emission_coef, light):
    nz, rows, cols = density.shape
    tiles = lax.axis_size("tile")

    sds = resident

    zmsg, xmsg, lmsg, pix = call(
        prep_kernel,
        (sds(HALO, rows, cols), sds(nz + PIX, HALO, cols), sds(nz + PIX, HALO, cols), sds(PIX, rows, cols)),
        (density, absorption, target_ids, view_dir),
        [VMEM, VMEM, VMEM, SMEM],
    )
    swap = [(0, 1), (1, 0)]
    near = [(i, i ^ 1) for i in range(tiles)]
    far = [(i, i + 1 if i % 2 else i - 1) for i in range(1, tiles - 1)]
    zrecv = lax.ppermute(zmsg, "depth", swap)
    xrecv = lax.ppermute(xmsg, "tile", near)
    lmsg = call(corner_kernel, sds(HALO + nz + PIX, HALO, cols), (zrecv, lmsg), [VMEM, VMEM])
    lrecv = lax.ppermute(lmsg, "tile", far)
    xcorner = lax.ppermute(xrecv[:HALO], "depth", swap)

    def residuals(band):
        planes = nz + 2
        return (
            sds(nz + 4, band + 8, cols),
            sds(planes, band, cols),
            sds(planes, band, cols),
            sds(planes, band, cols),
            sds(planes, band, cols),
            sds(planes + 1, band, cols),
            sds(planes, band, cols),
            sds(planes, band, cols),
            sds(4, band, cols),
            sds(PIX, band, cols),
        )

    main = call(
        main_forward_kernel,
        residuals(rows),
        (density, pix, zrecv, xrecv, xcorner, light, emission_coef),
        [VMEM] * 5 + [SMEM] * 2,
    )
    theirs = lax.ppermute(main[8], "depth", swap)
    near_grad, near_image = call(
        main_backward_kernel,
        (sds(nz, rows, cols), sds(3, rows, cols)),
        (*main, theirs, palette, light, emission_coef),
        [VMEM] * 12 + [SMEM] * 2,
        scratch=[pltpu.VMEM((nz + 2, rows, cols), F32)],
    )
    edge = call(
        far_forward_kernel,
        residuals(8),
        (density, pix, zrecv, lrecv, light, emission_coef),
        [VMEM] * 4 + [SMEM] * 2,
    )
    theirs = lax.ppermute(edge[8], "depth", swap)
    picture, grad = call(
        far_backward_kernel,
        (jax.ShapeDtypeStruct((3, 8, cols), F32), jax.ShapeDtypeStruct((nz, rows, cols), F32)),
        (*edge, theirs, palette, light, emission_coef, near_grad, near_image),
        [VMEM] * 12 + [SMEM] * 2 + [VMEM] * 2,
        scratch=[pltpu.VMEM((3, 8, cols), F32), pltpu.VMEM((nz + 2, 8, cols), F32)],
    )
    return picture, grad


def solution(mesh):
    placed = (P("depth", "tile", None), P("tile", None), P("tile"), P("tile", None), P(), P(), P())
    return jax.shard_map(
        shards,
        mesh=mesh,
        in_specs=placed,
        out_specs=(P(None, ("tile", "depth"), None), P("depth", "tile", None)),
        check_vma=False,
    )
```

```python
import functools

import jax
import jax.numpy as jnp
from jax import lax
from jax.experimental import pallas as pl
from jax.experimental.pallas import tpu as pltpu
from jax.sharding import PartitionSpec as P

F32 = jnp.float32
HALO = 4
UNROLL = 8
PIX = 3
VMEM = pl.BlockSpec(memory_space=pltpu.VMEM)
SMEM = pl.BlockSpec(memory_space=pltpu.SMEM)


def call(kernel, outs, args, specs, scratch=(), cost=None):
    args = [pltpu.with_memory_space_constraint(a, pltpu.VMEM) if s is VMEM else a for a, s in zip(args, specs)]
    return pl.pallas_call(
        kernel,
        out_shape=outs,
        in_specs=specs,
        out_specs=jax.tree.map(lambda _: VMEM, outs),
        scratch_shapes=scratch,
        cost_estimate=cost,
        compiler_params=pltpu.CompilerParams(vmem_limit_bytes=8 << 20),
    )(*args)


def resident(*shape):
    return pltpu.VMEM(shape, F32)


def where_am_i():
    return lax.axis_index("depth"), lax.rem(lax.axis_index("tile"), 2)


def local_plane(core, nz, z):
    return jnp.where(core == 0, z, nz - 1 - z)


def prep_kernel(dens, absorb, ids, view, zmsg, xmsg, lmsg, pix):
    nz, rows, cols = dens.shape
    core, odd = where_am_i()
    row = lax.broadcasted_iota(jnp.int32, (rows, cols), 0)
    seen = jnp.zeros((rows, cols), F32)
    for r in range(rows):
        seen = jnp.where(row == r, view[r].astype(F32), seen)
    pix[0] = absorb[...]
    pix[1] = ids[...].astype(F32)
    pix[2] = seen

    def edges(plane, x_to, l_to):
        head, tail = plane[:HALO], plane[rows - HALO :]
        xmsg[x_to] = jnp.where(odd == 1, head, tail)
        lmsg[l_to] = jnp.where(odd == 1, tail, head)

    for j in range(nz):
        plane = dens[local_plane(core, nz, nz - 1 - j)]
        edges(plane, j, j)
        if j < HALO:
            zmsg[j] = plane
    for j in range(PIX):
        edges(pix[j], nz + j, nz + j)


def corner_kernel(zrecv, early, lmsg):
    rows = zrecv.shape[1]
    _, odd = where_am_i()
    lmsg[HALO:] = early[...]
    for j in range(HALO):
        plane = zrecv[HALO - 1 - j]
        lmsg[j] = jnp.where(odd == 1, plane[rows - HALO :], plane[:HALO])


def lookup(palette, ids):
    rows, cols = ids.shape
    entries = palette.shape[1]
    index = ids.astype(jnp.int32)
    parts = []
    for c in range(3):
        strips = []
        for r in range(0, rows, 8):
            strip = []
            for x in range(0, cols, entries):
                table = jnp.broadcast_to(palette[c : c + 1, :], (8, entries))
                strip.append(jnp.take_along_axis(table, index[r : r + 8, x : x + entries], axis=1))
            strips.append(jnp.concatenate(strip, axis=1))
        parts.append(jnp.concatenate(strips, axis=0))
    return parts


def forward_block(band, depth, own, halo, shift, light, coef, out):
    core, _ = where_am_i()
    wide = band + 8
    smooth, dxs, dys, rnorm, phis, edge, sig, taus, mid, pixo = out

    def gather(o, h):
        return pltpu.roll(jnp.concatenate([o, h, h], axis=0), shift, axis=0)

    a, ids, view = [gather(own(-1 - j), halo(-1 - j))[:band] for j in range(PIX)]
    back = jnp.where(core == 0, view, 1.0 - view)
    sign = 1.0 - 2.0 * back
    scale = a * (1.0 / (2 * depth))
    pixo[0] = a
    pixo[1] = ids
    pixo[2] = back
    signed = scale * sign

    def smoothing(before, here, after):
        t = before + after + 2.0 * here
        t = t + pltpu.roll(here, 1, axis=0) + pltpu.roll(here, wide - 1, axis=0)
        cols = here.shape[1]
        t = t + pltpu.roll(here, 1, axis=1) + pltpu.roll(here, cols - 1, axis=1)
        return t * 0.125

    def optical(z, s):
        e = jnp.exp(s)
        soft = jnp.log(1.0 + e)
        sig[z] = 1.0 - jnp.exp(-soft)
        tau = signed * soft
        taus[z] = tau
        return tau

    first = gather(own(0), halo(0))
    zero = jnp.zeros_like(first)
    smooth[0] = first * 0.125

    def smooth_step(z, carry):
        before, here, total = carry
        after = gather(own(z + 1), halo(z + 1))
        s = smoothing(before, here, after)
        smooth[z + 1] = s
        return here, after, total + optical(z, s[:band])

    carry = (zero, first, jnp.zeros_like(a))
    carry = lax.fori_loop(0, depth - 1, smooth_step, carry, unroll=UNROLL)
    before, here, total = smooth_step_seam(depth - 1, carry, own, halo, gather, smoothing, smooth, optical, band)
    tot = total
    for z in range(depth, depth + 3):
        after = gather(own(z + 1), halo(z + 1))
        s = smoothing(before, here, after)
        smooth[z + 1] = s
        if z < depth + 2:
            optical(z, s[:band])
        before, here = here, after

    start = jnp.where(back == 1.0, tot, 0.0)
    lz = jnp.where(core == 0, light[0], -light[0])
    ly, lx = light[1], light[2]
    first_edge = jnp.exp(start)
    edge[0] = first_edge

    def shade_step(z, carry):
        run, seen, m0, m1, m2, m3 = carry
        wide_s = smooth[z + 1]
        cols = wide_s.shape[1]
        s = wide_s[:band]
        dz = smooth[z + 2, pl.ds(0, band)] - smooth[z, pl.ds(0, band)]
        dy = (pltpu.roll(wide_s, wide - 1, axis=0) - pltpu.roll(wide_s, 1, axis=0))[:band]
        dx = pltpu.roll(s, cols - 1, axis=1) - pltpu.roll(s, 1, axis=1)
        r = lax.rsqrt(4.0 + dz * dz + dy * dy + dx * dx)
        phi = (dz * lz + dy * ly + dx * lx) * r
        dxs[z] = dx
        dys[z] = dy
        rnorm[z] = r
        phis[z] = phi
        run = run - taus[z]
        nxt = jnp.exp(run)
        edge[z + 1] = nxt
        b = (seen - nxt) * (1.0 + phi)
        m0 = m0 + b
        b = b * s
        m1 = m1 + b
        b = b * s
        m2 = m2 + b
        b = b * s
        m3 = m3 + b
        return run, nxt, m0, m1, m2, m3

    nil = jnp.zeros_like(a)
    carry = (start, first_edge, nil, nil, nil, nil)
    carry = lax.fori_loop(0, depth, shade_step, carry, unroll=UNROLL)
    _, _, m0, m1, m2, m3 = carry
    half = 0.5 * sign
    mid[0] = sign * tot
    for c in range(3):
        mid[1 + c] = half * (m0 * coef[c, 0] + m1 * coef[c, 1] + m2 * coef[c, 2] + m3 * coef[c, 3])
    shade_step(depth, carry)
    shade_step(depth + 1, (carry[0] - taus[depth], *carry[1:]))


def smooth_step_seam(z, carry, own, halo, gather, smoothing, smooth, optical, band):
    before, here, total = carry
    after = gather(own(z + 1), halo(z + 1))
    s = smoothing(before, here, after)
    smooth[z + 1] = s
    return here, after, total + optical(z, s[:band])


def main_forward_kernel(dens, pix, zrecv, xrecv, xcorner, light, coef, *out):
    nz, rows, cols = dens.shape
    core, odd = where_am_i()

    def own(z):
        if isinstance(z, int):
            if z < 0:
                return pix[-1 - z]
            if z >= nz:
                return zrecv[z - nz]
        return dens[local_plane(core, nz, z)]

    def halo(z):
        if isinstance(z, int):
            if z < 0:
                return xrecv[nz - 1 - z]
            if z >= nz:
                return xcorner[z - nz]
        return xrecv[nz - 1 - z]

    shift = jnp.where(odd == 1, 2, rows + 8 - 2)
    forward_block(rows, nz, own, halo, shift, light, coef, out)


def far_forward_kernel(dens, pix, zrecv, lrecv, light, coef, *out):
    nz, rows, cols = dens.shape
    core, odd = where_am_i()
    at = pl.multiple_of(odd * (rows - 8), 8)

    def own(z):
        if isinstance(z, int):
            if z < 0:
                return pix[-1 - z, pl.ds(at, 8)]
            if z >= nz:
                return zrecv[z - nz, pl.ds(at, 8)]
        return dens[local_plane(core, nz, z), pl.ds(at, 8)]

    def halo(z):
        if isinstance(z, int) and z < 0:
            return lrecv[nz + HALO - 1 - z]
        return lrecv[nz + HALO - 1 - z]

    shift = jnp.where(odd == 1, 16 - 2, 2)
    forward_block(8, nz, own, halo, shift, light, coef, out)


def backward_block(band, depth, res, theirs, palette, light, coef, grads, image, emit):
    core, _ = where_am_i()
    smooth, dxs, dys, rnorm, phis, edge, sig, taus, mid, pixo = res
    back = pixo[2] == 1.0
    sign = jnp.where(back, -1.0, 1.0)
    mine_total, their_total = mid[0], theirs[0]
    through_me, through_them = jnp.exp(-mine_total), jnp.exp(-their_total)
    target = lookup(palette, pixo[1])
    g, flow = [], jnp.zeros_like(sign)
    for c in range(3):
        mine, other = mid[1 + c], theirs[1 + c]
        pic = jnp.where(back, other + through_them * mine, mine + through_me * other)
        image[c] = pic
        err = (pic - target[c]) * (2.0 * depth)
        g.append(err)
        flow = flow + err * pic
    kappa = jnp.where(back, 0.5 * through_them, 0.5)
    gam = [kappa * (g[0] * coef[0, k] + g[1] * coef[1, k] + g[2] * coef[2, k]) for k in range(4)]
    gam2, gam3 = 2.0 * gam[2], 3.0 * gam[3]
    queue = jnp.where(back, 0.0, -flow)
    weight = pixo[0] * (1.0 / (2 * depth))
    lz = jnp.where(core == 0, light[0], -light[0])
    ly, lx = light[1], light[2]

    def shade_back(z, carry):
        run, part, last = carry
        s = smooth[z + 1, pl.ds(0, band)]
        cols = s.shape[1]
        dz = smooth[z + 2, pl.ds(0, band)] - smooth[z, pl.ds(0, band)]
        phi, r, near, far = phis[z], rnorm[z], edge[z], edge[z + 1]
        shade = 1.0 + phi
        poly = gam[0] + s * (gam[1] + s * (gam[2] + s * gam[3]))
        slope = gam[1] + s * (gam2 + s * gam3)
        h = shade * poly
        lost = near - far
        w = sign * lost
        mine = (near * h + run) * (weight * sig[z]) + (w * shade) * slope
        run = run + lost * h
        t1 = w * poly * r
        t3 = t1 * phi * r
        az = t1 * lz - t3 * dz
        ay = t1 * ly - t3 * dys[z]
        ax = t1 * lx - t3 * dxs[z]
        grads[z] = part - az
        part = mine + last
        part = part + (pltpu.roll(ay, 1, axis=0) - pltpu.roll(ay, band - 1, axis=0))
        part = part + (pltpu.roll(ax, 1, axis=1) - pltpu.roll(ax, cols - 1, axis=1))
        return run, part, az

    nil = jnp.zeros_like(sign)
    lax.fori_loop(0, depth + 2, shade_back, (queue, nil, nil), unroll=UNROLL)

    def smooth_back(z, carry):
        here = grads[z + 1]
        cols = here.shape[1]
        t = grads[z] + grads[z + 2] + 2.0 * here
        t = t + pltpu.roll(here, 1, axis=0) + pltpu.roll(here, band - 1, axis=0)
        t = t + pltpu.roll(here, 1, axis=1) + pltpu.roll(here, cols - 1, axis=1)
        emit(z, t * 0.125)
        return carry

    lax.fori_loop(0, depth, smooth_back, 0, unroll=UNROLL)


def main_backward_kernel(*refs):
    res, (theirs, palette, light, coef, out, image, grads) = refs[:10], refs[10:]
    nz, rows, cols = out.shape
    core, odd = where_am_i()
    shift = jnp.where(odd == 1, rows - 2, 2)

    def emit(z, value):
        out[local_plane(core, nz, z)] = pltpu.roll(value, shift, axis=0)

    backward_block(rows, nz, res, theirs, palette, light, coef, grads, image, emit)


def far_backward_kernel(*refs):
    res = refs[:10]
    theirs, palette, light, coef, near_grad, near_image, picture, out, image, grads = refs[10:]
    nz, rows, cols = out.shape
    core, odd = where_am_i()
    shift = jnp.where(odd == 1, 2, rows - 2)
    unshift = jnp.where(odd == 1, rows - 2, 2)
    row = lax.broadcasted_iota(jnp.int32, (rows, cols), 0)
    low = odd * (rows - 4)
    mask = (row >= low) & (row < low + 4)

    def emit(z, value):
        at = local_plane(core, nz, z)
        both = pltpu.roll(jnp.concatenate([value, value], axis=0), shift, axis=0)
        out[at] = jnp.where(mask, both, near_grad[at])

    backward_block(8, nz, res, theirs, palette, light, coef, grads, image, emit)
    low = odd * (rows - 2)
    mask2 = (row >= low) & (row < low + 2)
    for c in range(3):
        both = pltpu.roll(jnp.concatenate([image[c], image[c]], axis=0), shift, axis=0)
        whole = jnp.where(mask2, both, pltpu.roll(near_image[c], unshift, axis=0))
        picture[c] = jnp.where(core == 0, whole[:8], whole[8:])


def shards(density, absorption, view_dir, target_ids, palette, emission_coef, light):
    nz, rows, cols = density.shape
    tiles = lax.axis_size("tile")

    sds = resident

    zmsg, xmsg, lmsg, pix = call(
        prep_kernel,
        (sds(HALO, rows, cols), sds(nz + PIX, HALO, cols), sds(nz + PIX, HALO, cols), sds(PIX, rows, cols)),
        (density, absorption, target_ids, view_dir),
        [VMEM, VMEM, VMEM, SMEM],
    )
    swap = [(0, 1), (1, 0)]
    near = [(i, i ^ 1) for i in range(tiles)]
    far = [(i, i + 1 if i % 2 else i - 1) for i in range(1, tiles - 1)]
    zrecv = lax.ppermute(zmsg, "depth", swap)
    xrecv = lax.ppermute(xmsg, "tile", near)
    lmsg = call(corner_kernel, sds(HALO + nz + PIX, HALO, cols), (zrecv, lmsg), [VMEM, VMEM])
    lrecv = lax.ppermute(lmsg, "tile", far)
    xcorner = lax.ppermute(xrecv[:HALO], "depth", swap)

    def residuals(band):
        planes = nz + 2
        return (
            sds(nz + 4, band + 8, cols),
            sds(planes, band, cols),
            sds(planes, band, cols),
            sds(planes, band, cols),
            sds(planes, band, cols),
            sds(planes + 1, band, cols),
            sds(planes, band, cols),
            sds(planes, band, cols),
            sds(4, band, cols),
            sds(PIX, band, cols),
        )

    main = call(
        main_forward_kernel,
        residuals(rows),
        (density, pix, zrecv, xrecv, xcorner, light, emission_coef),
        [VMEM] * 5 + [SMEM] * 2,
    )
    theirs = lax.ppermute(main[8], "depth", swap)
    near_grad, near_image = call(
        main_backward_kernel,
        (sds(nz, rows, cols), sds(3, rows, cols)),
        (*main, theirs, palette, light, emission_coef),
        [VMEM] * 12 + [SMEM] * 2,
        scratch=[pltpu.VMEM((nz + 2, rows, cols), F32)],
    )
    edge = call(
        far_forward_kernel,
        residuals(8),
        (density, pix, zrecv, lrecv, light, emission_coef),
        [VMEM] * 4 + [SMEM] * 2,
    )
    theirs = lax.ppermute(edge[8], "depth", swap)
    picture, grad = call(
        far_backward_kernel,
        (jax.ShapeDtypeStruct((3, 8, cols), F32), jax.ShapeDtypeStruct((nz, rows, cols), F32)),
        (*edge, theirs, palette, light, emission_coef, near_grad, near_image),
        [VMEM] * 12 + [SMEM] * 2 + [VMEM] * 2,
        scratch=[pltpu.VMEM((3, 8, cols), F32), pltpu.VMEM((nz + 2, 8, cols), F32)],
    )
    return picture, grad


def solution(mesh):
    placed = (P("depth", "tile", None), P("tile", None), P("tile"), P("tile", None), P(), P(), P())
    return jax.shard_map(
        shards,
        mesh=mesh,
        in_specs=placed,
        out_specs=(P(None, ("tile", "depth"), None), P("depth", "tile", None)),
        check_vma=False,
    )
```

```python
import jax
import jax.numpy as jnp
from jax import lax
from jax.experimental import pallas as pl
from jax.experimental.pallas import tpu as pltpu
from jax.sharding import PartitionSpec as P

F32 = jnp.float32
HALO = 4
PIX = 3
GROUP_MAIN = (16,16,16,16)
GROUP_FAR = (16,16,34,32)
LATE = True
VMEM = pl.BlockSpec(memory_space=pltpu.VMEM)
HBM = pl.BlockSpec(memory_space=pl.ANY)


def call(kernel, outs, args, specs, scratch=(), cost=None, out_specs=None):
    args = [pltpu.with_memory_space_constraint(a, pltpu.VMEM if s is VMEM else pltpu.HBM) for a, s in zip(args, specs)]
    return pl.pallas_call(
        kernel,
        out_shape=outs,
        in_specs=specs,
        out_specs=out_specs or jax.tree.map(lambda _: VMEM, outs),
        scratch_shapes=scratch,
        cost_estimate=cost,
        compiler_params=pltpu.CompilerParams(vmem_limit_bytes=8 << 20),
    )(*args)


def resident(*shape):
    return pltpu.VMEM(shape, F32)


def where_am_i():
    return lax.axis_index("depth"), lax.rem(lax.axis_index("tile"), 2)


def local_plane(core, nz, z):
    return jnp.where(core == 0, z, nz - 1 - z)


def in_groups(body, count, group, carry):
    full = count // group
    if full:
        carry = lax.fori_loop(0, full, lambda i, c: body(i * group, group, c), carry)
    if count % group:
        carry = body(full * group, count % group, carry)
    return carry


class Stores:
    def __init__(self):
        self.todo = []

    def put(self, ref, at, value):
        if LATE:
            self.todo.append((ref, at, value))
        else:
            ref[at] = value

    def flush(self):
        for ref, at, value in self.todo:
            ref[at] = value


def spread(par, i, rows, cols):
    t = par[i]
    t = jnp.concatenate([t] * (cols // t.shape[1]), axis=1)
    return jnp.concatenate([t] * (rows // t.shape[0]), axis=0)


def fetch_kernel(dens_h, absorb_h, ids_h, view_h, pal_h, coef_h, light_h, zmsg, dens, pix, pal, par, ids, view, coef, light, sem):
    nz, rows, cols = dens.shape
    core, odd = where_am_i()
    pairs = ((dens_h, dens), (view_h, view), (ids_h, ids), (absorb_h, pix.at[0]), (coef_h, coef), (light_h, light), (pal_h, pal))
    copies = [pltpu.make_async_copy(a, b, sem.at[i]) for i, (a, b) in enumerate(pairs)]
    for c in copies:
        c.start()
    for c in copies[1:]:
        c.wait()
    row = lax.broadcasted_iota(jnp.int32, (rows, cols), 0)
    seen = jnp.zeros((rows, cols), F32)
    for r in range(rows):
        seen = jnp.where(row == r, view[r].astype(F32), seen)
    pix[1] = ids[...].astype(F32)
    pix[2] = seen
    for i in range(3):
        for k in range(4):
            par[4 * i + k] = jnp.full(par.shape[1:], coef[i, k])
        value = light[i]
        if i == 0:
            value = jnp.where(core == 0, value, -value)
        par[12 + i] = jnp.full(par.shape[1:], value)
    copies[0].wait()
    for j in range(HALO):
        zmsg[j] = dens[local_plane(core, nz, nz - 1 - j)]


def edges_kernel(dens, pix, xmsg, lmsg):
    nz, rows, cols = dens.shape
    core, odd = where_am_i()

    def edges(plane, to):
        head, tail = plane[:HALO], plane[rows - HALO :]
        xmsg[to] = jnp.where(odd == 1, head, tail)
        lmsg[to] = jnp.where(odd == 1, tail, head)

    for j in range(PIX):
        edges(pix[j], nz + j)
    for j in range(nz):
        edges(dens[local_plane(core, nz, nz - 1 - j)], j)


def corner_kernel(zrecv, early, lmsg):
    rows = zrecv.shape[1]
    _, odd = where_am_i()
    lmsg[HALO:] = early[...]
    for j in range(HALO):
        plane = zrecv[HALO - 1 - j]
        lmsg[j] = jnp.where(odd == 1, plane[rows - HALO :], plane[:HALO])


def lookup(palette, ids):
    rows, cols = ids.shape
    entries = palette.shape[1]
    index = ids.astype(jnp.int32)
    parts = []
    for c in range(3):
        strips = []
        for r in range(0, rows, 8):
            strip = []
            for x in range(0, cols, entries):
                table = jnp.broadcast_to(palette[c : c + 1, :], (8, entries))
                strip.append(jnp.take_along_axis(table, index[r : r + 8, x : x + entries], axis=1))
            strips.append(jnp.concatenate(strip, axis=1))
        parts.append(jnp.concatenate(strips, axis=0))
    return parts


class Block:
    def __init__(self, band, shift, own, halo):
        self.band, self.shift, self.own, self.halo = band, shift, own, halo

    def plane(self, z):
        h = self.halo(z)
        return pltpu.roll(jnp.concatenate([self.own(z), h, h], axis=0), self.shift, axis=0)


def pixels(block, core, depth):
    a, ids, view = [block.plane(-1 - j)[: block.band] for j in range(PIX)]
    back = jnp.where(core == 0, view, 1.0 - view)
    return a, ids, back


def smooth_planes(block, first, n, signed, depth, smooth, taus, sig, total, lead=None):
    band, wide = block.band, block.band + 8
    out = Stores()
    zs = [first - 1 + i for i in range(n + 2)]
    planes = [lead if i == 0 and lead is not None else block.plane(z) for i, z in enumerate(zs)]
    for i in range(n):
        here = planes[i + 1]
        cols = here.shape[1]
        t = planes[i] + planes[i + 2] + 2.0 * here
        t = t + pltpu.roll(here, 1, axis=0) + pltpu.roll(here, wide - 1, axis=0)
        t = t + pltpu.roll(here, 1, axis=1) + pltpu.roll(here, cols - 1, axis=1)
        s = t * 0.125
        out.put(smooth, zs[i + 1] + 1, s)
        static = isinstance(first, int)
        if not static or first + i < depth + 2:
            soft = jnp.log(1.0 + jnp.exp(s[:band]))
            tau = signed * soft
            out.put(taus, zs[i + 1], tau)
            out.put(sig, zs[i + 1], 1.0 - jnp.exp(-soft))
            if not static or first + i < depth:
                total = total + tau
    out.flush()
    return total


def smooth_slab(block, core, depth, group, smooth, taus, sig, pixo):
    a, ids, back = pixels(block, core, depth)
    signed = a * (1.0 / (2 * depth)) * (1.0 - 2.0 * back)
    pixo[0], pixo[1], pixo[2] = a, ids, back
    face = block.plane(0)
    smooth[0] = face * 0.125
    zero = jnp.zeros_like(face)
    total = smooth_planes(block, 0, 1, signed, depth, smooth, taus, sig, jnp.zeros_like(a), lead=zero)

    def body(z, n, total):
        return smooth_planes(block, z + 1, n, signed, depth, smooth, taus, sig, total)

    return in_groups(body, depth - 2, group, total)


def smooth_seam(block, depth, smooth, taus, sig, pixo, total):
    a, back = pixo[0], pixo[2]
    signed = a * (1.0 / (2 * depth)) * (1.0 - 2.0 * back)
    return smooth_planes(block, depth - 1, 4, signed, depth, smooth, taus, sig, total)


def shade_slab(band, depth, group, total, par, smooth, taus, dxs, dys, rnorm, phis, edge, mid, pixo):
    wide, cols = band + 8, smooth.shape[2]
    back = pixo[2]
    sign = 1.0 - 2.0 * back
    lz, ly, lx = [spread(par, 12 + i, band, cols) for i in range(3)]
    start = jnp.where(back == 1.0, total, 0.0)
    opened = jnp.exp(start)
    edge[0] = opened

    def body(z0, n, carry):
        run, seen, m0, m1, m2, m3 = carry
        out = Stores()
        planes = [smooth[z0 + i] for i in range(n + 2)]
        absorbed = [taus[z0 + i] for i in range(n)]
        for i in range(n):
            here = planes[i + 1]
            s = here[:band]
            dz = planes[i + 2][:band] - planes[i][:band]
            dy = (pltpu.roll(here, wide - 1, axis=0) - pltpu.roll(here, 1, axis=0))[:band]
            dx = pltpu.roll(s, cols - 1, axis=1) - pltpu.roll(s, 1, axis=1)
            r = lax.rsqrt(4.0 + dz * dz + dy * dy + dx * dx)
            phi = (dz * lz + dy * ly + dx * lx) * r
            run = run - absorbed[i]
            nxt = jnp.exp(run)
            for ref, v in ((dxs, dx), (dys, dy), (rnorm, r), (phis, phi)):
                out.put(ref, z0 + i, v)
            out.put(edge, z0 + i + 1, nxt)
            b = (seen - nxt) * (1.0 + phi)
            m0 = m0 + b
            b = b * s
            m1 = m1 + b
            b = b * s
            m2 = m2 + b
            b = b * s
            m3 = m3 + b
            seen = nxt
        out.flush()
        return run, seen, m0, m1, m2, m3

    nil = jnp.zeros_like(back)
    carry = in_groups(body, depth, group, (start, opened, nil, nil, nil, nil))
    _, _, m0, m1, m2, m3 = carry
    half = 0.5 * sign
    mid[0] = sign * total
    for c in range(3):
        k0, k1, k2, k3 = [spread(par, 4 * c + k, band, cols) for k in range(4)]
        mid[1 + c] = half * (m0 * k0 + m1 * k1 + m2 * k2 + m3 * k3)
    body(depth, 2, carry)


def main_block(dens, pix, xrecv, zrecv=None, xcorner=None):
    nz, rows, _ = dens.shape
    core, odd = where_am_i()

    def own(z):
        if isinstance(z, int):
            if z < 0:
                return pix[-1 - z]
            if z >= nz:
                return zrecv[z - nz]
        return dens[local_plane(core, nz, z)]

    def halo(z):
        if isinstance(z, int):
            if z < 0:
                return xrecv[nz - 1 - z]
            if z >= nz:
                return xcorner[z - nz]
        return xrecv[nz - 1 - z]

    return Block(rows, jnp.where(odd == 1, 2, rows + 8 - 2), own, halo)


def far_forward_kernel(dens, pix, zrecv, lrecv, par, smooth, dxs, dys, rnorm, phis, edge, sig, taus, mid, pixo):
    nz, rows, cols = dens.shape
    core, odd = where_am_i()
    at = pl.multiple_of(odd * (rows - 8), 8)

    def own(z):
        if isinstance(z, int):
            if z < 0:
                return pix[-1 - z, pl.ds(at, 8)]
            if z >= nz:
                return zrecv[z - nz, pl.ds(at, 8)]
        return dens[local_plane(core, nz, z), pl.ds(at, 8)]

    def halo(z):
        return lrecv[nz + HALO - 1 - z]

    block = Block(8, jnp.where(odd == 1, 16 - 2, 2), own, halo)
    total = smooth_slab(block, core, nz, GROUP_FAR[0], smooth, taus, sig, pixo)
    total = smooth_seam(block, nz, smooth, taus, sig, pixo, total)
    shade_slab(8, nz, GROUP_FAR[1], total, par, smooth, taus, dxs, dys, rnorm, phis, edge, mid, pixo)


def main_forward_kernel(dens, pix, zrecv, xrecv, xcorner, par, smooth, dxs, dys, rnorm, phis, edge, sig, taus, mid, pixo):
    nz, rows, cols = dens.shape
    core, _ = where_am_i()
    block = main_block(dens, pix, xrecv, zrecv, xcorner)
    total = smooth_slab(block, core, nz, GROUP_MAIN[0], smooth, taus, sig, pixo)
    total = smooth_seam(block, nz, smooth, taus, sig, pixo, total)
    shade_slab(rows, nz, GROUP_MAIN[1], total, par, smooth, taus, dxs, dys, rnorm, phis, edge, mid, pixo)


def backward_block(band, depth, groups, res, theirs, palette, par, grads, image, emit):
    smooth, dxs, dys, rnorm, phis, edge, sig, taus, mid, pixo = res
    cols = smooth.shape[2]
    back = pixo[2] == 1.0
    sign = jnp.where(back, -1.0, 1.0)
    mine_total, their_total = mid[0], theirs[0]
    through_me, through_them = jnp.exp(-mine_total), jnp.exp(-their_total)
    target = lookup(palette, pixo[1])
    g, flow = [], jnp.zeros_like(sign)
    for c in range(3):
        mine, other = mid[1 + c], theirs[1 + c]
        pic = jnp.where(back, other + through_them * mine, mine + through_me * other)
        image[c] = pic
        err = (pic - target[c]) * (2.0 * depth)
        g.append(err)
        flow = flow + err * pic
    kappa = jnp.where(back, 0.5 * through_them, 0.5)
    gam = []
    for k in range(4):
        k0, k1, k2 = [spread(par, 4 * c + k, band, cols) for c in range(3)]
        gam.append(kappa * (g[0] * k0 + g[1] * k1 + g[2] * k2))
    gam2, gam3 = 2.0 * gam[2], 3.0 * gam[3]
    queue = jnp.where(back, 0.0, -flow)
    weight = pixo[0] * (1.0 / (2 * depth))
    lz, ly, lx = [spread(par, 12 + i, band, cols) for i in range(3)]

    def shade_back(z0, n, carry):
        run, part, last = carry
        out = Stores()
        planes = [smooth[z0 + i, pl.ds(0, band)] for i in range(n + 2)]
        edges = [edge[z0 + i] for i in range(n + 1)]
        rest = [(phis[z0 + i], rnorm[z0 + i], sig[z0 + i], dys[z0 + i], dxs[z0 + i]) for i in range(n)]
        for i in range(n):
            s = planes[i + 1]
            dz = planes[i + 2] - planes[i]
            phi, r, sg, dy, dx = rest[i]
            near, far = edges[i], edges[i + 1]
            shade = 1.0 + phi
            poly = gam[0] + s * (gam[1] + s * (gam[2] + s * gam[3]))
            slope = gam[1] + s * (gam2 + s * gam3)
            h = shade * poly
            lost = near - far
            w = sign * lost
            mine = (near * h + run) * (weight * sg) + (w * shade) * slope
            run = run + lost * h
            t1 = w * poly * r
            t3 = t1 * phi * r
            az = t1 * lz - t3 * dz
            ay = t1 * ly - t3 * dy
            ax = t1 * lx - t3 * dx
            out.put(grads, z0 + i, part - az)
            part = mine + last
            part = part + (pltpu.roll(ay, 1, axis=0) - pltpu.roll(ay, band - 1, axis=0))
            part = part + (pltpu.roll(ax, 1, axis=1) - pltpu.roll(ax, cols - 1, axis=1))
            last = az
        out.flush()
        return run, part, last

    nil = jnp.zeros_like(sign)
    in_groups(shade_back, depth + 2, groups[2], (queue, nil, nil))

    def smooth_back(z0, n, carry):
        planes = [grads[z0 + i] for i in range(n + 2)]
        done = []
        for i in range(n):
            here = planes[i + 1]
            t = planes[i] + planes[i + 2] + 2.0 * here
            t = t + pltpu.roll(here, 1, axis=0) + pltpu.roll(here, band - 1, axis=0)
            t = t + pltpu.roll(here, 1, axis=1) + pltpu.roll(here, cols - 1, axis=1)
            done.append(t * 0.125)
        emit(z0, done)
        return carry

    in_groups(smooth_back, depth, groups[3], 0)


def main_backward_kernel(*refs):
    res, (theirs, palette, par, out, image, grads) = refs[:10], refs[10:]
    nz, rows, cols = out.shape
    core, odd = where_am_i()
    shift = jnp.where(odd == 1, rows - 2, 2)

    def emit(z0, values):
        values = [pltpu.roll(v, shift, axis=0) for v in values]
        for i, v in enumerate(values):
            out[local_plane(core, nz, z0 + i)] = v

    backward_block(rows, nz, GROUP_MAIN, res, theirs, palette, par, grads, image, emit)


def far_backward_kernel(*refs):
    res = refs[:10]
    theirs, palette, par, near_grad, near_image, picture_h, out_h, image, grads, picture, out, sem = refs[10:]
    nz, rows, cols = out.shape
    size = GROUP_FAR[3]
    core, odd = where_am_i()
    shift = jnp.where(odd == 1, 2, rows - 2)
    unshift = jnp.where(odd == 1, rows - 2, 2)
    row = lax.broadcasted_iota(jnp.int32, (rows, cols), 0)
    low = odd * (rows - 4)
    mask = (row >= low) & (row < low + 4)

    def emit(z0, values):
        ats = [local_plane(core, nz, z0 + i) for i in range(len(values))]
        nears = [near_grad[at] for at in ats]
        both = [pltpu.roll(jnp.concatenate([v, v], axis=0), shift, axis=0) for v in values]
        both = [jnp.where(mask, b, v) for b, v in zip(both, nears)]
        for at, b in zip(ats, both):
            out[at] = b
        send(out, out_h, z0).start()

    def send(a, b, z0):
        at = pl.ds(jnp.where(core == 0, z0, nz - size - z0), size)
        return pltpu.make_async_copy(a.at[at], b.at[at], sem.at[z0 // size])

    backward_block(8, nz, GROUP_FAR, res, theirs, palette, par, grads, image, emit)
    low = odd * (rows - 2)
    mask2 = (row >= low) & (row < low + 2)
    for c in range(3):
        both = pltpu.roll(jnp.concatenate([image[c], image[c]], axis=0), shift, axis=0)
        whole = jnp.where(mask2, both, pltpu.roll(near_image[c], unshift, axis=0))
        picture[c] = jnp.where(core == 0, whole[:8], whole[8:])
    shown = pltpu.make_async_copy(picture, picture_h, sem.at[nz // size])
    shown.start()
    for z0 in range(0, nz, size):
        send(out, out_h, z0).wait()
    shown.wait()


def shards(density, absorption, view_dir, target_ids, palette, emission_coef, light):
    nz, rows, cols = density.shape
    tiles = lax.axis_size("tile")
    sds = resident

    zmsg, dens, pix, pal, par = call(
        fetch_kernel,
        (sds(HALO, rows, cols), sds(nz, rows, cols), sds(PIX, rows, cols), sds(*palette.shape), sds(15, 8, 128)),
        (density, absorption, target_ids, view_dir, palette, emission_coef, light),
        [HBM] * 7,
        scratch=[
            pltpu.VMEM((rows, cols), jnp.int32),
            pltpu.SMEM(view_dir.shape, jnp.int32),
            pltpu.SMEM(emission_coef.shape, F32),
            pltpu.SMEM(light.shape, F32),
            pltpu.SemaphoreType.DMA((7,)),
        ],
    )
    xmsg, lmsg = call(edges_kernel, (sds(nz + PIX, HALO, cols), sds(nz + PIX, HALO, cols)), (dens, pix), [VMEM] * 2)
    swap = [(0, 1), (1, 0)]
    near = [(i, i ^ 1) for i in range(tiles)]
    far = [(i, i + 1 if i % 2 else i - 1) for i in range(1, tiles - 1)]
    zrecv = lax.ppermute(zmsg, "depth", swap)
    xrecv = lax.ppermute(xmsg, "tile", near)
    lmsg = call(corner_kernel, sds(HALO + nz + PIX, HALO, cols), (zrecv, lmsg), [VMEM, VMEM])
    lrecv = lax.ppermute(lmsg, "tile", far)
    xcorner = lax.ppermute(xrecv[:HALO], "depth", swap)

    def residuals(band):
        planes = nz + 2
        return (
            sds(nz + 4, band + 8, cols),
            sds(planes, band, cols),
            sds(planes, band, cols),
            sds(planes, band, cols),
            sds(planes, band, cols),
            sds(planes + 1, band, cols),
            sds(planes, band, cols),
            sds(planes, band, cols),
            sds(4, band, cols),
            sds(PIX, band, cols),
        )

    main = call(main_forward_kernel, residuals(rows), (dens, pix, zrecv, xrecv, xcorner, par), [VMEM] * 6)
    theirs = lax.ppermute(main[8], "depth", swap)
    near_grad, near_image = call(
        main_backward_kernel,
        (sds(nz, rows, cols), sds(3, rows, cols)),
        (*main, theirs, pal, par),
        [VMEM] * 13,
        scratch=[pltpu.VMEM((nz + 2, rows, cols), F32)],
    )
    lrecv, near_image = lax.optimization_barrier((lrecv, near_image))
    edge = call(far_forward_kernel, residuals(8), (dens, pix, zrecv, lrecv, par), [VMEM] * 5)
    theirs = lax.ppermute(edge[8], "depth", swap)
    picture, grad = call(
        far_backward_kernel,
        (jax.ShapeDtypeStruct((3, 8, cols), F32), jax.ShapeDtypeStruct((nz, rows, cols), F32)),
        (*edge, theirs, pal, par, near_grad, near_image),
        [VMEM] * 15,
        scratch=[
            pltpu.VMEM((3, 8, cols), F32),
            pltpu.VMEM((nz + 2, 8, cols), F32),
            pltpu.VMEM((3, 8, cols), F32),
            pltpu.VMEM((nz, rows, cols), F32),
            pltpu.SemaphoreType.DMA((nz // GROUP_FAR[3] + 1,)),
        ],
        out_specs=(HBM, HBM),
    )
    return picture, grad


def solution(mesh):
    placed = (P("depth", "tile", None), P("tile", None), P("tile"), P("tile", None), P(), P(), P())
    return jax.shard_map(
        shards,
        mesh=mesh,
        in_specs=placed,
        out_specs=(P(None, ("tile", "depth"), None), P("depth", "tile", None)),
        check_vma=False,
    )
```

```python
import jax
import jax.numpy as jnp
from jax import lax
from jax.experimental import pallas as pl
from jax.experimental.pallas import tpu as pltpu
from jax.sharding import PartitionSpec as P


F32 = jnp.float32
HALO = 4
PIX = 3
GROUP_MAIN = (8,16,17,16)
GROUP_FAR = (30,32,34,32)
CHUNK = 8
LATE = True
VMEM = pl.BlockSpec(memory_space=pltpu.VMEM)
HBM = pl.BlockSpec(memory_space=pl.ANY)


def call(kernel, outs, args, specs, scratch=(), cost=None, out_specs=None):
    args = [pltpu.with_memory_space_constraint(a, pltpu.VMEM if s is VMEM else pltpu.HBM) for a, s in zip(args, specs)]
    return pl.pallas_call(
        kernel,
        out_shape=outs,
        in_specs=specs,
        out_specs=out_specs or jax.tree.map(lambda _: VMEM, outs),
        scratch_shapes=scratch,
        cost_estimate=cost,
        compiler_params=pltpu.CompilerParams(vmem_limit_bytes=8 << 20),
    )(*args)


def resident(*shape):
    return pltpu.VMEM(shape, F32)


def where_am_i():
    return lax.axis_index("depth"), lax.rem(lax.axis_index("tile"), 2)


def local_plane(core, nz, z):
    return jnp.where(core == 0, z, nz - 1 - z)


def in_groups(body, count, group, carry):
    full = count // group
    for i in range(full):
        carry = body(i * group, group, carry)
    if count % group:
        carry = body(full * group, count % group, carry)
    return carry


class Joined:
    def __init__(self, head, tail, cut):
        self.head, self.tail, self.cut = head, tail, cut
        self.shape = (cut + tail.shape[0], *tail.shape[1:])

    def find(self, key):
        at, *rest = key if isinstance(key, tuple) else (key,)
        return (self.head, (at, *rest)) if at < self.cut else (self.tail, (at - self.cut, *rest))

    def __getitem__(self, key):
        ref, at = self.find(key)
        return ref[at]

    def __setitem__(self, key, value):
        ref, at = self.find(key)
        ref[at] = value


class Stores:
    def __init__(self):
        self.todo = []

    def put(self, ref, at, value):
        if LATE:
            self.todo.append((ref, at, value))
        else:
            ref[at] = value

    def flush(self):
        for ref, at, value in self.todo:
            ref[at] = value


def spread(par, i, rows, cols):
    t = par[i]
    t = jnp.concatenate([t] * (cols // t.shape[1]), axis=1)
    return jnp.concatenate([t] * (rows // t.shape[0]), axis=0)


def fetch_kernel(dens_h, absorb_h, ids_h, view_h, pal_h, coef_h, light_h, zmsg, dens, pix, pal, par, ids, view, coef, light, sem):
    nz, rows, cols = dens.shape
    core, _ = where_am_i()
    pairs = ((dens_h, dens), (view_h, view), (ids_h, ids), (absorb_h, pix.at[0]), (coef_h, coef), (light_h, light), (pal_h, pal))
    copies = [pltpu.make_async_copy(a, b, sem.at[i]) for i, (a, b) in enumerate(pairs)]
    for c in copies:
        c.start()
    for c in copies[1:]:
        c.wait()
    row = lax.broadcasted_iota(jnp.int32, (rows, cols), 0)
    seen = jnp.zeros((rows, cols), F32)
    for r in range(rows):
        seen = jnp.where(row == r, view[r].astype(F32), seen)
    pix[1] = ids[...].astype(F32)
    pix[2] = seen
    for i in range(3):
        for k in range(4):
            par[4 * i + k] = jnp.full(par.shape[1:], coef[i, k])
        value = light[i]
        if i == 0:
            value = jnp.where(core == 0, value, -value)
        par[12 + i] = jnp.full(par.shape[1:], value)
    copies[0].wait()
    for j in range(HALO):
        zmsg[j] = dens[local_plane(core, nz, nz - 1 - j)]


def edges_kernel(dens, pix, xmsg, lmsg):
    nz, rows, _ = dens.shape
    core, odd = where_am_i()

    def edges(plane, to):
        head, tail = plane[:HALO], plane[rows - HALO :]
        xmsg[to] = jnp.where(odd == 1, head, tail)
        lmsg[to] = jnp.where(odd == 1, tail, head)

    for j in range(PIX):
        edges(pix[j], nz + j)
    for j in range(nz):
        edges(dens[local_plane(core, nz, nz - 1 - j)], j)


def corner_kernel(zrecv, early, lmsg):
    rows = zrecv.shape[1]
    _, odd = where_am_i()
    lmsg[HALO:] = early[...]
    for j in range(HALO):
        plane = zrecv[HALO - 1 - j]
        lmsg[j] = jnp.where(odd == 1, plane[rows - HALO :], plane[:HALO])


def lookup(palette, ids):
    rows, cols = ids.shape
    entries = palette.shape[1]
    index = ids.astype(jnp.int32)
    parts = []
    for c in range(3):
        strips = []
        for r in range(0, rows, 8):
            strip = []
            for x in range(0, cols, entries):
                table = jnp.broadcast_to(palette[c : c + 1, :], (8, entries))
                strip.append(jnp.take_along_axis(table, index[r : r + 8, x : x + entries], axis=1))
            strips.append(jnp.concatenate(strip, axis=1))
        parts.append(jnp.concatenate(strips, axis=0))
    return parts


class Block:
    def __init__(self, band, shift, own, halo):
        self.band, self.shift, self.own, self.halo = band, shift, own, halo

    def plane(self, z):
        h = self.halo(z)
        return pltpu.roll(jnp.concatenate([self.own(z), h, h], axis=0), self.shift, axis=0)


def pixels(block, core):
    a, ids, view = [block.plane(-1 - j)[: block.band] for j in range(PIX)]
    back = jnp.where(core == 0, view, 1.0 - view)
    return a, ids, back


def smooth_planes(block, first, n, signed, depth, smooth, taus, sig, total, lead=None):
    band, wide = block.band, block.band + 8
    out = Stores()
    zs = [first - 1 + i for i in range(n + 2)]
    planes = [lead if i == 0 and lead is not None else block.plane(z) for i, z in enumerate(zs)]
    for i in range(n):
        here = planes[i + 1]
        cols = here.shape[1]
        t = planes[i] + planes[i + 2] + 2.0 * here
        t = t + pltpu.roll(here, 1, axis=0) + pltpu.roll(here, wide - 1, axis=0)
        t = t + pltpu.roll(here, 1, axis=1) + pltpu.roll(here, cols - 1, axis=1)
        s = t * 0.125
        out.put(smooth, zs[i + 1] + 1, s)
        static = isinstance(first, int)
        if not static or first + i < depth + 2:
            soft = jnp.log(1.0 + jnp.exp(s[:band]))
            tau = signed * soft
            out.put(taus, zs[i + 1], tau)
            out.put(sig, zs[i + 1], 1.0 - jnp.exp(-soft))
            if not static or first + i < depth:
                total = total + tau
    out.flush()
    return total


def smooth_slab(block, core, depth, group, smooth, taus, sig, pixo):
    a, ids, back = pixels(block, core)
    signed = a * (1.0 / (2 * depth)) * (1.0 - 2.0 * back)
    pixo[0], pixo[1], pixo[2] = a, ids, back
    face = block.plane(0)
    smooth[0] = face * 0.125
    zero = jnp.zeros_like(face)
    total = smooth_planes(block, 0, 1, signed, depth, smooth, taus, sig, jnp.zeros_like(a), lead=zero)

    def body(z, n, total):
        return smooth_planes(block, z + 1, n, signed, depth, smooth, taus, sig, total)

    return in_groups(body, depth - 2, group, total)


def smooth_seam(block, depth, smooth, taus, sig, pixo, total):
    a, back = pixo[0], pixo[2]
    signed = a * (1.0 / (2 * depth)) * (1.0 - 2.0 * back)
    return smooth_planes(block, depth - 1, 4, signed, depth, smooth, taus, sig, total)


def shade_slab(band, depth, group, total, par, smooth, taus, dxs, dys, rnorm, phis, edge, mid, pixo):
    wide, cols = band + 8, smooth.shape[2]
    back = pixo[2]
    sign = 1.0 - 2.0 * back
    lz, ly, lx = [spread(par, 12 + i, band, cols) for i in range(3)]
    start = jnp.where(back == 1.0, total, 0.0)
    opened = jnp.exp(start)
    edge[0] = opened

    def body(z0, n, carry):
        run, seen, m0, m1, m2, m3 = carry
        out = Stores()
        planes = [smooth[z0 + i] for i in range(n + 2)]
        absorbed = [taus[z0 + i] for i in range(n)]
        for i in range(n):
            here = planes[i + 1]
            s = here[:band]
            dz = planes[i + 2][:band] - planes[i][:band]
            dy = (pltpu.roll(here, wide - 1, axis=0) - pltpu.roll(here, 1, axis=0))[:band]
            dx = pltpu.roll(s, cols - 1, axis=1) - pltpu.roll(s, 1, axis=1)
            r = lax.rsqrt(4.0 + dz * dz + dy * dy + dx * dx)
            phi = (dz * lz + dy * ly + dx * lx) * r
            run = run - absorbed[i]
            nxt = jnp.exp(run)
            for ref, v in ((dxs, dx), (dys, dy), (rnorm, r), (phis, phi)):
                out.put(ref, z0 + i, v)
            out.put(edge, z0 + i + 1, nxt)
            b = (seen - nxt) * (1.0 + phi)
            m0 = m0 + b
            b = b * s
            m1 = m1 + b
            b = b * s
            m2 = m2 + b
            b = b * s
            m3 = m3 + b
            seen = nxt
        out.flush()
        return run, seen, m0, m1, m2, m3

    nil = jnp.zeros_like(back)
    carry = in_groups(body, depth, group, (start, opened, nil, nil, nil, nil))
    _, _, m0, m1, m2, m3 = carry
    half = 0.5 * sign
    mid[0] = sign * total
    for c in range(3):
        k0, k1, k2, k3 = [spread(par, 4 * c + k, band, cols) for k in range(4)]
        mid[1 + c] = half * (m0 * k0 + m1 * k1 + m2 * k2 + m3 * k3)
    body(depth, 2, carry)


def main_block(dens, pix, xrecv, zrecv=None, xcorner=None):
    nz, rows, _ = dens.shape
    core, odd = where_am_i()

    def own(z):
        if isinstance(z, int):
            if z < 0:
                return pix[-1 - z]
            if z >= nz:
                return zrecv[z - nz]
        return dens[local_plane(core, nz, z)]

    def halo(z):
        if isinstance(z, int):
            if z < 0:
                return xrecv[nz - 1 - z]
            if z >= nz:
                return xcorner[z - nz]
        return xrecv[nz - 1 - z]

    return Block(rows, jnp.where(odd == 1, 2, rows + 8 - 2), own, halo)


def far_forward_kernel(dens, pix, zrecv, lrecv, par, smooth, dxs, dys, rnorm, phis, edge, sig, taus, mid, pixo):
    nz, rows, _ = dens.shape
    core, odd = where_am_i()
    at = pl.multiple_of(odd * (rows - 8), 8)

    def own(z):
        if isinstance(z, int):
            if z < 0:
                return pix[-1 - z, pl.ds(at, 8)]
            if z >= nz:
                return zrecv[z - nz, pl.ds(at, 8)]
        return dens[local_plane(core, nz, z), pl.ds(at, 8)]

    def halo(z):
        return lrecv[nz + HALO - 1 - z]

    block = Block(8, jnp.where(odd == 1, 16 - 2, 2), own, halo)
    total = smooth_slab(block, core, nz, GROUP_FAR[0], smooth, taus, sig, pixo)
    total = smooth_seam(block, nz, smooth, taus, sig, pixo, total)
    shade_slab(8, nz, GROUP_FAR[1], total, par, smooth, taus, dxs, dys, rnorm, phis, edge, mid, pixo)


def main_smooth_kernel(dens, pix, xrecv, smooth, taus, sig, pixo, total):
    core, _ = where_am_i()
    block = main_block(dens, pix, xrecv)
    total[...] = smooth_slab(block, core, dens.shape[0], GROUP_MAIN[0], smooth, taus, sig, pixo)


def joined(depth, refs):
    smooth, taus, sig, smooth_tail, taus_tail, sig_tail = refs
    return Joined(smooth, smooth_tail, depth), Joined(taus, taus_tail, depth - 1), Joined(sig, sig_tail, depth - 1)


def main_shade_kernel(smooth, taus, sig, pixo, total, dens, pix, zrecv, xrecv, xcorner, par, smooth_tail, taus_tail, sig_tail, *rest):
    nz, rows, _ = dens.shape
    block = main_block(dens, pix, xrecv, zrecv, xcorner)
    smooth, taus, sig = joined(nz, (smooth, taus, sig, smooth_tail, taus_tail, sig_tail))
    whole = smooth_seam(block, nz, smooth, taus, sig, pixo, total[...])
    shade_slab(rows, nz, GROUP_MAIN[1], whole, par, smooth, taus, *rest, pixo)


def prepare_block(band, depth, group, smooth, dxs, dys, rnorm, phis, edge, sig, pixo, palette, par, bx, by, bz, gained, damped, targets):
    cols = smooth.shape[2]
    sign = 1.0 - 2.0 * pixo[2]
    weight = pixo[0] * (1.0 / (2 * depth))
    lz, ly, lx = [spread(par, 12 + i, band, cols) for i in range(3)]
    for c, t in enumerate(lookup(palette, pixo[1])):
        targets[c] = t

    def body(z0, n, carry):
        out = Stores()
        planes = [smooth[z0 + i, pl.ds(0, band)] for i in range(n + 2)]
        edges = [edge[z0 + i] for i in range(n + 1)]
        rest = [(phis[z0 + i], rnorm[z0 + i], sig[z0 + i], dys[z0 + i], dxs[z0 + i]) for i in range(n)]
        for i in range(n):
            phi, r, sg, dy, dx = rest[i]
            dz = planes[i + 2] - planes[i]
            w = sign * (edges[i] - edges[i + 1])
            p = w * r
            q = p * (phi * r)
            out.put(bx, z0 + i, p * lx - q * dx)
            out.put(by, z0 + i, p * ly - q * dy)
            out.put(bz, z0 + i, p * lz - q * dz)
            out.put(gained, z0 + i, w * (1.0 + phi))
            out.put(damped, z0 + i, weight * sg)
        out.flush()
        return carry

    in_groups(body, depth + 2, group, 0)


def backward_block(band, depth, group, smooth, phis, edge, bx, by, bz, gained, damped, targets, mid, pixo, theirs, par, image, grads):
    cols = smooth.shape[2]
    back = pixo[2] == 1.0
    through_me, through_them = jnp.exp(-mid[0]), jnp.exp(-theirs[0])
    g, flow = [], jnp.zeros_like(through_me)
    for c in range(3):
        mine, other = mid[1 + c], theirs[1 + c]
        pic = jnp.where(back, other + through_them * mine, mine + through_me * other)
        image[c] = pic
        err = (pic - targets[c]) * (2.0 * depth)
        g.append(err)
        flow = flow + err * pic
    kappa = jnp.where(back, 0.5 * through_them, 0.5)
    g = [kappa * e for e in g]
    gam = []
    for k in range(4):
        k0, k1, k2 = [spread(par, 4 * c + k, band, cols) for c in range(3)]
        gam.append(g[0] * k0 + g[1] * k1 + g[2] * k2)
    queue = jnp.where(back, 0.0, -flow)

    def shade_back(z0, n, carry):
        run, part, last = carry
        out = Stores()
        rest = [[ref[z0 + i] for ref in (phis, bx, by, bz, gained, damped)] for i in range(n)]
        values = [smooth[z0 + i + 1, pl.ds(0, band)] for i in range(n)]
        edges = [edge[z0 + i] for i in range(n + 1)]
        for i in range(n):
            s = values[i]
            phi, dx, dy, dz, gain, damp = rest[i]
            near, far = edges[i], edges[i + 1]
            top = s * gam[3]
            inner = gam[2] + top
            outer = gam[1] + s * inner
            poly = gam[0] + s * outer
            slope = outer + s * (inner + top)
            h = poly + phi * poly
            mine = (near * h + run) * damp + gain * slope
            run = run + (near - far) * h
            az, ay, ax = dz * poly, dy * poly, dx * poly
            out.put(grads, z0 + i, part - az)
            part = mine + last
            part = part + (pltpu.roll(ay, 1, axis=0) - pltpu.roll(ay, band - 1, axis=0))
            part = part + (pltpu.roll(ax, 1, axis=1) - pltpu.roll(ax, cols - 1, axis=1))
            last = az
        out.flush()
        return run, part, last

    nil = jnp.zeros_like(through_me)
    in_groups(shade_back, depth + 2, group, (queue, nil, nil))


def smooth_transpose(band, depth, group, grads, emit):
    cols = grads.shape[2]

    def smooth_back(z0, n, carry):
        planes = [grads[z0 + i] for i in range(n + 2)]
        done = []
        for i in range(n):
            here = planes[i + 1]
            t = planes[i] + planes[i + 2] + 2.0 * here
            t = t + pltpu.roll(here, 1, axis=0) + pltpu.roll(here, band - 1, axis=0)
            t = t + pltpu.roll(here, 1, axis=1) + pltpu.roll(here, cols - 1, axis=1)
            done.append(t * 0.125)
            if len(done) == CHUNK:
                emit(z0 + i + 1 - CHUNK, done)
                done = []
        return carry

    in_groups(smooth_back, depth, group, 0)


def main_prepare_kernel(*refs):
    slab, (dxs, dys, rnorm, phis, edge, pixo, palette, par, *out) = refs[:6], refs[6:]
    nz, rows = slab[0].shape[0], dxs.shape[1]
    smooth, _, sig = joined(nz, slab)
    prepare_block(rows, nz, GROUP_MAIN[2], smooth, dxs, dys, rnorm, phis, edge, sig, pixo, palette, par, *out)


def main_backward_kernel(smooth, smooth_tail, *refs):
    nz, rows = smooth.shape[0], refs[0].shape[1]
    backward_block(rows, nz, GROUP_MAIN[2], Joined(smooth, smooth_tail, nz), *refs)


def far_prepare_kernel(smooth, *refs):
    prepare_block(8, smooth.shape[0] - HALO, GROUP_FAR[2], smooth, *refs)


def main_result_kernel(grads, image, out, shown):
    nz, rows, _ = out.shape
    core, odd = where_am_i()
    shift = jnp.where(odd == 1, rows - 2, 2)
    for c in range(3):
        shown[c] = pltpu.roll(image[c], shift, axis=0)

    def emit(z0, values):
        values = [pltpu.roll(v, shift, axis=0) for v in values]
        for i, v in enumerate(values):
            out[local_plane(core, nz, z0 + i)] = v

    smooth_transpose(rows, nz, GROUP_MAIN[3], grads, emit)


def far_backward_kernel(*refs):
    res = refs[:13]
    near_grad, near_image, picture_h, out_h, image, grads, picture, out, sem = refs[13:]
    nz, rows, cols = out.shape
    size = CHUNK
    core, odd = where_am_i()
    shift = jnp.where(odd == 1, 2, rows - 2)
    row = lax.broadcasted_iota(jnp.int32, (rows, cols), 0)
    low = odd * (rows - 4)
    mask = (row >= low) & (row < low + 4)

    def emit(z0, values):
        for i in range(0, len(values), size):
            emit_chunk(z0 + i, values[i : i + size])

    def emit_chunk(z0, values):
        ats = [local_plane(core, nz, z0 + i) for i in range(len(values))]
        nears = [near_grad[at] for at in ats]
        both = [pltpu.roll(jnp.concatenate([v, v], axis=0), shift, axis=0) for v in values]
        both = [jnp.where(mask, b, v) for b, v in zip(both, nears)]
        for at, b in zip(ats, both):
            out[at] = b
        send(out, out_h, z0).start()

    def send(a, b, z0):
        at = pl.ds(jnp.where(core == 0, z0, nz - size - z0), size)
        return pltpu.make_async_copy(a.at[at], b.at[at], sem.at[z0 // size])

    backward_block(8, nz, GROUP_FAR[2], *res, image, grads)
    smooth_transpose(8, nz, GROUP_FAR[3], grads, emit)
    low = odd * (rows - 2)
    mask2 = (row >= low) & (row < low + 2)
    for c in range(3):
        both = pltpu.roll(jnp.concatenate([image[c], image[c]], axis=0), shift, axis=0)
        whole = jnp.where(mask2, both, near_image[c])
        picture[c] = jnp.where(core == 0, whole[:8], whole[8:])
    shown = pltpu.make_async_copy(picture, picture_h, sem.at[nz // size])
    shown.start()
    for z0 in range(0, nz, size):
        send(out, out_h, z0).wait()
    shown.wait()


def shards(density, absorption, view_dir, target_ids, palette, emission_coef, light):
    nz, rows, cols = density.shape
    tiles = lax.axis_size("tile")
    sds = resident

    zmsg, dens, pix, pal, par = call(
        fetch_kernel,
        (sds(HALO, rows, cols), sds(nz, rows, cols), sds(PIX, rows, cols), sds(*palette.shape), sds(15, 8, 128)),
        (density, absorption, target_ids, view_dir, palette, emission_coef, light),
        [HBM] * 7,
        scratch=[
            pltpu.VMEM((rows, cols), jnp.int32),
            pltpu.SMEM(view_dir.shape, jnp.int32),
            pltpu.SMEM(emission_coef.shape, F32),
            pltpu.SMEM(light.shape, F32),
            pltpu.SemaphoreType.DMA((7,)),
        ],
    )
    xmsg, lmsg = call(edges_kernel, (sds(nz + PIX, HALO, cols), sds(nz + PIX, HALO, cols)), (dens, pix), [VMEM] * 2)
    swap = [(0, 1), (1, 0)]
    near = [(i, i ^ 1) for i in range(tiles)]
    far = [(i, i + 1 if i % 2 else i - 1) for i in range(1, tiles - 1)]
    zrecv = lax.ppermute(zmsg, "depth", swap)
    xrecv = lax.ppermute(xmsg, "tile", near)
    lmsg = call(corner_kernel, sds(HALO + nz + PIX, HALO, cols), (zrecv, lmsg), [VMEM, VMEM])
    lrecv = lax.ppermute(lmsg, "tile", far)
    xcorner = lax.ppermute(xrecv[:HALO], "depth", swap)

    def residuals(band):
        planes = nz + 2
        return (
            sds(nz + 4, band + 8, cols),
            sds(planes, band, cols),
            sds(planes, band, cols),
            sds(planes, band, cols),
            sds(planes, band, cols),
            sds(planes + 1, band, cols),
            sds(planes, band, cols),
            sds(planes, band, cols),
            sds(4, band, cols),
            sds(PIX, band, cols),
        )

    parts = residuals(rows)
    smooth, taus, sig, pixo, total = call(
        main_smooth_kernel,
        (sds(nz, rows + 8, cols), sds(nz - 1, rows, cols), sds(nz - 1, rows, cols), parts[9], sds(rows, cols)),
        (dens, pix, xrecv),
        [VMEM] * 3,
    )
    xcorner, total = lax.optimization_barrier((xcorner, total))
    *tails, dxs, dys, rnorm, phis, edge, mid = call(
        main_shade_kernel,
        (sds(4, rows + 8, cols), sds(3, rows, cols), sds(3, rows, cols), *parts[1:6], parts[8]),
        (smooth, taus, sig, pixo, total, dens, pix, zrecv, xrecv, xcorner, par),
        [VMEM] * 11,
    )
    theirs = lax.ppermute(mid, "depth", swap)

    def prepared(band):
        return (*[sds(nz + 2, band, cols)] * 5, sds(3, band, cols))

    ready = call(
        main_prepare_kernel,
        prepared(rows),
        (smooth, taus, sig, *tails, dxs, dys, rnorm, phis, edge, pixo, pal, par),
        [VMEM] * 14,
    )
    near_image, grads = call(
        main_backward_kernel,
        (sds(3, rows, cols), sds(nz + 2, rows, cols)),
        (smooth, tails[0], phis, edge, *ready, mid, pixo, theirs, par),
        [VMEM] * 14,
    )
    lrecv, near_image = lax.optimization_barrier((lrecv, near_image))
    smooth, dxs, dys, rnorm, phis, edge, sig, taus, mid, pixo = call(
        far_forward_kernel, residuals(8), (dens, pix, zrecv, lrecv, par), [VMEM] * 5
    )
    theirs = lax.ppermute(mid, "depth", swap)
    near_image, pixo = lax.optimization_barrier((near_image, pixo))
    near_grad, near_image = call(main_result_kernel, (sds(nz, rows, cols), sds(3, rows, cols)), (grads, near_image), [VMEM] * 2)
    ready = call(
        far_prepare_kernel,
        prepared(8),
        (smooth, dxs, dys, rnorm, phis, edge, sig, pixo, pal, par),
        [VMEM] * 10,
    )
    picture, grad = call(
        far_backward_kernel,
        (jax.ShapeDtypeStruct((3, 8, cols), F32), jax.ShapeDtypeStruct((nz, rows, cols), F32)),
        (smooth, phis, edge, *ready, mid, pixo, theirs, par, near_grad, near_image),
        [VMEM] * 15,
        scratch=[
            pltpu.VMEM((3, 8, cols), F32),
            pltpu.VMEM((nz + 2, 8, cols), F32),
            pltpu.VMEM((3, 8, cols), F32),
            pltpu.VMEM((nz, rows, cols), F32),
            pltpu.SemaphoreType.DMA((nz // CHUNK + 1,)),
        ],
        out_specs=(HBM, HBM),
    )
    return picture, grad


def solution(mesh):
    placed = (P("depth", "tile", None), P("tile", None), P("tile"), P("tile", None), P(), P(), P())
    return jax.shard_map(
        shards,
        mesh=mesh,
        in_specs=placed,
        out_specs=(P(None, ("tile", "depth"), None), P("depth", "tile", None)),
        check_vma=False,
    )
```

```python
import jax
import jax.numpy as jnp
from jax import lax
from jax.experimental import pallas as pl
from jax.experimental.pallas import tpu as pltpu
from jax.sharding import PartitionSpec as P


F32 = jnp.float32
HALO = 4
PIX = 3
GROUP_MAIN = (10,16,17,16)
GROUP_FAR = (30,32,34,32)
CHUNK = 8
LATE = True
VMEM = pl.BlockSpec(memory_space=pltpu.VMEM)
HBM = pl.BlockSpec(memory_space=pl.ANY)


def call(kernel, outs, args, specs, scratch=(), cost=None, out_specs=None):
    args = [pltpu.with_memory_space_constraint(a, pltpu.VMEM if s is VMEM else pltpu.HBM) for a, s in zip(args, specs)]
    return pl.pallas_call(
        kernel,
        out_shape=outs,
        in_specs=specs,
        out_specs=out_specs or jax.tree.map(lambda _: VMEM, outs),
        scratch_shapes=scratch,
        cost_estimate=cost,
        compiler_params=pltpu.CompilerParams(vmem_limit_bytes=8 << 20),
    )(*args)


def resident(*shape):
    return pltpu.VMEM(shape, F32)


def where_am_i():
    return lax.axis_index("depth"), lax.rem(lax.axis_index("tile"), 2)


def local_plane(core, nz, z):
    return jnp.where(core == 0, z, nz - 1 - z)


def in_groups(body, count, group, carry, loop=False):
    full = count // group
    if loop:
        carry = lax.fori_loop(0, full, lambda i, c: body(i * group, group, c), carry)
    for i in range(0 if not loop else full, full):
        carry = body(i * group, group, carry)
    if count % group:
        carry = body(full * group, count % group, carry)
    return carry


class Joined:
    def __init__(self, head, tail, cut):
        self.head, self.tail, self.cut = head, tail, cut
        self.shape = (cut + tail.shape[0], *tail.shape[1:])

    def find(self, key):
        at, *rest = key if isinstance(key, tuple) else (key,)
        return (self.head, (at, *rest)) if at < self.cut else (self.tail, (at - self.cut, *rest))

    def __getitem__(self, key):
        ref, at = self.find(key)
        return ref[at]

    def __setitem__(self, key, value):
        ref, at = self.find(key)
        ref[at] = value


class Stores:
    def __init__(self):
        self.todo = []

    def put(self, ref, at, value):
        if LATE:
            self.todo.append((ref, at, value))
        else:
            ref[at] = value

    def flush(self):
        for ref, at, value in self.todo:
            ref[at] = value


def spread(par, i, rows, cols):
    t = par[i]
    t = jnp.concatenate([t] * (cols // t.shape[1]), axis=1)
    return jnp.concatenate([t] * (rows // t.shape[0]), axis=0)


def fetch_kernel(dens_h, absorb_h, ids_h, view_h, pal_h, coef_h, light_h, zmsg, dens, pix, pal, par, ids, view, coef, light, sem):
    nz, rows, cols = dens.shape
    core, _ = where_am_i()
    pairs = ((dens_h, dens), (view_h, view), (ids_h, ids), (absorb_h, pix.at[0]), (coef_h, coef), (light_h, light), (pal_h, pal))
    copies = [pltpu.make_async_copy(a, b, sem.at[i]) for i, (a, b) in enumerate(pairs)]
    for c in copies:
        c.start()
    for c in copies[1:]:
        c.wait()
    row = lax.broadcasted_iota(jnp.int32, (rows, cols), 0)
    seen = jnp.zeros((rows, cols), F32)
    for r in range(rows):
        seen = jnp.where(row == r, view[r].astype(F32), seen)
    pix[1] = ids[...].astype(F32)
    pix[2] = seen
    for i in range(3):
        for k in range(4):
            par[4 * i + k] = jnp.full(par.shape[1:], coef[i, k])
        value = light[i]
        if i == 0:
            value = jnp.where(core == 0, value, -value)
        par[12 + i] = jnp.full(par.shape[1:], value)
    copies[0].wait()
    for j in range(HALO):
        zmsg[j] = dens[local_plane(core, nz, nz - 1 - j)]


def edges_kernel(dens, pix, xmsg, lmsg):
    nz, rows, _ = dens.shape
    core, odd = where_am_i()

    def edges(plane, to):
        head, tail = plane[:HALO], plane[rows - HALO :]
        xmsg[to] = jnp.where(odd == 1, head, tail)
        lmsg[to] = jnp.where(odd == 1, tail, head)

    for j in range(PIX):
        edges(pix[j], nz + j)
    for j in range(nz):
        edges(dens[local_plane(core, nz, nz - 1 - j)], j)


def corner_kernel(zrecv, early, lmsg):
    rows = zrecv.shape[1]
    _, odd = where_am_i()
    lmsg[HALO:] = early[...]
    for j in range(HALO):
        plane = zrecv[HALO - 1 - j]
        lmsg[j] = jnp.where(odd == 1, plane[rows - HALO :], plane[:HALO])


def lookup(palette, ids):
    rows, cols = ids.shape
    entries = palette.shape[1]
    index = ids.astype(jnp.int32)
    parts = []
    for c in range(3):
        strips = []
        for r in range(0, rows, 8):
            strip = []
            for x in range(0, cols, entries):
                table = jnp.broadcast_to(palette[c : c + 1, :], (8, entries))
                strip.append(jnp.take_along_axis(table, index[r : r + 8, x : x + entries], axis=1))
            strips.append(jnp.concatenate(strip, axis=1))
        parts.append(jnp.concatenate(strips, axis=0))
    return parts


class Block:
    def __init__(self, band, shift, own, halo):
        self.band, self.shift, self.own, self.halo = band, shift, own, halo

    def plane(self, z):
        h = self.halo(z)
        return pltpu.roll(jnp.concatenate([self.own(z), h, h], axis=0), self.shift, axis=0)


def pixels(block, core):
    a, ids, view = [block.plane(-1 - j)[: block.band] for j in range(PIX)]
    back = jnp.where(core == 0, view, 1.0 - view)
    return a, ids, back


def smooth_planes(block, first, n, signed, depth, smooth, taus, sig, total, lead=None):
    band, wide = block.band, block.band + 8
    out = Stores()
    zs = [first - 1 + i for i in range(n + 2)]
    planes = [lead if i == 0 and lead is not None else block.plane(z) for i, z in enumerate(zs)]
    for i in range(n):
        here = planes[i + 1]
        cols = here.shape[1]
        t = planes[i] + planes[i + 2] + 2.0 * here
        t = t + pltpu.roll(here, 1, axis=0) + pltpu.roll(here, wide - 1, axis=0)
        t = t + pltpu.roll(here, 1, axis=1) + pltpu.roll(here, cols - 1, axis=1)
        s = t * 0.125
        out.put(smooth, zs[i + 1] + 1, s)
        static = isinstance(first, int)
        if not static or first + i < depth + 2:
            soft = jnp.log(1.0 + jnp.exp(s[:band]))
            tau = signed * soft
            out.put(taus, zs[i + 1], tau)
            out.put(sig, zs[i + 1], 1.0 - jnp.exp(-soft))
            if not static or first + i < depth:
                total = total + tau
    out.flush()
    return total


def smooth_slab(block, core, depth, group, smooth, taus, sig, pixo):
    a, ids, back = pixels(block, core)
    signed = a * (1.0 / (2 * depth)) * (1.0 - 2.0 * back)
    pixo[0], pixo[1], pixo[2] = a, ids, back
    face = block.plane(0)
    smooth[0] = face * 0.125
    zero = jnp.zeros_like(face)
    total = smooth_planes(block, 0, 1, signed, depth, smooth, taus, sig, jnp.zeros_like(a), lead=zero)

    def body(z, n, total):
        return smooth_planes(block, z + 1, n, signed, depth, smooth, taus, sig, total)

    return in_groups(body, depth - 2, group, total, loop=block.band > 8)


def smooth_seam(block, depth, smooth, taus, sig, pixo, total):
    a, back = pixo[0], pixo[2]
    signed = a * (1.0 / (2 * depth)) * (1.0 - 2.0 * back)
    return smooth_planes(block, depth - 1, 4, signed, depth, smooth, taus, sig, total)


def shade_slab(band, depth, group, total, par, smooth, taus, dxs, dys, rnorm, phis, edge, mid, pixo):
    wide, cols = band + 8, smooth.shape[2]
    back = pixo[2]
    sign = 1.0 - 2.0 * back
    lz, ly, lx = [spread(par, 12 + i, band, cols) for i in range(3)]
    start = jnp.where(back == 1.0, total, 0.0)
    opened = jnp.exp(start)
    edge[0] = opened

    def body(z0, n, carry):
        run, seen, m0, m1, m2, m3 = carry
        out = Stores()
        planes = [smooth[z0 + i] for i in range(n + 2)]
        absorbed = [taus[z0 + i] for i in range(n)]
        for i in range(n):
            here = planes[i + 1]
            s = here[:band]
            dz = planes[i + 2][:band] - planes[i][:band]
            dy = (pltpu.roll(here, wide - 1, axis=0) - pltpu.roll(here, 1, axis=0))[:band]
            dx = pltpu.roll(s, cols - 1, axis=1) - pltpu.roll(s, 1, axis=1)
            r = lax.rsqrt(4.0 + dz * dz + dy * dy + dx * dx)
            phi = (dz * lz + dy * ly + dx * lx) * r
            run = run - absorbed[i]
            nxt = jnp.exp(run)
            for ref, v in ((dxs, dx), (dys, dy), (rnorm, r), (phis, phi)):
                out.put(ref, z0 + i, v)
            out.put(edge, z0 + i + 1, nxt)
            b = (seen - nxt) * (1.0 + phi)
            m0 = m0 + b
            b = b * s
            m1 = m1 + b
            b = b * s
            m2 = m2 + b
            b = b * s
            m3 = m3 + b
            seen = nxt
        out.flush()
        return run, seen, m0, m1, m2, m3

    nil = jnp.zeros_like(back)
    carry = in_groups(body, depth, group, (start, opened, nil, nil, nil, nil))
    _, _, m0, m1, m2, m3 = carry
    half = 0.5 * sign
    mid[0] = sign * total
    for c in range(3):
        k0, k1, k2, k3 = [spread(par, 4 * c + k, band, cols) for k in range(4)]
        mid[1 + c] = half * (m0 * k0 + m1 * k1 + m2 * k2 + m3 * k3)
    body(depth, 2, carry)


def main_block(dens, pix, xrecv, zrecv=None, xcorner=None):
    nz, rows, _ = dens.shape
    core, odd = where_am_i()

    def own(z):
        if isinstance(z, int):
            if z < 0:
                return pix[-1 - z]
            if z >= nz:
                return zrecv[z - nz]
        return dens[local_plane(core, nz, z)]

    def halo(z):
        if isinstance(z, int):
            if z < 0:
                return xrecv[nz - 1 - z]
            if z >= nz:
                return xcorner[z - nz]
        return xrecv[nz - 1 - z]

    return Block(rows, jnp.where(odd == 1, 2, rows + 8 - 2), own, halo)


def far_forward_kernel(dens, pix, zrecv, lrecv, par, smooth, dxs, dys, rnorm, phis, edge, sig, mid, pixo, taus):
    nz, rows, _ = dens.shape
    core, odd = where_am_i()
    at = pl.multiple_of(odd * (rows - 8), 8)

    def own(z):
        if isinstance(z, int):
            if z < 0:
                return pix[-1 - z, pl.ds(at, 8)]
            if z >= nz:
                return zrecv[z - nz, pl.ds(at, 8)]
        return dens[local_plane(core, nz, z), pl.ds(at, 8)]

    def halo(z):
        return lrecv[nz + HALO - 1 - z]

    block = Block(8, jnp.where(odd == 1, 16 - 2, 2), own, halo)
    total = smooth_slab(block, core, nz, GROUP_FAR[0], smooth, taus, sig, pixo)
    total = smooth_seam(block, nz, smooth, taus, sig, pixo, total)
    shade_slab(8, nz, GROUP_FAR[1], total, par, smooth, taus, dxs, dys, rnorm, phis, edge, mid, pixo)


def main_smooth_kernel(dens, pix, xrecv, smooth, taus, sig, pixo, total):
    core, _ = where_am_i()
    block = main_block(dens, pix, xrecv)
    total[...] = smooth_slab(block, core, dens.shape[0], GROUP_MAIN[0], smooth, taus, sig, pixo)


def main_shade_kernel(smooth, taus, sig, pixo, total, dens, pix, zrecv, xrecv, xcorner, par, smooth_tail, sig_tail, dxs, dys, rnorm, phis, edge, mid, taus_tail):
    nz, rows, _ = dens.shape
    block = main_block(dens, pix, xrecv, zrecv, xcorner)
    smooth, taus, sig = Joined(smooth, smooth_tail, nz), Joined(taus, taus_tail, nz - 1), Joined(sig, sig_tail, nz - 1)
    whole = smooth_seam(block, nz, smooth, taus, sig, pixo, total[...])
    shade_slab(rows, nz, GROUP_MAIN[1], whole, par, smooth, taus, dxs, dys, rnorm, phis, edge, mid, pixo)


def prepare_block(band, depth, group, smooth, dxs, dys, rnorm, phis, edge, sig, pixo, palette, par, bx, by, bz, gained, damped, targets):
    cols = smooth.shape[2]
    sign = 1.0 - 2.0 * pixo[2]
    weight = pixo[0] * (1.0 / (2 * depth))
    lz, ly, lx = [spread(par, 12 + i, band, cols) for i in range(3)]
    for c, t in enumerate(lookup(palette, pixo[1])):
        targets[c] = t

    def body(z0, n, carry):
        out = Stores()
        planes = [smooth[z0 + i, pl.ds(0, band)] for i in range(n + 2)]
        edges = [edge[z0 + i] for i in range(n + 1)]
        rest = [(phis[z0 + i], rnorm[z0 + i], sig[z0 + i], dys[z0 + i], dxs[z0 + i]) for i in range(n)]
        for i in range(n):
            phi, r, sg, dy, dx = rest[i]
            dz = planes[i + 2] - planes[i]
            w = sign * (edges[i] - edges[i + 1])
            p = w * r
            q = p * (phi * r)
            out.put(bx, z0 + i, p * lx - q * dx)
            out.put(by, z0 + i, p * ly - q * dy)
            out.put(bz, z0 + i, p * lz - q * dz)
            out.put(gained, z0 + i, w * (1.0 + phi))
            out.put(damped, z0 + i, weight * sg)
        out.flush()
        return carry

    in_groups(body, depth + 2, group, 0)


def backward_block(band, depth, group, smooth, phis, edge, bx, by, bz, gained, damped, targets, mid, pixo, theirs, par, image, grads):
    cols = smooth.shape[2]
    back = pixo[2] == 1.0
    through_me, through_them = jnp.exp(-mid[0]), jnp.exp(-theirs[0])
    g, flow = [], jnp.zeros_like(through_me)
    for c in range(3):
        mine, other = mid[1 + c], theirs[1 + c]
        pic = jnp.where(back, other + through_them * mine, mine + through_me * other)
        image[c] = pic
        err = (pic - targets[c]) * (2.0 * depth)
        g.append(err)
        flow = flow + err * pic
    kappa = jnp.where(back, 0.5 * through_them, 0.5)
    g = [kappa * e for e in g]
    gam = []
    for k in range(4):
        k0, k1, k2 = [spread(par, 4 * c + k, band, cols) for c in range(3)]
        gam.append(g[0] * k0 + g[1] * k1 + g[2] * k2)
    queue = jnp.where(back, 0.0, -flow)

    def shade_back(z0, n, carry):
        run, part, last = carry
        out = Stores()
        rest = [[ref[z0 + i] for ref in (phis, bx, by, bz, gained, damped)] for i in range(n)]
        values = [smooth[z0 + i + 1, pl.ds(0, band)] for i in range(n)]
        edges = [edge[z0 + i] for i in range(n + 1)]
        for i in range(n):
            s = values[i]
            phi, dx, dy, dz, gain, damp = rest[i]
            near, far = edges[i], edges[i + 1]
            top = s * gam[3]
            inner = gam[2] + top
            outer = gam[1] + s * inner
            poly = gam[0] + s * outer
            slope = outer + s * (inner + top)
            h = poly + phi * poly
            mine = (near * h + run) * damp + gain * slope
            run = run + (near - far) * h
            az, ay, ax = dz * poly, dy * poly, dx * poly
            out.put(grads, z0 + i, part - az)
            part = mine + last
            part = part + (pltpu.roll(ay, 1, axis=0) - pltpu.roll(ay, band - 1, axis=0))
            part = part + (pltpu.roll(ax, 1, axis=1) - pltpu.roll(ax, cols - 1, axis=1))
            last = az
        out.flush()
        return run, part, last

    nil = jnp.zeros_like(through_me)
    in_groups(shade_back, depth + 2, group, (queue, nil, nil))


def smooth_transpose(band, depth, group, grads, emit):
    cols = grads.shape[2]

    def smooth_back(z0, n, carry):
        planes = [grads[z0 + i] for i in range(n + 2)]
        done = []
        for i in range(n):
            here = planes[i + 1]
            t = planes[i] + planes[i + 2] + 2.0 * here
            t = t + pltpu.roll(here, 1, axis=0) + pltpu.roll(here, band - 1, axis=0)
            t = t + pltpu.roll(here, 1, axis=1) + pltpu.roll(here, cols - 1, axis=1)
            done.append(t * 0.125)
            if len(done) == CHUNK:
                emit(z0 + i + 1 - CHUNK, done)
                done = []
        return carry

    in_groups(smooth_back, depth, group, 0, loop=band > 8)


def main_prepare_kernel(smooth, sig, smooth_tail, sig_tail, dxs, dys, rnorm, phis, edge, pixo, palette, par, *out):
    nz, rows, _ = dxs.shape
    nz = nz - 2
    smooth, sig = Joined(smooth, smooth_tail, nz), Joined(sig, sig_tail, nz - 1)
    prepare_block(rows, nz, GROUP_MAIN[2], smooth, dxs, dys, rnorm, phis, edge, sig, pixo, palette, par, *out)


def main_backward_kernel(smooth, smooth_tail, *refs):
    nz, rows = smooth.shape[0], refs[0].shape[1]
    backward_block(rows, nz, GROUP_MAIN[2], Joined(smooth, smooth_tail, nz), *refs)


def far_prepare_kernel(smooth, *refs):
    prepare_block(8, smooth.shape[0] - HALO, GROUP_FAR[2], smooth, *refs)


def main_result_kernel(grads, image, out, shown):
    nz, rows, _ = out.shape
    core, odd = where_am_i()
    shift = jnp.where(odd == 1, rows - 2, 2)
    for c in range(3):
        shown[c] = pltpu.roll(image[c], shift, axis=0)

    def emit(z0, values):
        values = [pltpu.roll(v, shift, axis=0) for v in values]
        for i, v in enumerate(values):
            out[local_plane(core, nz, z0 + i)] = v

    smooth_transpose(rows, nz, GROUP_MAIN[3], grads, emit)


def far_backward_kernel(*refs):
    res = refs[:13]
    near_grad, near_image, picture_h, out_h, image, grads, picture, out, sem = refs[13:]
    nz, rows, cols = out.shape
    size = CHUNK
    core, odd = where_am_i()
    shift = jnp.where(odd == 1, 2, rows - 2)
    row = lax.broadcasted_iota(jnp.int32, (rows, cols), 0)
    low = odd * (rows - 4)
    mask = (row >= low) & (row < low + 4)

    def emit(z0, values):
        for i in range(0, len(values), size):
            emit_chunk(z0 + i, values[i : i + size])

    def emit_chunk(z0, values):
        ats = [local_plane(core, nz, z0 + i) for i in range(len(values))]
        nears = [near_grad[at] for at in ats]
        both = [pltpu.roll(jnp.concatenate([v, v], axis=0), shift, axis=0) for v in values]
        both = [jnp.where(mask, b, v) for b, v in zip(both, nears)]
        for at, b in zip(ats, both):
            out[at] = b
        send(out, out_h, z0).start()

    def send(a, b, z0):
        at = pl.ds(jnp.where(core == 0, z0, nz - size - z0), size)
        return pltpu.make_async_copy(a.at[at], b.at[at], sem.at[z0 // size])

    backward_block(8, nz, GROUP_FAR[2], *res, image, grads)
    smooth_transpose(8, nz, GROUP_FAR[3], grads, emit)
    low = odd * (rows - 2)
    mask2 = (row >= low) & (row < low + 2)
    for c in range(3):
        both = pltpu.roll(jnp.concatenate([image[c], image[c]], axis=0), shift, axis=0)
        whole = jnp.where(mask2, both, near_image[c])
        picture[c] = jnp.where(core == 0, whole[:8], whole[8:])
    shown = pltpu.make_async_copy(picture, picture_h, sem.at[nz // size])
    shown.start()
    for z0 in range(0, nz, size):
        send(out, out_h, z0).wait()
    shown.wait()


def shards(density, absorption, view_dir, target_ids, palette, emission_coef, light):
    nz, rows, cols = density.shape
    tiles = lax.axis_size("tile")
    sds = resident

    zmsg, dens, pix, pal, par = call(
        fetch_kernel,
        (sds(HALO, rows, cols), sds(nz, rows, cols), sds(PIX, rows, cols), sds(*palette.shape), sds(15, 8, 128)),
        (density, absorption, target_ids, view_dir, palette, emission_coef, light),
        [HBM] * 7,
        scratch=[
            pltpu.VMEM((rows, cols), jnp.int32),
            pltpu.SMEM(view_dir.shape, jnp.int32),
            pltpu.SMEM(emission_coef.shape, F32),
            pltpu.SMEM(light.shape, F32),
            pltpu.SemaphoreType.DMA((7,)),
        ],
    )
    xmsg, lmsg = call(edges_kernel, (sds(nz + PIX, HALO, cols), sds(nz + PIX, HALO, cols)), (dens, pix), [VMEM] * 2)
    swap = [(0, 1), (1, 0)]
    near = [(i, i ^ 1) for i in range(tiles)]
    far = [(i, i + 1 if i % 2 else i - 1) for i in range(1, tiles - 1)]
    zrecv = lax.ppermute(zmsg, "depth", swap)
    xrecv = lax.ppermute(xmsg, "tile", near)
    lmsg = call(corner_kernel, sds(HALO + nz + PIX, HALO, cols), (zrecv, lmsg), [VMEM, VMEM])
    lrecv = lax.ppermute(lmsg, "tile", far)
    xcorner = lax.ppermute(xrecv[:HALO], "depth", swap)

    def residuals(band):
        planes = nz + 2
        return (
            sds(nz + 4, band + 8, cols),
            *[sds(planes, band, cols)] * 4,
            sds(planes + 1, band, cols),
            sds(planes, band, cols),
            sds(4, band, cols),
            sds(PIX, band, cols),
        )

    parts = residuals(rows)
    smooth, taus, sig, pixo, total = call(
        main_smooth_kernel,
        (sds(nz, rows + 8, cols), sds(nz - 1, rows, cols), sds(nz - 1, rows, cols), parts[8], sds(rows, cols)),
        (dens, pix, xrecv),
        [VMEM] * 3,
    )
    xcorner, total = lax.optimization_barrier((xcorner, total))
    smooth_tail, sig_tail, dxs, dys, rnorm, phis, edge, mid = call(
        main_shade_kernel,
        (sds(4, rows + 8, cols), sds(3, rows, cols), *parts[1:6], parts[7]),
        (smooth, taus, sig, pixo, total, dens, pix, zrecv, xrecv, xcorner, par),
        [VMEM] * 11,
        scratch=[pltpu.VMEM((3, rows, cols), F32)],
    )
    theirs = lax.ppermute(mid, "depth", swap)

    def prepared(band):
        return (*[sds(nz + 2, band, cols)] * 5, sds(3, band, cols))

    ready = call(
        main_prepare_kernel,
        prepared(rows),
        (smooth, sig, smooth_tail, sig_tail, dxs, dys, rnorm, phis, edge, pixo, pal, par),
        [VMEM] * 12,
    )
    near_image, grads = call(
        main_backward_kernel,
        (sds(3, rows, cols), sds(nz + 2, rows, cols)),
        (smooth, smooth_tail, phis, edge, *ready, mid, pixo, theirs, par),
        [VMEM] * 14,
    )
    lrecv, near_image = lax.optimization_barrier((lrecv, near_image))
    smooth, dxs, dys, rnorm, phis, edge, sig, mid, pixo = call(
        far_forward_kernel,
        residuals(8),
        (dens, pix, zrecv, lrecv, par),
        [VMEM] * 5,
        scratch=[pltpu.VMEM((nz + 2, 8, cols), F32)],
    )
    theirs = lax.ppermute(mid, "depth", swap)
    near_image, pixo = lax.optimization_barrier((near_image, pixo))
    near_grad, near_image = call(main_result_kernel, (sds(nz, rows, cols), sds(3, rows, cols)), (grads, near_image), [VMEM] * 2)
    ready = call(
        far_prepare_kernel,
        prepared(8),
        (smooth, dxs, dys, rnorm, phis, edge, sig, pixo, pal, par),
        [VMEM] * 10,
    )
    picture, grad = call(
        far_backward_kernel,
        (jax.ShapeDtypeStruct((3, 8, cols), F32), jax.ShapeDtypeStruct((nz, rows, cols), F32)),
        (smooth, phis, edge, *ready, mid, pixo, theirs, par, near_grad, near_image),
        [VMEM] * 15,
        scratch=[
            pltpu.VMEM((3, 8, cols), F32),
            pltpu.VMEM((nz + 2, 8, cols), F32),
            pltpu.VMEM((3, 8, cols), F32),
            pltpu.VMEM((nz, rows, cols), F32),
            pltpu.SemaphoreType.DMA((nz // CHUNK + 1,)),
        ],
        out_specs=(HBM, HBM),
    )
    return picture, grad


def solution(mesh):
    placed = (P("depth", "tile", None), P("tile", None), P("tile"), P("tile", None), P(), P(), P())
    return jax.shard_map(
        shards,
        mesh=mesh,
        in_specs=placed,
        out_specs=(P(None, ("tile", "depth"), None), P("depth", "tile", None)),
        check_vma=False,
    )
```

```python
import jax
import jax.numpy as jnp
from jax import lax
from jax.experimental import pallas as pl
from jax.experimental.pallas import tpu as pltpu
from jax.sharding import PartitionSpec as P


F32 = jnp.float32
HALO = 4
PIX = 3
GROUP_MAIN = (10,16,17,16)
GROUP_FAR = (30,32,34,32)
CHUNK = 8
LATE = True
VMEM = pl.BlockSpec(memory_space=pltpu.VMEM)
HBM = pl.BlockSpec(memory_space=pl.ANY)


def call(kernel, outs, args, specs, scratch=(), cost=None, out_specs=None):
    args = [pltpu.with_memory_space_constraint(a, pltpu.VMEM if s is VMEM else pltpu.HBM) for a, s in zip(args, specs)]
    return pl.pallas_call(
        kernel,
        out_shape=outs,
        in_specs=specs,
        out_specs=out_specs or jax.tree.map(lambda _: VMEM, outs),
        scratch_shapes=scratch,
        cost_estimate=cost,
        compiler_params=pltpu.CompilerParams(vmem_limit_bytes=8 << 20),
    )(*args)


def resident(*shape):
    return pltpu.VMEM(shape, F32)


def where_am_i():
    return lax.axis_index("depth"), lax.rem(lax.axis_index("tile"), 2)


def local_plane(core, nz, z):
    return jnp.where(core == 0, z, nz - 1 - z)


def in_groups(body, count, group, carry, loop=False):
    full = count // group
    if loop:
        carry = lax.fori_loop(0, full, lambda i, c: body(i * group, group, c), carry)
    for i in range(0 if not loop else full, full):
        carry = body(i * group, group, carry)
    if count % group:
        carry = body(full * group, count % group, carry)
    return carry


class Joined:
    def __init__(self, head, tail, cut):
        self.head, self.tail, self.cut = head, tail, cut
        self.shape = (cut + tail.shape[0], *tail.shape[1:])

    def find(self, key):
        at, *rest = key if isinstance(key, tuple) else (key,)
        return (self.head, (at, *rest)) if at < self.cut else (self.tail, (at - self.cut, *rest))

    def __getitem__(self, key):
        ref, at = self.find(key)
        return ref[at]

    def __setitem__(self, key, value):
        ref, at = self.find(key)
        ref[at] = value


class Stores:
    def __init__(self):
        self.todo = []

    def put(self, ref, at, value):
        if LATE:
            self.todo.append((ref, at, value))
        else:
            ref[at] = value

    def flush(self):
        for ref, at, value in self.todo:
            ref[at] = value


def spread(par, i, rows, cols):
    t = par[i]
    t = jnp.concatenate([t] * (cols // t.shape[1]), axis=1)
    return jnp.concatenate([t] * (rows // t.shape[0]), axis=0)


def fetch_kernel(dens_h, absorb_h, ids_h, view_h, pal_h, coef_h, light_h, zmsg, dens, pix, pal, par, ids, view, coef, light, sem):
    nz, rows, cols = dens.shape
    core, _ = where_am_i()
    pairs = ((dens_h, dens), (view_h, view), (ids_h, ids), (absorb_h, pix.at[0]), (coef_h, coef), (light_h, light), (pal_h, pal))
    copies = [pltpu.make_async_copy(a, b, sem.at[i]) for i, (a, b) in enumerate(pairs)]
    for c in copies:
        c.start()
    for c in copies[1:]:
        c.wait()
    row = lax.broadcasted_iota(jnp.int32, (rows, cols), 0)
    seen = jnp.zeros((rows, cols), F32)
    for r in range(rows):
        seen = jnp.where(row == r, view[r].astype(F32), seen)
    pix[1] = ids[...].astype(F32)
    pix[2] = seen
    for i in range(3):
        for k in range(4):
            par[4 * i + k] = jnp.full(par.shape[1:], coef[i, k])
        value = light[i]
        if i == 0:
            value = jnp.where(core == 0, value, -value)
        par[12 + i] = jnp.full(par.shape[1:], value)
    copies[0].wait()
    for j in range(HALO):
        zmsg[j] = dens[local_plane(core, nz, nz - 1 - j)]


def edges_kernel(dens, pix, xmsg, lmsg):
    nz, rows, _ = dens.shape
    core, odd = where_am_i()

    def edges(head, tail, to):
        xmsg[to] = jnp.where(odd == 1, head, tail)
        lmsg[to] = jnp.where(odd == 1, tail, head)

    a, ids, view = pix[0], pix[1], pix[2]
    edges(jnp.concatenate([a[:2], ids[:2]], axis=0), jnp.concatenate([ids[rows - 2 :], a[rows - 2 :]], axis=0), nz)
    edges(view[:HALO], view[rows - HALO :], nz + 1)
    for j in range(nz):
        plane = dens[local_plane(core, nz, nz - 1 - j)]
        edges(plane[:HALO], plane[rows - HALO :], j)


def corner_kernel(zrecv, early, lmsg):
    rows = zrecv.shape[1]
    _, odd = where_am_i()
    lmsg[2:] = early[...]
    one, two, three = zrecv[0], zrecv[1], zrecv[2]
    lmsg[1] = jnp.where(odd == 1, one[rows - HALO :], one[:HALO])
    tail = jnp.concatenate([three[rows - 1 :], two[rows - HALO + 1 :]], axis=0)
    head = jnp.concatenate([two[: HALO - 1], three[:1]], axis=0)
    lmsg[0] = jnp.where(odd == 1, tail, head)


def lookup(palette, ids):
    rows, cols = ids.shape
    entries = palette.shape[1]
    index = ids.astype(jnp.int32)
    parts = []
    for c in range(3):
        strips = []
        for r in range(0, rows, 8):
            strip = []
            for x in range(0, cols, entries):
                table = jnp.broadcast_to(palette[c : c + 1, :], (8, entries))
                strip.append(jnp.take_along_axis(table, index[r : r + 8, x : x + entries], axis=1))
            strips.append(jnp.concatenate(strip, axis=1))
        parts.append(jnp.concatenate(strips, axis=0))
    return parts


def pixel_rows(planes, z):
    if z == -1:
        return planes[0]
    if z == -2:
        return jnp.concatenate([planes[0][2:], planes[0][:2]], axis=0)
    return planes[1]


class Block:
    def __init__(self, band, shift, own, halo):
        self.band, self.shift, self.own, self.halo = band, shift, own, halo

    def plane(self, z):
        h = self.halo(z)
        return pltpu.roll(jnp.concatenate([self.own(z), h, h], axis=0), self.shift, axis=0)


def pixels(block, core):
    a, ids, view = [block.plane(-1 - j)[: block.band] for j in range(PIX)]
    back = jnp.where(core == 0, view, 1.0 - view)
    return a, ids, back


def smooth_planes(block, first, n, signed, depth, smooth, taus, sig, total, lead=None):
    band, wide = block.band, block.band + 8
    out = Stores()
    zs = [first - 1 + i for i in range(n + 2)]
    planes = [lead if i == 0 and lead is not None else block.plane(z) for i, z in enumerate(zs)]
    for i in range(n):
        here = planes[i + 1]
        cols = here.shape[1]
        t = planes[i] + planes[i + 2] + 2.0 * here
        t = t + pltpu.roll(here, 1, axis=0) + pltpu.roll(here, wide - 1, axis=0)
        t = t + pltpu.roll(here, 1, axis=1) + pltpu.roll(here, cols - 1, axis=1)
        s = t * 0.125
        out.put(smooth, zs[i + 1] + 1, s)
        static = isinstance(first, int)
        if not static or first + i < depth + 2:
            soft = jnp.log(1.0 + jnp.exp(s[:band]))
            tau = signed * soft
            out.put(taus, zs[i + 1], tau)
            out.put(sig, zs[i + 1], 1.0 - jnp.exp(-soft))
            if not static or first + i < depth:
                total = total + tau
    out.flush()
    return total


def smooth_slab(block, core, depth, group, smooth, taus, sig, pixo):
    a, ids, back = pixels(block, core)
    signed = a * (1.0 / (2 * depth)) * (1.0 - 2.0 * back)
    pixo[0], pixo[1], pixo[2] = a, ids, back
    face = block.plane(0)
    smooth[0] = face * 0.125
    zero = jnp.zeros_like(face)
    total = smooth_planes(block, 0, 1, signed, depth, smooth, taus, sig, jnp.zeros_like(a), lead=zero)

    def body(z, n, total):
        return smooth_planes(block, z + 1, n, signed, depth, smooth, taus, sig, total)

    return in_groups(body, depth - 2, group, total, loop=block.band > 8)


def smooth_seam(block, depth, smooth, taus, sig, pixo, total):
    a, back = pixo[0], pixo[2]
    signed = a * (1.0 / (2 * depth)) * (1.0 - 2.0 * back)
    return smooth_planes(block, depth - 1, 4, signed, depth, smooth, taus, sig, total)


def shade_slab(band, depth, group, total, par, smooth, taus, dxs, dys, rnorm, phis, edge, mid, pixo):
    wide, cols = band + 8, smooth.shape[2]
    back = pixo[2]
    sign = 1.0 - 2.0 * back
    lz, ly, lx = [spread(par, 12 + i, band, cols) for i in range(3)]
    start = jnp.where(back == 1.0, total, 0.0)
    opened = jnp.exp(start)
    edge[0] = opened

    def body(z0, n, carry):
        run, seen, m0, m1, m2, m3 = carry
        out = Stores()
        planes = [smooth[z0 + i] for i in range(n + 2)]
        absorbed = [taus[z0 + i] for i in range(n)]
        for i in range(n):
            here = planes[i + 1]
            s = here[:band]
            dz = planes[i + 2][:band] - planes[i][:band]
            dy = (pltpu.roll(here, wide - 1, axis=0) - pltpu.roll(here, 1, axis=0))[:band]
            dx = pltpu.roll(s, cols - 1, axis=1) - pltpu.roll(s, 1, axis=1)
            r = lax.rsqrt(4.0 + dz * dz + dy * dy + dx * dx)
            phi = (dz * lz + dy * ly + dx * lx) * r
            run = run - absorbed[i]
            nxt = jnp.exp(run)
            for ref, v in ((dxs, dx), (dys, dy), (rnorm, r), (phis, phi)):
                out.put(ref, z0 + i, v)
            out.put(edge, z0 + i + 1, nxt)
            b = (seen - nxt) * (1.0 + phi)
            m0 = m0 + b
            b = b * s
            m1 = m1 + b
            b = b * s
            m2 = m2 + b
            b = b * s
            m3 = m3 + b
            seen = nxt
        out.flush()
        return run, seen, m0, m1, m2, m3

    nil = jnp.zeros_like(back)
    carry = in_groups(body, depth, group, (start, opened, nil, nil, nil, nil))
    _, _, m0, m1, m2, m3 = carry
    half = 0.5 * sign
    mid[0] = sign * total
    for c in range(3):
        k0, k1, k2, k3 = [spread(par, 4 * c + k, band, cols) for k in range(4)]
        mid[1 + c] = half * (m0 * k0 + m1 * k1 + m2 * k2 + m3 * k3)
    body(depth, 2, carry)


def main_block(dens, pix, xrecv, zrecv=None, xcorner=None):
    nz, rows, _ = dens.shape
    core, odd = where_am_i()

    def own(z):
        if isinstance(z, int):
            if z < 0:
                return pix[-1 - z]
            if z >= nz:
                return zrecv[z - nz]
        return dens[local_plane(core, nz, z)]

    def halo(z):
        if isinstance(z, int):
            if z < 0:
                return pixel_rows((xrecv[nz], xrecv[nz + 1]), z)
            if z >= nz:
                return xcorner[z - nz]
        return xrecv[nz - 1 - z]

    return Block(rows, jnp.where(odd == 1, 2, rows + 8 - 2), own, halo)


def far_forward_kernel(dens, pix, zrecv, lrecv, par, smooth, dxs, dys, rnorm, phis, edge, sig, mid, pixo, taus):
    nz, rows, _ = dens.shape
    core, odd = where_am_i()
    at = pl.multiple_of(odd * (rows - 8), 8)

    def own(z):
        if isinstance(z, int):
            if z < 0:
                return pix[-1 - z, pl.ds(at, 8)]
            if z >= nz:
                return zrecv[z - nz, pl.ds(at, 8)]
        return dens[local_plane(core, nz, z), pl.ds(at, 8)]

    def halo(z):
        if isinstance(z, int):
            if z < 0:
                return pixel_rows((lrecv[nz + 2], lrecv[nz + 3]), z)
            if z == nz:
                return lrecv[1]
            if z > nz:
                plane = lrecv[0]
                if z != nz + 2:
                    return plane
                up = jnp.concatenate([plane[1:], plane[:1]], axis=0)
                return jnp.where(odd == 1, jnp.concatenate([plane[HALO - 1 :], plane[: HALO - 1]], axis=0), up)
        return lrecv[nz + 1 - z]

    block = Block(8, jnp.where(odd == 1, 16 - 2, 2), own, halo)
    total = smooth_slab(block, core, nz, GROUP_FAR[0], smooth, taus, sig, pixo)
    total = smooth_seam(block, nz, smooth, taus, sig, pixo, total)
    shade_slab(8, nz, GROUP_FAR[1], total, par, smooth, taus, dxs, dys, rnorm, phis, edge, mid, pixo)


def main_smooth_kernel(dens, pix, xrecv, smooth, taus, sig, pixo, total):
    core, _ = where_am_i()
    block = main_block(dens, pix, xrecv)
    total[...] = smooth_slab(block, core, dens.shape[0], GROUP_MAIN[0], smooth, taus, sig, pixo)


def main_shade_kernel(smooth, taus, sig, pixo, total, dens, pix, zrecv, xrecv, xcorner, par, smooth_tail, sig_tail, dxs, dys, rnorm, phis, edge, mid, taus_tail):
    nz, rows, _ = dens.shape
    block = main_block(dens, pix, xrecv, zrecv, xcorner)
    smooth, taus, sig = Joined(smooth, smooth_tail, nz), Joined(taus, taus_tail, nz - 1), Joined(sig, sig_tail, nz - 1)
    whole = smooth_seam(block, nz, smooth, taus, sig, pixo, total[...])
    shade_slab(rows, nz, GROUP_MAIN[1], whole, par, smooth, taus, dxs, dys, rnorm, phis, edge, mid, pixo)


def prepare_block(band, depth, group, smooth, dxs, dys, rnorm, phis, edge, sig, pixo, palette, par, bx, by, bz, gained, damped, targets):
    cols = smooth.shape[2]
    sign = 1.0 - 2.0 * pixo[2]
    weight = pixo[0] * (1.0 / (2 * depth))
    lz, ly, lx = [spread(par, 12 + i, band, cols) for i in range(3)]
    for c, t in enumerate(lookup(palette, pixo[1])):
        targets[c] = t

    def body(z0, n, carry):
        out = Stores()
        planes = [smooth[z0 + i, pl.ds(0, band)] for i in range(n + 2)]
        edges = [edge[z0 + i] for i in range(n + 1)]
        rest = [(phis[z0 + i], rnorm[z0 + i], sig[z0 + i], dys[z0 + i], dxs[z0 + i]) for i in range(n)]
        for i in range(n):
            phi, r, sg, dy, dx = rest[i]
            dz = planes[i + 2] - planes[i]
            w = sign * (edges[i] - edges[i + 1])
            p = w * r
            q = p * (phi * r)
            out.put(bx, z0 + i, p * lx - q * dx)
            out.put(by, z0 + i, p * ly - q * dy)
            out.put(bz, z0 + i, p * lz - q * dz)
            out.put(gained, z0 + i, w * (1.0 + phi))
            out.put(damped, z0 + i, weight * sg)
        out.flush()
        return carry

    in_groups(body, depth + 2, group, 0)


def backward_block(band, depth, group, smooth, phis, edge, bx, by, bz, gained, damped, targets, mid, pixo, theirs, par, image, grads):
    cols = smooth.shape[2]
    back = pixo[2] == 1.0
    through_me, through_them = jnp.exp(-mid[0]), jnp.exp(-theirs[0])
    g, flow = [], jnp.zeros_like(through_me)
    for c in range(3):
        mine, other = mid[1 + c], theirs[1 + c]
        pic = jnp.where(back, other + through_them * mine, mine + through_me * other)
        image[c] = pic
        err = (pic - targets[c]) * (2.0 * depth)
        g.append(err)
        flow = flow + err * pic
    kappa = jnp.where(back, 0.5 * through_them, 0.5)
    g = [kappa * e for e in g]
    gam = []
    for k in range(4):
        k0, k1, k2 = [spread(par, 4 * c + k, band, cols) for c in range(3)]
        gam.append(g[0] * k0 + g[1] * k1 + g[2] * k2)
    queue = jnp.where(back, 0.0, -flow)

    def shade_back(z0, n, carry):
        run, part, last = carry
        out = Stores()
        rest = [[ref[z0 + i] for ref in (phis, bx, by, bz, gained, damped)] for i in range(n)]
        values = [smooth[z0 + i + 1, pl.ds(0, band)] for i in range(n)]
        edges = [edge[z0 + i] for i in range(n + 1)]
        for i in range(n):
            s = values[i]
            phi, dx, dy, dz, gain, damp = rest[i]
            near, far = edges[i], edges[i + 1]
            top = s * gam[3]
            inner = gam[2] + top
            outer = gam[1] + s * inner
            poly = gam[0] + s * outer
            slope = outer + s * (inner + top)
            h = poly + phi * poly
            mine = (near * h + run) * damp + gain * slope
            run = run + (near - far) * h
            az, ay, ax = dz * poly, dy * poly, dx * poly
            out.put(grads, z0 + i, part - az)
            part = mine + last
            part = part + (pltpu.roll(ay, 1, axis=0) - pltpu.roll(ay, band - 1, axis=0))
            part = part + (pltpu.roll(ax, 1, axis=1) - pltpu.roll(ax, cols - 1, axis=1))
            last = az
        out.flush()
        return run, part, last

    nil = jnp.zeros_like(through_me)
    in_groups(shade_back, depth + 2, group, (queue, nil, nil))


def smooth_transpose(band, depth, group, grads, emit):
    cols = grads.shape[2]

    def smooth_back(z0, n, carry):
        planes = [grads[z0 + i] for i in range(n + 2)]
        done = []
        for i in range(n):
            here = planes[i + 1]
            t = planes[i] + planes[i + 2] + 2.0 * here
            t = t + pltpu.roll(here, 1, axis=0) + pltpu.roll(here, band - 1, axis=0)
            t = t + pltpu.roll(here, 1, axis=1) + pltpu.roll(here, cols - 1, axis=1)
            done.append(t * 0.125)
            if len(done) == CHUNK:
                emit(z0 + i + 1 - CHUNK, done)
                done = []
        return carry

    in_groups(smooth_back, depth, group, 0, loop=band > 8)


def main_prepare_kernel(smooth, sig, smooth_tail, sig_tail, dxs, dys, rnorm, phis, edge, pixo, palette, par, *out):
    nz, rows, _ = dxs.shape
    nz = nz - 2
    smooth, sig = Joined(smooth, smooth_tail, nz), Joined(sig, sig_tail, nz - 1)
    prepare_block(rows, nz, GROUP_MAIN[2], smooth, dxs, dys, rnorm, phis, edge, sig, pixo, palette, par, *out)


def main_backward_kernel(smooth, smooth_tail, *refs):
    nz, rows = smooth.shape[0], refs[0].shape[1]
    backward_block(rows, nz, GROUP_MAIN[2], Joined(smooth, smooth_tail, nz), *refs)


def far_prepare_kernel(smooth, *refs):
    prepare_block(8, smooth.shape[0] - HALO, GROUP_FAR[2], smooth, *refs)


def main_result_kernel(grads, image, out, shown):
    nz, rows, _ = out.shape
    core, odd = where_am_i()
    shift = jnp.where(odd == 1, rows - 2, 2)
    for c in range(3):
        shown[c] = pltpu.roll(image[c], shift, axis=0)

    def emit(z0, values):
        values = [pltpu.roll(v, shift, axis=0) for v in values]
        for i, v in enumerate(values):
            out[local_plane(core, nz, z0 + i)] = v

    smooth_transpose(rows, nz, GROUP_MAIN[3], grads, emit)


def far_backward_kernel(*refs):
    res = refs[:13]
    near_grad, near_image, picture_h, out_h, image, grads, picture, out, sem = refs[13:]
    nz, rows, cols = out.shape
    size = CHUNK
    core, odd = where_am_i()
    shift = jnp.where(odd == 1, 2, rows - 2)
    row = lax.broadcasted_iota(jnp.int32, (rows, cols), 0)
    low = odd * (rows - 4)
    mask = (row >= low) & (row < low + 4)

    def emit(z0, values):
        for i in range(0, len(values), size):
            emit_chunk(z0 + i, values[i : i + size])

    def emit_chunk(z0, values):
        ats = [local_plane(core, nz, z0 + i) for i in range(len(values))]
        nears = [near_grad[at] for at in ats]
        both = [pltpu.roll(jnp.concatenate([v, v], axis=0), shift, axis=0) for v in values]
        both = [jnp.where(mask, b, v) for b, v in zip(both, nears)]
        for at, b in zip(ats, both):
            out[at] = b
        send(out, out_h, z0).start()

    def send(a, b, z0):
        at = pl.ds(jnp.where(core == 0, z0, nz - size - z0), size)
        return pltpu.make_async_copy(a.at[at], b.at[at], sem.at[z0 // size])

    backward_block(8, nz, GROUP_FAR[2], *res, image, grads)
    smooth_transpose(8, nz, GROUP_FAR[3], grads, emit)
    low = odd * (rows - 2)
    mask2 = (row >= low) & (row < low + 2)
    for c in range(3):
        both = pltpu.roll(jnp.concatenate([image[c], image[c]], axis=0), shift, axis=0)
        whole = jnp.where(mask2, both, near_image[c])
        picture[c] = jnp.where(core == 0, whole[:8], whole[8:])
    shown = pltpu.make_async_copy(picture, picture_h, sem.at[nz // size])
    shown.start()
    for z0 in range(0, nz, size):
        send(out, out_h, z0).wait()
    shown.wait()


def shards(density, absorption, view_dir, target_ids, palette, emission_coef, light):
    nz, rows, cols = density.shape
    tiles = lax.axis_size("tile")
    sds = resident

    zmsg, dens, pix, pal, par = call(
        fetch_kernel,
        (sds(HALO, rows, cols), sds(nz, rows, cols), sds(PIX, rows, cols), sds(*palette.shape), sds(15, 8, 128)),
        (density, absorption, target_ids, view_dir, palette, emission_coef, light),
        [HBM] * 7,
        scratch=[
            pltpu.VMEM((rows, cols), jnp.int32),
            pltpu.SMEM(view_dir.shape, jnp.int32),
            pltpu.SMEM(emission_coef.shape, F32),
            pltpu.SMEM(light.shape, F32),
            pltpu.SemaphoreType.DMA((7,)),
        ],
    )
    xmsg, lmsg = call(edges_kernel, (sds(nz + 2, HALO, cols), sds(nz + 2, HALO, cols)), (dens, pix), [VMEM] * 2)
    swap = [(0, 1), (1, 0)]
    near = [(i, i ^ 1) for i in range(tiles)]
    far = [(i, i + 1 if i % 2 else i - 1) for i in range(1, tiles - 1)]
    zrecv = lax.ppermute(zmsg, "depth", swap)
    xrecv = lax.ppermute(xmsg, "tile", near)
    lmsg = call(corner_kernel, sds(nz + 4, HALO, cols), (zrecv, lmsg), [VMEM, VMEM])
    lrecv = lax.ppermute(lmsg, "tile", far)
    xcorner = lax.ppermute(xrecv[:HALO], "depth", swap)

    def residuals(band):
        planes = nz + 2
        return (
            sds(nz + 4, band + 8, cols),
            *[sds(planes, band, cols)] * 4,
            sds(planes + 1, band, cols),
            sds(planes, band, cols),
            sds(4, band, cols),
            sds(PIX, band, cols),
        )

    parts = residuals(rows)
    smooth, taus, sig, pixo, total = call(
        main_smooth_kernel,
        (sds(nz, rows + 8, cols), sds(nz - 1, rows, cols), sds(nz - 1, rows, cols), parts[8], sds(rows, cols)),
        (dens, pix, xrecv),
        [VMEM] * 3,
    )
    xcorner, total = lax.optimization_barrier((xcorner, total))
    smooth_tail, sig_tail, dxs, dys, rnorm, phis, edge, mid = call(
        main_shade_kernel,
        (sds(4, rows + 8, cols), sds(3, rows, cols), *parts[1:6], parts[7]),
        (smooth, taus, sig, pixo, total, dens, pix, zrecv, xrecv, xcorner, par),
        [VMEM] * 11,
        scratch=[pltpu.VMEM((3, rows, cols), F32)],
    )
    theirs = lax.ppermute(mid, "depth", swap)

    def prepared(band):
        return (*[sds(nz + 2, band, cols)] * 5, sds(3, band, cols))

    ready = call(
        main_prepare_kernel,
        prepared(rows),
        (smooth, sig, smooth_tail, sig_tail, dxs, dys, rnorm, phis, edge, pixo, pal, par),
        [VMEM] * 12,
    )
    near_image, grads = call(
        main_backward_kernel,
        (sds(3, rows, cols), sds(nz + 2, rows, cols)),
        (smooth, smooth_tail, phis, edge, *ready, mid, pixo, theirs, par),
        [VMEM] * 14,
    )
    lrecv, near_image = lax.optimization_barrier((lrecv, near_image))
    smooth, dxs, dys, rnorm, phis, edge, sig, mid, pixo = call(
        far_forward_kernel,
        residuals(8),
        (dens, pix, zrecv, lrecv, par),
        [VMEM] * 5,
        scratch=[pltpu.VMEM((nz + 2, 8, cols), F32)],
    )
    theirs = lax.ppermute(mid, "depth", swap)
    near_image, pixo = lax.optimization_barrier((near_image, pixo))
    near_grad, near_image = call(main_result_kernel, (sds(nz, rows, cols), sds(3, rows, cols)), (grads, near_image), [VMEM] * 2)
    ready = call(
        far_prepare_kernel,
        prepared(8),
        (smooth, dxs, dys, rnorm, phis, edge, sig, pixo, pal, par),
        [VMEM] * 10,
    )
    picture, grad = call(
        far_backward_kernel,
        (jax.ShapeDtypeStruct((3, 8, cols), F32), jax.ShapeDtypeStruct((nz, rows, cols), F32)),
        (smooth, phis, edge, *ready, mid, pixo, theirs, par, near_grad, near_image),
        [VMEM] * 15,
        scratch=[
            pltpu.VMEM((3, 8, cols), F32),
            pltpu.VMEM((nz + 2, 8, cols), F32),
            pltpu.VMEM((3, 8, cols), F32),
            pltpu.VMEM((nz, rows, cols), F32),
            pltpu.SemaphoreType.DMA((nz // CHUNK + 1,)),
        ],
        out_specs=(HBM, HBM),
    )
    return picture, grad


def solution(mesh):
    placed = (P("depth", "tile", None), P("tile", None), P("tile"), P("tile", None), P(), P(), P())
    return jax.shard_map(
        shards,
        mesh=mesh,
        in_specs=placed,
        out_specs=(P(None, ("tile", "depth"), None), P("depth", "tile", None)),
        check_vma=False,
    )
```

```python
import jax
import jax.numpy as jnp
from jax import lax
from jax.experimental import pallas as pl
from jax.experimental.pallas import tpu as pltpu
from jax.sharding import PartitionSpec as P


F32 = jnp.float32
HALO = 4
PIX = 3
GROUP_MAIN = (10,16,17,16)
GROUP_FAR = (30,32,34,32)
CHUNK = 8
LATE = True
VMEM = pl.BlockSpec(memory_space=pltpu.VMEM)
HBM = pl.BlockSpec(memory_space=pl.ANY)


def call(kernel, outs, args, specs, scratch=(), cost=None, out_specs=None):
    args = [pltpu.with_memory_space_constraint(a, pltpu.VMEM if s is VMEM else pltpu.HBM) for a, s in zip(args, specs)]
    return pl.pallas_call(
        kernel,
        out_shape=outs,
        in_specs=specs,
        out_specs=out_specs or jax.tree.map(lambda _: VMEM, outs),
        scratch_shapes=scratch,
        cost_estimate=cost,
        compiler_params=pltpu.CompilerParams(vmem_limit_bytes=8 << 20),
    )(*args)


def resident(*shape):
    return pltpu.VMEM(shape, F32)


def where_am_i():
    return lax.axis_index("depth"), lax.rem(lax.axis_index("tile"), 2)


def local_plane(core, nz, z):
    return jnp.where(core == 0, z, nz - 1 - z)


def in_groups(body, count, group, carry, loop=False):
    full = count // group
    if loop:
        carry = lax.fori_loop(0, full, lambda i, c: body(i * group, group, c), carry)
    for i in range(0 if not loop else full, full):
        carry = body(i * group, group, carry)
    if count % group:
        carry = body(full * group, count % group, carry)
    return carry


class Joined:
    def __init__(self, head, tail, cut):
        self.head, self.tail, self.cut = head, tail, cut
        self.shape = (cut + tail.shape[0], *tail.shape[1:])

    def find(self, key):
        at, *rest = key if isinstance(key, tuple) else (key,)
        return (self.head, (at, *rest)) if at < self.cut else (self.tail, (at - self.cut, *rest))

    def __getitem__(self, key):
        ref, at = self.find(key)
        return ref[at]

    def __setitem__(self, key, value):
        ref, at = self.find(key)
        ref[at] = value


class Stores:
    def __init__(self):
        self.todo = []

    def put(self, ref, at, value):
        if LATE:
            self.todo.append((ref, at, value))
        else:
            ref[at] = value

    def flush(self):
        for ref, at, value in self.todo:
            ref[at] = value


def spread(par, i, rows, cols):
    t = par[i]
    t = jnp.concatenate([t] * (cols // t.shape[1]), axis=1)
    return jnp.concatenate([t] * (rows // t.shape[0]), axis=0)


def fetch_kernel(dens_h, absorb_h, ids_h, view_h, pal_h, coef_h, light_h, zmsg, dens, pix, pal, par, ids, view, coef, light, sem):
    nz, rows, cols = dens.shape
    core, _ = where_am_i()
    pairs = ((dens_h, dens), (view_h, view), (ids_h, ids), (absorb_h, pix.at[0]), (coef_h, coef), (light_h, light), (pal_h, pal))
    copies = [pltpu.make_async_copy(a, b, sem.at[i]) for i, (a, b) in enumerate(pairs)]
    for c in copies:
        c.start()
    for c in copies[1:]:
        c.wait()
    row = lax.broadcasted_iota(jnp.int32, (rows, cols), 0)
    seen = jnp.zeros((rows, cols), F32)
    for r in range(rows):
        seen = jnp.where(row == r, view[r].astype(F32), seen)
    pix[1] = ids[...].astype(F32)
    pix[2] = seen
    for i in range(3):
        for k in range(4):
            par[4 * i + k] = jnp.full(par.shape[1:], coef[i, k])
        value = light[i]
        if i == 0:
            value = jnp.where(core == 0, value, -value)
        par[12 + i] = jnp.full(par.shape[1:], value)
    copies[0].wait()
    for j in range(HALO):
        zmsg[j] = dens[local_plane(core, nz, nz - 1 - j)]


def edges_kernel(dens, pix, xmsg, lmsg):
    nz, rows, _ = dens.shape
    core, odd = where_am_i()

    def edges(head, tail, to):
        xmsg[to] = jnp.where(odd == 1, head, tail)
        lmsg[to] = jnp.where(odd == 1, tail, head)

    a, ids, view = pix[0], pix[1], pix[2]
    edges(jnp.concatenate([a[:2], ids[:2]], axis=0), jnp.concatenate([ids[rows - 2 :], a[rows - 2 :]], axis=0), nz)
    edges(view[:HALO], view[rows - HALO :], nz + 1)
    for j in range(nz):
        plane = dens[local_plane(core, nz, nz - 1 - j)]
        edges(plane[:HALO], plane[rows - HALO :], j)


def corner_kernel(zrecv, early, lmsg):
    rows = zrecv.shape[1]
    _, odd = where_am_i()
    lmsg[2:] = early[...]
    one, two, three = zrecv[0], zrecv[1], zrecv[2]
    lmsg[1] = jnp.where(odd == 1, one[rows - HALO :], one[:HALO])
    tail = jnp.concatenate([three[rows - 1 :], two[rows - HALO + 1 :]], axis=0)
    head = jnp.concatenate([two[: HALO - 1], three[:1]], axis=0)
    lmsg[0] = jnp.where(odd == 1, tail, head)


def lookup(palette, ids):
    rows, cols = ids.shape
    entries = palette.shape[1]
    index = ids.astype(jnp.int32)
    parts = []
    for c in range(3):
        strips = []
        for r in range(0, rows, 8):
            strip = []
            for x in range(0, cols, entries):
                table = jnp.broadcast_to(palette[c : c + 1, :], (8, entries))
                strip.append(jnp.take_along_axis(table, index[r : r + 8, x : x + entries], axis=1))
            strips.append(jnp.concatenate(strip, axis=1))
        parts.append(jnp.concatenate(strips, axis=0))
    return parts


def pixel_rows(planes, z):
    if z == -1:
        return planes[0]
    if z == -2:
        return jnp.concatenate([planes[0][2:], planes[0][:2]], axis=0)
    return planes[1]


class Block:
    def __init__(self, band, shift, own, halo):
        self.band, self.shift, self.own, self.halo = band, shift, own, halo

    def plane(self, z):
        h = self.halo(z)
        return pltpu.roll(jnp.concatenate([self.own(z), h, h], axis=0), self.shift, axis=0)


def pixels(block, core):
    a, ids, view = [block.plane(-1 - j)[: block.band] for j in range(PIX)]
    back = jnp.where(core == 0, view, 1.0 - view)
    return a, ids, back


def smooth_planes(block, first, n, signed, depth, smooth, taus, sig, total, lead=None):
    band, wide = block.band, block.band + 8
    out = Stores()
    zs = [first - 1 + i for i in range(n + 2)]
    planes = [lead if i == 0 and lead is not None else block.plane(z) for i, z in enumerate(zs)]
    for i in range(n):
        here = planes[i + 1]
        cols = here.shape[1]
        t = planes[i] + planes[i + 2] + 2.0 * here
        t = t + pltpu.roll(here, 1, axis=0) + pltpu.roll(here, wide - 1, axis=0)
        t = t + pltpu.roll(here, 1, axis=1) + pltpu.roll(here, cols - 1, axis=1)
        s = t * 0.125
        out.put(smooth, zs[i + 1] + 1, s)
        static = isinstance(first, int)
        if not static or first + i < depth + 2:
            soft = jnp.log(1.0 + jnp.exp(s[:band]))
            tau = signed * soft
            out.put(taus, zs[i + 1], tau)
            out.put(sig, zs[i + 1], 1.0 - jnp.exp(-soft))
            if not static or first + i < depth:
                total = total + tau
    out.flush()
    return total


def smooth_slab(block, core, depth, group, smooth, taus, sig, pixo):
    a, ids, back = pixels(block, core)
    signed = a * (1.0 / (2 * depth)) * (1.0 - 2.0 * back)
    pixo[0], pixo[1], pixo[2] = a, ids, back
    face = block.plane(0)
    smooth[0] = face * 0.125
    zero = jnp.zeros_like(face)
    total = smooth_planes(block, 0, 1, signed, depth, smooth, taus, sig, jnp.zeros_like(a), lead=zero)

    def body(z, n, total):
        return smooth_planes(block, z + 1, n, signed, depth, smooth, taus, sig, total)

    return in_groups(body, depth - 2, group, total, loop=block.band > 8)


def smooth_seam(block, depth, smooth, taus, sig, pixo, total):
    a, back = pixo[0], pixo[2]
    signed = a * (1.0 / (2 * depth)) * (1.0 - 2.0 * back)
    return smooth_planes(block, depth - 1, 4, signed, depth, smooth, taus, sig, total)


def shade_slab(band, depth, group, total, par, smooth, taus, dxs, dys, rnorm, phis, edge, mid, pixo):
    wide, cols = band + 8, smooth.shape[2]
    back = pixo[2]
    sign = 1.0 - 2.0 * back
    lz, ly, lx = [spread(par, 12 + i, band, cols) for i in range(3)]
    start = jnp.where(back == 1.0, total, 0.0)
    opened = jnp.exp(start)
    edge[0] = opened

    def body(z0, n, carry):
        run, seen, m0, m1, m2, m3 = carry
        out = Stores()
        planes = [smooth[z0 + i] for i in range(n + 2)]
        absorbed = [taus[z0 + i] for i in range(n)]
        for i in range(n):
            here = planes[i + 1]
            s = here[:band]
            dz = planes[i + 2][:band] - planes[i][:band]
            dy = (pltpu.roll(here, wide - 1, axis=0) - pltpu.roll(here, 1, axis=0))[:band]
            dx = pltpu.roll(s, cols - 1, axis=1) - pltpu.roll(s, 1, axis=1)
            r = lax.rsqrt(4.0 + dz * dz + dy * dy + dx * dx)
            phi = (dz * lz + dy * ly + dx * lx) * r
            run = run - absorbed[i]
            nxt = jnp.exp(run)
            for ref, v in ((dxs, dx), (dys, dy), (rnorm, r), (phis, phi)):
                out.put(ref, z0 + i, v)
            out.put(edge, z0 + i + 1, nxt)
            b = (seen - nxt) * (1.0 + phi)
            m0 = m0 + b
            b = b * s
            m1 = m1 + b
            b = b * s
            m2 = m2 + b
            b = b * s
            m3 = m3 + b
            seen = nxt
        out.flush()
        return run, seen, m0, m1, m2, m3

    nil = jnp.zeros_like(back)
    carry = in_groups(body, depth, group, (start, opened, nil, nil, nil, nil))
    _, _, m0, m1, m2, m3 = carry
    half = 0.5 * sign
    mid[0] = sign * total
    for c in range(3):
        k0, k1, k2, k3 = [spread(par, 4 * c + k, band, cols) for k in range(4)]
        mid[1 + c] = half * (m0 * k0 + m1 * k1 + m2 * k2 + m3 * k3)
    body(depth, 2, carry)


def main_block(dens, pix, xrecv, zrecv=None, xcorner=None):
    nz, rows, _ = dens.shape
    core, odd = where_am_i()

    def own(z):
        if isinstance(z, int):
            if z < 0:
                return pix[-1 - z]
            if z >= nz:
                return zrecv[z - nz]
        return dens[local_plane(core, nz, z)]

    def halo(z):
        if isinstance(z, int):
            if z < 0:
                return pixel_rows((xrecv[nz], xrecv[nz + 1]), z)
            if z >= nz:
                return xcorner[z - nz]
        return xrecv[nz - 1 - z]

    return Block(rows, jnp.where(odd == 1, 2, rows + 8 - 2), own, halo)


def far_forward_kernel(dens, pix, zrecv, lrecv, par, smooth, dxs, dys, rnorm, phis, edge, sig, mid, pixo, taus):
    nz, rows, _ = dens.shape
    core, odd = where_am_i()
    at = pl.multiple_of(odd * (rows - 8), 8)

    def own(z):
        if isinstance(z, int):
            if z < 0:
                return pix[-1 - z, pl.ds(at, 8)]
            if z >= nz:
                return zrecv[z - nz, pl.ds(at, 8)]
        return dens[local_plane(core, nz, z), pl.ds(at, 8)]

    def halo(z):
        if isinstance(z, int):
            if z < 0:
                return pixel_rows((lrecv[nz + 2], lrecv[nz + 3]), z)
            if z == nz:
                return lrecv[1]
            if z > nz:
                plane = lrecv[0]
                if z != nz + 2:
                    return plane
                up = jnp.concatenate([plane[1:], plane[:1]], axis=0)
                return jnp.where(odd == 1, jnp.concatenate([plane[HALO - 1 :], plane[: HALO - 1]], axis=0), up)
        return lrecv[nz + 1 - z]

    block = Block(8, jnp.where(odd == 1, 16 - 2, 2), own, halo)
    total = smooth_slab(block, core, nz, GROUP_FAR[0], smooth, taus, sig, pixo)
    total = smooth_seam(block, nz, smooth, taus, sig, pixo, total)
    shade_slab(8, nz, GROUP_FAR[1], total, par, smooth, taus, dxs, dys, rnorm, phis, edge, mid, pixo)


def main_smooth_kernel(dens, pix, xrecv, smooth, taus, sig, pixo, total):
    core, _ = where_am_i()
    block = main_block(dens, pix, xrecv)
    total[...] = smooth_slab(block, core, dens.shape[0], GROUP_MAIN[0], smooth, taus, sig, pixo)


def main_shade_kernel(smooth, taus, sig, pixo, total, dens, pix, zrecv, xrecv, xcorner, par, smooth_tail, sig_tail, dxs, dys, rnorm, phis, edge, mid, taus_tail):
    nz, rows, _ = dens.shape
    block = main_block(dens, pix, xrecv, zrecv, xcorner)
    smooth, taus, sig = Joined(smooth, smooth_tail, nz), Joined(taus, taus_tail, nz - 1), Joined(sig, sig_tail, nz - 1)
    whole = smooth_seam(block, nz, smooth, taus, sig, pixo, total[...])
    shade_slab(rows, nz, GROUP_MAIN[1], whole, par, smooth, taus, dxs, dys, rnorm, phis, edge, mid, pixo)


def prepare_block(band, depth, group, smooth, dxs, dys, rnorm, phis, edge, sig, pixo, palette, par, bx, by, bz, gained, damped, targets):
    cols = smooth.shape[2]
    sign = 1.0 - 2.0 * pixo[2]
    weight = pixo[0] * (1.0 / (2 * depth))
    lz, ly, lx = [spread(par, 12 + i, band, cols) for i in range(3)]
    for c, t in enumerate(lookup(palette, pixo[1])):
        targets[c] = t

    def body(z0, n, carry):
        out = Stores()
        planes = [smooth[z0 + i, pl.ds(0, band)] for i in range(n + 2)]
        edges = [edge[z0 + i] for i in range(n + 1)]
        rest = [(phis[z0 + i], rnorm[z0 + i], sig[z0 + i], dys[z0 + i], dxs[z0 + i]) for i in range(n)]
        for i in range(n):
            phi, r, sg, dy, dx = rest[i]
            dz = planes[i + 2] - planes[i]
            w = sign * (edges[i] - edges[i + 1])
            p = w * r
            q = p * (phi * r)
            out.put(bx, z0 + i, p * lx - q * dx)
            out.put(by, z0 + i, p * ly - q * dy)
            out.put(bz, z0 + i, p * lz - q * dz)
            out.put(gained, z0 + i, w * (1.0 + phi))
            out.put(damped, z0 + i, weight * sg)
        out.flush()
        return carry

    in_groups(body, depth + 2, group, 0)


def combine(band, depth, targets, mid, pixo, theirs, par, image):
    cols = mid.shape[2]
    back = pixo[2] == 1.0
    through_me, through_them = jnp.exp(-mid[0]), jnp.exp(-theirs[0])
    g, flow = [], jnp.zeros_like(through_me)
    for c in range(3):
        mine, other = mid[1 + c], theirs[1 + c]
        pic = jnp.where(back, other + through_them * mine, mine + through_me * other)
        image[c] = pic
        err = (pic - targets[c]) * (2.0 * depth)
        g.append(err)
        flow = flow + err * pic
    kappa = jnp.where(back, 0.5 * through_them, 0.5)
    g = [kappa * e for e in g]
    gam = []
    for k in range(4):
        k0, k1, k2 = [spread(par, 4 * c + k, band, cols) for c in range(3)]
        gam.append(g[0] * k0 + g[1] * k1 + g[2] * k2)
    queue = jnp.where(back, 0.0, -flow)

    nil = jnp.zeros_like(through_me)
    return gam, (queue, nil, nil)


def shade_transpose(band, first, count, group, gam, carry, smooth, phis, edge, bx, by, bz, gained, damped, grads):
    cols = bx.shape[2]

    def shade_back(z0, n, carry):
        run, part, last = carry
        out = Stores()
        rest = [[ref[z0 + i] for ref in (phis, bx, by, bz, gained, damped)] for i in range(n)]
        values = [smooth[z0 + i + 1, pl.ds(0, band)] for i in range(n)]
        edges = [edge[z0 + i] for i in range(n + 1)]
        for i in range(n):
            s = values[i]
            phi, dx, dy, dz, gain, damp = rest[i]
            near, far = edges[i], edges[i + 1]
            top = s * gam[3]
            inner = gam[2] + top
            outer = gam[1] + s * inner
            poly = gam[0] + s * outer
            slope = outer + s * (inner + top)
            h = poly + phi * poly
            mine = (near * h + run) * damp + gain * slope
            run = run + (near - far) * h
            az, ay, ax = dz * poly, dy * poly, dx * poly
            out.put(grads, z0 + i, part - az)
            part = mine + last
            part = part + (pltpu.roll(ay, 1, axis=0) - pltpu.roll(ay, band - 1, axis=0))
            part = part + (pltpu.roll(ax, 1, axis=1) - pltpu.roll(ax, cols - 1, axis=1))
            last = az
        out.flush()
        return run, part, last

    def step(z0, n, carry):
        return shade_back(first + z0, n, carry)

    return in_groups(step, count, group, carry)


def smooth_transpose(band, depth, group, grads, emit):
    cols = grads.shape[2]

    def smooth_back(z0, n, carry):
        planes = [grads[z0 + i] for i in range(n + 2)]
        done = []
        for i in range(n):
            here = planes[i + 1]
            t = planes[i] + planes[i + 2] + 2.0 * here
            t = t + pltpu.roll(here, 1, axis=0) + pltpu.roll(here, band - 1, axis=0)
            t = t + pltpu.roll(here, 1, axis=1) + pltpu.roll(here, cols - 1, axis=1)
            done.append(t * 0.125)
            if len(done) == CHUNK:
                emit(z0 + i + 1 - CHUNK, done)
                done = []
        return carry

    in_groups(smooth_back, depth, group, 0)


def main_prepare_kernel(smooth, sig, smooth_tail, sig_tail, dxs, dys, rnorm, phis, edge, pixo, palette, par, *out):
    nz, rows, _ = dxs.shape
    nz = nz - 2
    smooth, sig = Joined(smooth, smooth_tail, nz), Joined(sig, sig_tail, nz - 1)
    prepare_block(rows, nz, GROUP_MAIN[2], smooth, dxs, dys, rnorm, phis, edge, sig, pixo, palette, par, *out)


def main_backward_kernel(smooth, phis, edge, bx, by, bz, gained, damped, targets, mid, pixo, theirs, par, image, grads, state):
    rows = image.shape[1]
    nz = phis.shape[0] - 2
    gam, carry = combine(rows, nz, targets, mid, pixo, theirs, par, image)
    carry = shade_transpose(rows, 0, grads.shape[0], grads.shape[0], gam, carry, smooth, phis, edge, bx, by, bz, gained, damped, grads)
    for i, v in enumerate((*gam, *carry)):
        state[i] = v


def far_prepare_kernel(smooth, *refs):
    prepare_block(8, smooth.shape[0] - HALO, GROUP_FAR[2], smooth, *refs)


def main_result_kernel(state, early, smooth, smooth_tail, phis, edge, bx, by, bz, gained, damped, image, out, shown, late):
    nz, rows, _ = out.shape
    core, odd = where_am_i()
    shift = jnp.where(odd == 1, rows - 2, 2)
    for c in range(3):
        shown[c] = pltpu.roll(image[c], shift, axis=0)

    def emit(z0, values):
        values = [pltpu.roll(v, shift, axis=0) for v in values]
        for i, v in enumerate(values):
            out[local_plane(core, nz, z0 + i)] = v

    first = early.shape[0]
    smooth = Joined(smooth, smooth_tail, nz)
    gam, carry = [state[i] for i in range(4)], tuple(state[4 + i] for i in range(3))
    grads = Joined(early, late, first)
    shade_transpose(rows, first, nz + 2 - first, nz + 2 - first, gam, carry, smooth, phis, edge, bx, by, bz, gained, damped, grads)
    smooth_transpose(rows, nz, GROUP_MAIN[3], grads, emit)


def far_backward_kernel(*refs):
    res = refs[:13]
    near_grad, near_image, picture_h, out_h, image, grads, picture, out, sem = refs[13:]
    nz, rows, cols = out.shape
    size = CHUNK
    core, odd = where_am_i()
    shift = jnp.where(odd == 1, 2, rows - 2)
    row = lax.broadcasted_iota(jnp.int32, (rows, cols), 0)
    low = odd * (rows - 4)
    mask = (row >= low) & (row < low + 4)

    def emit(z0, values):
        for i in range(0, len(values), size):
            emit_chunk(z0 + i, values[i : i + size])

    def emit_chunk(z0, values):
        ats = [local_plane(core, nz, z0 + i) for i in range(len(values))]
        nears = [near_grad[at] for at in ats]
        both = [pltpu.roll(jnp.concatenate([v, v], axis=0), shift, axis=0) for v in values]
        both = [jnp.where(mask, b, v) for b, v in zip(both, nears)]
        for at, b in zip(ats, both):
            out[at] = b
        send(out, out_h, z0).start()

    def send(a, b, z0):
        at = pl.ds(jnp.where(core == 0, z0, nz - size - z0), size)
        return pltpu.make_async_copy(a.at[at], b.at[at], sem.at[z0 // size])

    smooth, phis, edge, bx, by, bz, gained, damped, targets, mid, pixo, theirs, par = res
    gam, carry = combine(8, nz, targets, mid, pixo, theirs, par, image)
    shade_transpose(8, 0, nz + 2, GROUP_FAR[2], gam, carry, smooth, phis, edge, bx, by, bz, gained, damped, grads)
    smooth_transpose(8, nz, GROUP_FAR[3], grads, emit)
    low = odd * (rows - 2)
    mask2 = (row >= low) & (row < low + 2)
    for c in range(3):
        both = pltpu.roll(jnp.concatenate([image[c], image[c]], axis=0), shift, axis=0)
        whole = jnp.where(mask2, both, near_image[c])
        picture[c] = jnp.where(core == 0, whole[:8], whole[8:])
    shown = pltpu.make_async_copy(picture, picture_h, sem.at[nz // size])
    shown.start()
    for z0 in range(0, nz, size):
        send(out, out_h, z0).wait()
    shown.wait()


def shards(density, absorption, view_dir, target_ids, palette, emission_coef, light):
    nz, rows, cols = density.shape
    tiles = lax.axis_size("tile")
    sds = resident

    zmsg, dens, pix, pal, par = call(
        fetch_kernel,
        (sds(HALO, rows, cols), sds(nz, rows, cols), sds(PIX, rows, cols), sds(*palette.shape), sds(15, 8, 128)),
        (density, absorption, target_ids, view_dir, palette, emission_coef, light),
        [HBM] * 7,
        scratch=[
            pltpu.VMEM((rows, cols), jnp.int32),
            pltpu.SMEM(view_dir.shape, jnp.int32),
            pltpu.SMEM(emission_coef.shape, F32),
            pltpu.SMEM(light.shape, F32),
            pltpu.SemaphoreType.DMA((7,)),
        ],
    )
    xmsg, lmsg = call(edges_kernel, (sds(nz + 2, HALO, cols), sds(nz + 2, HALO, cols)), (dens, pix), [VMEM] * 2)
    swap = [(0, 1), (1, 0)]
    near = [(i, i ^ 1) for i in range(tiles)]
    far = [(i, i + 1 if i % 2 else i - 1) for i in range(1, tiles - 1)]
    zrecv = lax.ppermute(zmsg, "depth", swap)
    xrecv = lax.ppermute(xmsg, "tile", near)
    lmsg = call(corner_kernel, sds(nz + 4, HALO, cols), (zrecv, lmsg), [VMEM, VMEM])
    lrecv = lax.ppermute(lmsg, "tile", far)
    xcorner = lax.ppermute(xrecv[:HALO], "depth", swap)

    def residuals(band):
        planes = nz + 2
        return (
            sds(nz + 4, band + 8, cols),
            *[sds(planes, band, cols)] * 4,
            sds(planes + 1, band, cols),
            sds(planes, band, cols),
            sds(4, band, cols),
            sds(PIX, band, cols),
        )

    parts = residuals(rows)
    smooth, taus, sig, pixo, total = call(
        main_smooth_kernel,
        (sds(nz, rows + 8, cols), sds(nz - 1, rows, cols), sds(nz - 1, rows, cols), parts[8], sds(rows, cols)),
        (dens, pix, xrecv),
        [VMEM] * 3,
    )
    xcorner, total = lax.optimization_barrier((xcorner, total))
    smooth_tail, sig_tail, dxs, dys, rnorm, phis, edge, mid = call(
        main_shade_kernel,
        (sds(4, rows + 8, cols), sds(3, rows, cols), *parts[1:6], parts[7]),
        (smooth, taus, sig, pixo, total, dens, pix, zrecv, xrecv, xcorner, par),
        [VMEM] * 11,
        scratch=[pltpu.VMEM((3, rows, cols), F32)],
    )
    theirs = lax.ppermute(mid, "depth", swap)

    def prepared(band):
        return (*[sds(nz + 2, band, cols)] * 5, sds(3, band, cols))

    ready = call(
        main_prepare_kernel,
        prepared(rows),
        (smooth, sig, smooth_tail, sig_tail, dxs, dys, rnorm, phis, edge, pixo, pal, par),
        [VMEM] * 12,
    )
    half = nz // 2 + 1
    near_image, early, state = call(
        main_backward_kernel,
        (sds(3, rows, cols), sds(half, rows, cols), sds(7, rows, cols)),
        (smooth, phis, edge, *ready, mid, pixo, theirs, par),
        [VMEM] * 13,
    )
    main = (early, smooth, smooth_tail, phis, edge, *ready[:5])
    lrecv, near_image = lax.optimization_barrier((lrecv, near_image))
    smooth, dxs, dys, rnorm, phis, edge, sig, mid, pixo = call(
        far_forward_kernel,
        residuals(8),
        (dens, pix, zrecv, lrecv, par),
        [VMEM] * 5,
        scratch=[pltpu.VMEM((nz + 2, 8, cols), F32)],
    )
    theirs = lax.ppermute(mid, "depth", swap)
    near_image, state, pixo = lax.optimization_barrier((near_image, state, pixo))
    near_grad, near_image = call(
        main_result_kernel,
        (sds(nz, rows, cols), sds(3, rows, cols)),
        (state, *main, near_image),
        [VMEM] * 12,
        scratch=[pltpu.VMEM((nz + 2 - half, rows, cols), F32)],
    )
    ready = call(
        far_prepare_kernel,
        prepared(8),
        (smooth, dxs, dys, rnorm, phis, edge, sig, pixo, pal, par),
        [VMEM] * 10,
    )
    picture, grad = call(
        far_backward_kernel,
        (jax.ShapeDtypeStruct((3, 8, cols), F32), jax.ShapeDtypeStruct((nz, rows, cols), F32)),
        (smooth, phis, edge, *ready, mid, pixo, theirs, par, near_grad, near_image),
        [VMEM] * 15,
        scratch=[
            pltpu.VMEM((3, 8, cols), F32),
            pltpu.VMEM((nz + 2, 8, cols), F32),
            pltpu.VMEM((3, 8, cols), F32),
            pltpu.VMEM((nz, rows, cols), F32),
            pltpu.SemaphoreType.DMA((nz // CHUNK + 1,)),
        ],
        out_specs=(HBM, HBM),
    )
    return picture, grad


def solution(mesh):
    placed = (P("depth", "tile", None), P("tile", None), P("tile"), P("tile", None), P(), P(), P())
    return jax.shard_map(
        shards,
        mesh=mesh,
        in_specs=placed,
        out_specs=(P(None, ("tile", "depth"), None), P("depth", "tile", None)),
        check_vma=False,
    )
```

```python
import jax
import jax.numpy as jnp
from jax import lax
from jax.experimental import pallas as pl
from jax.experimental.pallas import tpu as pltpu
from jax.sharding import PartitionSpec as P


F32 = jnp.float32
HALO = 4
PIX = 3
GROUP_MAIN = (10,16,17,16)
GROUP_FAR = (30,32,34,32)
CHUNK = 8
LATE = True
VMEM = pl.BlockSpec(memory_space=pltpu.VMEM)
HBM = pl.BlockSpec(memory_space=pl.ANY)


def call(kernel, outs, args, specs, scratch=(), cost=None, out_specs=None):
    args = [pltpu.with_memory_space_constraint(a, pltpu.VMEM if s is VMEM else pltpu.HBM) for a, s in zip(args, specs)]
    return pl.pallas_call(
        kernel,
        out_shape=outs,
        in_specs=specs,
        out_specs=out_specs or jax.tree.map(lambda _: VMEM, outs),
        scratch_shapes=scratch,
        cost_estimate=cost,
        compiler_params=pltpu.CompilerParams(vmem_limit_bytes=8 << 20),
    )(*args)


def resident(*shape):
    return pltpu.VMEM(shape, F32)


def where_am_i():
    return lax.axis_index("depth"), lax.rem(lax.axis_index("tile"), 2)


def local_plane(core, nz, z):
    return jnp.where(core == 0, z, nz - 1 - z)


def in_groups(body, count, group, carry, loop=False):
    full = count // group
    if loop:
        carry = lax.fori_loop(0, full, lambda i, c: body(i * group, group, c), carry)
    for i in range(0 if not loop else full, full):
        carry = body(i * group, group, carry)
    if count % group:
        carry = body(full * group, count % group, carry)
    return carry


class Joined:
    def __init__(self, head, tail, cut):
        self.head, self.tail, self.cut = head, tail, cut
        self.shape = (cut + tail.shape[0], *tail.shape[1:])

    def find(self, key):
        at, *rest = key if isinstance(key, tuple) else (key,)
        return (self.head, (at, *rest)) if at < self.cut else (self.tail, (at - self.cut, *rest))

    def __getitem__(self, key):
        ref, at = self.find(key)
        return ref[at]

    def __setitem__(self, key, value):
        ref, at = self.find(key)
        ref[at] = value


class Stores:
    def __init__(self):
        self.todo = []

    def put(self, ref, at, value):
        if LATE:
            self.todo.append((ref, at, value))
        else:
            ref[at] = value

    def flush(self):
        for ref, at, value in self.todo:
            ref[at] = value


def spread(par, i, rows, cols):
    t = par[i]
    t = jnp.concatenate([t] * (cols // t.shape[1]), axis=1)
    return jnp.concatenate([t] * (rows // t.shape[0]), axis=0)


def fetch_kernel(dens_h, absorb_h, ids_h, view_h, pal_h, coef_h, light_h, zmsg, pix, pal, par, ids, view, coef, light, sem):
    nz, rows, cols = dens_h.shape
    core, _ = where_am_i()
    seam = [(dens_h.at[local_plane(core, nz, nz - 1 - j)], zmsg.at[j]) for j in range(HALO)]
    pairs = (*seam, (view_h, view), (ids_h, ids), (absorb_h, pix.at[0]), (coef_h, coef), (light_h, light), (pal_h, pal))
    copies = [pltpu.make_async_copy(a, b, sem.at[i]) for i, (a, b) in enumerate(pairs)]
    for c in copies:
        c.start()
    for c in copies[HALO:]:
        c.wait()
    row = lax.broadcasted_iota(jnp.int32, (rows, cols), 0)
    seen = jnp.zeros((rows, cols), F32)
    for r in range(rows):
        seen = jnp.where(row == r, view[r].astype(F32), seen)
    pix[1] = ids[...].astype(F32)
    pix[2] = seen
    for i in range(3):
        for k in range(4):
            par[4 * i + k] = jnp.full(par.shape[1:], coef[i, k])
        value = light[i]
        if i == 0:
            value = jnp.where(core == 0, value, -value)
        par[12 + i] = jnp.full(par.shape[1:], value)
    for c in copies[:HALO]:
        c.wait()


def edges_kernel(dens, pix, xmsg, lmsg):
    nz, rows, _ = dens.shape
    core, odd = where_am_i()

    def edges(head, tail, to):
        xmsg[to] = jnp.where(odd == 1, head, tail)
        lmsg[to] = jnp.where(odd == 1, tail, head)

    a, ids, view = pix[0], pix[1], pix[2]
    edges(jnp.concatenate([a[:2], ids[:2]], axis=0), jnp.concatenate([ids[rows - 2 :], a[rows - 2 :]], axis=0), nz)
    edges(view[:HALO], view[rows - HALO :], nz + 1)
    for j in range(nz):
        plane = dens[local_plane(core, nz, nz - 1 - j)]
        edges(plane[:HALO], plane[rows - HALO :], j)


def corner_kernel(zrecv, early, lmsg):
    rows = zrecv.shape[1]
    _, odd = where_am_i()
    lmsg[2:] = early[...]
    one, two, three = zrecv[0], zrecv[1], zrecv[2]
    lmsg[1] = jnp.where(odd == 1, one[rows - HALO :], one[:HALO])
    tail = jnp.concatenate([three[rows - 1 :], two[rows - HALO + 1 :]], axis=0)
    head = jnp.concatenate([two[: HALO - 1], three[:1]], axis=0)
    lmsg[0] = jnp.where(odd == 1, tail, head)


def lookup(palette, ids):
    rows, cols = ids.shape
    entries = palette.shape[1]
    index = ids.astype(jnp.int32)
    parts = []
    for c in range(3):
        strips = []
        for r in range(0, rows, 8):
            strip = []
            for x in range(0, cols, entries):
                table = jnp.broadcast_to(palette[c : c + 1, :], (8, entries))
                strip.append(jnp.take_along_axis(table, index[r : r + 8, x : x + entries], axis=1))
            strips.append(jnp.concatenate(strip, axis=1))
        parts.append(jnp.concatenate(strips, axis=0))
    return parts


def pixel_rows(planes, z):
    if z == -1:
        return planes[0]
    if z == -2:
        return jnp.concatenate([planes[0][2:], planes[0][:2]], axis=0)
    return planes[1]


class Block:
    def __init__(self, band, shift, own, halo):
        self.band, self.shift, self.own, self.halo = band, shift, own, halo

    def plane(self, z):
        h = self.halo(z)
        return pltpu.roll(jnp.concatenate([self.own(z), h, h], axis=0), self.shift, axis=0)


def pixels(block, core):
    a, ids, view = [block.plane(-1 - j)[: block.band] for j in range(PIX)]
    back = jnp.where(core == 0, view, 1.0 - view)
    return a, ids, back


def smooth_planes(block, first, n, signed, depth, smooth, taus, sig, total, lead=None):
    band, wide = block.band, block.band + 8
    out = Stores()
    zs = [first - 1 + i for i in range(n + 2)]
    planes = [lead if i == 0 and lead is not None else block.plane(z) for i, z in enumerate(zs)]
    for i in range(n):
        here = planes[i + 1]
        cols = here.shape[1]
        t = planes[i] + planes[i + 2] + 2.0 * here
        t = t + pltpu.roll(here, 1, axis=0) + pltpu.roll(here, wide - 1, axis=0)
        t = t + pltpu.roll(here, 1, axis=1) + pltpu.roll(here, cols - 1, axis=1)
        s = t * 0.125
        out.put(smooth, zs[i + 1] + 1, s)
        static = isinstance(first, int)
        if not static or first + i < depth + 2:
            soft = jnp.log(1.0 + jnp.exp(s[:band]))
            tau = signed * soft
            out.put(taus, zs[i + 1], tau)
            out.put(sig, zs[i + 1], 1.0 - jnp.exp(-soft))
            if not static or first + i < depth:
                total = total + tau
    out.flush()
    return total


def smooth_slab(block, core, depth, group, smooth, taus, sig, pixo):
    a, ids, back = pixels(block, core)
    signed = a * (1.0 / (2 * depth)) * (1.0 - 2.0 * back)
    pixo[0], pixo[1], pixo[2] = a, ids, back
    face = block.plane(0)
    smooth[0] = face * 0.125
    zero = jnp.zeros_like(face)
    total = smooth_planes(block, 0, 1, signed, depth, smooth, taus, sig, jnp.zeros_like(a), lead=zero)

    def body(z, n, total):
        return smooth_planes(block, z + 1, n, signed, depth, smooth, taus, sig, total)

    return in_groups(body, depth - 2, group, total, loop=block.band > 8)


def smooth_seam(block, depth, smooth, taus, sig, pixo, total):
    a, back = pixo[0], pixo[2]
    signed = a * (1.0 / (2 * depth)) * (1.0 - 2.0 * back)
    return smooth_planes(block, depth - 1, 4, signed, depth, smooth, taus, sig, total)


def shade_slab(band, depth, group, total, par, smooth, taus, dxs, dys, rnorm, phis, edge, mid, pixo):
    wide, cols = band + 8, smooth.shape[2]
    back = pixo[2]
    sign = 1.0 - 2.0 * back
    lz, ly, lx = [spread(par, 12 + i, band, cols) for i in range(3)]
    start = jnp.where(back == 1.0, total, 0.0)
    opened = jnp.exp(start)
    edge[0] = opened

    def body(z0, n, carry):
        run, seen, m0, m1, m2, m3 = carry
        out = Stores()
        planes = [smooth[z0 + i] for i in range(n + 2)]
        absorbed = [taus[z0 + i] for i in range(n)]
        for i in range(n):
            here = planes[i + 1]
            s = here[:band]
            dz = planes[i + 2][:band] - planes[i][:band]
            dy = (pltpu.roll(here, wide - 1, axis=0) - pltpu.roll(here, 1, axis=0))[:band]
            dx = pltpu.roll(s, cols - 1, axis=1) - pltpu.roll(s, 1, axis=1)
            r = lax.rsqrt(4.0 + dz * dz + dy * dy + dx * dx)
            phi = (dz * lz + dy * ly + dx * lx) * r
            run = run - absorbed[i]
            nxt = jnp.exp(run)
            for ref, v in ((dxs, dx), (dys, dy), (rnorm, r), (phis, phi)):
                out.put(ref, z0 + i, v)
            out.put(edge, z0 + i + 1, nxt)
            b = (seen - nxt) * (1.0 + phi)
            m0 = m0 + b
            b = b * s
            m1 = m1 + b
            b = b * s
            m2 = m2 + b
            b = b * s
            m3 = m3 + b
            seen = nxt
        out.flush()
        return run, seen, m0, m1, m2, m3

    nil = jnp.zeros_like(back)
    carry = in_groups(body, depth, group, (start, opened, nil, nil, nil, nil))
    _, _, m0, m1, m2, m3 = carry
    half = 0.5 * sign
    mid[0] = sign * total
    for c in range(3):
        k0, k1, k2, k3 = [spread(par, 4 * c + k, band, cols) for k in range(4)]
        mid[1 + c] = half * (m0 * k0 + m1 * k1 + m2 * k2 + m3 * k3)
    body(depth, 2, carry)


def main_block(dens, pix, xrecv, zrecv=None, xcorner=None):
    nz, rows, _ = dens.shape
    core, odd = where_am_i()

    def own(z):
        if isinstance(z, int):
            if z < 0:
                return pix[-1 - z]
            if z >= nz:
                return zrecv[z - nz]
        return dens[local_plane(core, nz, z)]

    def halo(z):
        if isinstance(z, int):
            if z < 0:
                return pixel_rows((xrecv[nz], xrecv[nz + 1]), z)
            if z >= nz:
                return xcorner[z - nz]
        return xrecv[nz - 1 - z]

    return Block(rows, jnp.where(odd == 1, 2, rows + 8 - 2), own, halo)


def far_forward_kernel(dens, pix, zrecv, lrecv, par, smooth, dxs, dys, rnorm, phis, edge, sig, mid, pixo, taus):
    nz, rows, _ = dens.shape
    core, odd = where_am_i()
    at = pl.multiple_of(odd * (rows - 8), 8)

    def own(z):
        if isinstance(z, int):
            if z < 0:
                return pix[-1 - z, pl.ds(at, 8)]
            if z >= nz:
                return zrecv[z - nz, pl.ds(at, 8)]
        return dens[local_plane(core, nz, z), pl.ds(at, 8)]

    def halo(z):
        if isinstance(z, int):
            if z < 0:
                return pixel_rows((lrecv[nz + 2], lrecv[nz + 3]), z)
            if z == nz:
                return lrecv[1]
            if z > nz:
                plane = lrecv[0]
                if z != nz + 2:
                    return plane
                up = jnp.concatenate([plane[1:], plane[:1]], axis=0)
                return jnp.where(odd == 1, jnp.concatenate([plane[HALO - 1 :], plane[: HALO - 1]], axis=0), up)
        return lrecv[nz + 1 - z]

    block = Block(8, jnp.where(odd == 1, 16 - 2, 2), own, halo)
    total = smooth_slab(block, core, nz, GROUP_FAR[0], smooth, taus, sig, pixo)
    total = smooth_seam(block, nz, smooth, taus, sig, pixo, total)
    shade_slab(8, nz, GROUP_FAR[1], total, par, smooth, taus, dxs, dys, rnorm, phis, edge, mid, pixo)


def main_smooth_kernel(dens, pix, xrecv, smooth, taus, sig, pixo, total):
    core, _ = where_am_i()
    block = main_block(dens, pix, xrecv)
    total[...] = smooth_slab(block, core, dens.shape[0], GROUP_MAIN[0], smooth, taus, sig, pixo)


def main_shade_kernel(smooth, taus, sig, pixo, total, dens, pix, zrecv, xrecv, xcorner, par, smooth_tail, sig_tail, dxs, dys, rnorm, phis, edge, mid, taus_tail):
    nz, rows, _ = dens.shape
    block = main_block(dens, pix, xrecv, zrecv, xcorner)
    smooth, taus, sig = Joined(smooth, smooth_tail, nz), Joined(taus, taus_tail, nz - 1), Joined(sig, sig_tail, nz - 1)
    whole = smooth_seam(block, nz, smooth, taus, sig, pixo, total[...])
    shade_slab(rows, nz, GROUP_MAIN[1], whole, par, smooth, taus, dxs, dys, rnorm, phis, edge, mid, pixo)


def prepare_block(band, depth, group, smooth, dxs, dys, rnorm, phis, edge, sig, pixo, palette, par, bx, by, bz, gained, damped, targets):
    cols = smooth.shape[2]
    sign = 1.0 - 2.0 * pixo[2]
    weight = pixo[0] * (1.0 / (2 * depth))
    lz, ly, lx = [spread(par, 12 + i, band, cols) for i in range(3)]
    for c, t in enumerate(lookup(palette, pixo[1])):
        targets[c] = t

    def body(z0, n, carry):
        out = Stores()
        planes = [smooth[z0 + i, pl.ds(0, band)] for i in range(n + 2)]
        edges = [edge[z0 + i] for i in range(n + 1)]
        rest = [(phis[z0 + i], rnorm[z0 + i], sig[z0 + i], dys[z0 + i], dxs[z0 + i]) for i in range(n)]
        for i in range(n):
            phi, r, sg, dy, dx = rest[i]
            dz = planes[i + 2] - planes[i]
            w = sign * (edges[i] - edges[i + 1])
            p = w * r
            q = p * (phi * r)
            out.put(bx, z0 + i, p * lx - q * dx)
            out.put(by, z0 + i, p * ly - q * dy)
            out.put(bz, z0 + i, p * lz - q * dz)
            out.put(gained, z0 + i, w * (1.0 + phi))
            out.put(damped, z0 + i, weight * sg)
        out.flush()
        return carry

    in_groups(body, depth + 2, group, 0)


def backward_block(band, depth, group, smooth, phis, edge, bx, by, bz, gained, damped, targets, mid, pixo, theirs, par, image, grads):
    cols = smooth.shape[2]
    back = pixo[2] == 1.0
    through_me, through_them = jnp.exp(-mid[0]), jnp.exp(-theirs[0])
    g, flow = [], jnp.zeros_like(through_me)
    for c in range(3):
        mine, other = mid[1 + c], theirs[1 + c]
        pic = jnp.where(back, other + through_them * mine, mine + through_me * other)
        image[c] = pic
        err = (pic - targets[c]) * (2.0 * depth)
        g.append(err)
        flow = flow + err * pic
    kappa = jnp.where(back, 0.5 * through_them, 0.5)
    g = [kappa * e for e in g]
    gam = []
    for k in range(4):
        k0, k1, k2 = [spread(par, 4 * c + k, band, cols) for c in range(3)]
        gam.append(g[0] * k0 + g[1] * k1 + g[2] * k2)
    queue = jnp.where(back, 0.0, -flow)

    def shade_back(z0, n, carry):
        run, part, last = carry
        out = Stores()
        rest = [[ref[z0 + i] for ref in (phis, bx, by, bz, gained, damped)] for i in range(n)]
        values = [smooth[z0 + i + 1, pl.ds(0, band)] for i in range(n)]
        edges = [edge[z0 + i] for i in range(n + 1)]
        for i in range(n):
            s = values[i]
            phi, dx, dy, dz, gain, damp = rest[i]
            near, far = edges[i], edges[i + 1]
            top = s * gam[3]
            inner = gam[2] + top
            outer = gam[1] + s * inner
            poly = gam[0] + s * outer
            slope = outer + s * (inner + top)
            h = poly + phi * poly
            mine = (near * h + run) * damp + gain * slope
            run = run + (near - far) * h
            az, ay, ax = dz * poly, dy * poly, dx * poly
            out.put(grads, z0 + i, part - az)
            part = mine + last
            part = part + (pltpu.roll(ay, 1, axis=0) - pltpu.roll(ay, band - 1, axis=0))
            part = part + (pltpu.roll(ax, 1, axis=1) - pltpu.roll(ax, cols - 1, axis=1))
            last = az
        out.flush()
        return run, part, last

    nil = jnp.zeros_like(through_me)
    in_groups(shade_back, depth + 2, group, (queue, nil, nil))


def smooth_transpose(band, depth, group, grads, emit):
    cols = grads.shape[2]

    def smooth_back(z0, n, carry):
        planes = [grads[z0 + i] for i in range(n + 2)]
        done = []
        for i in range(n):
            here = planes[i + 1]
            t = planes[i] + planes[i + 2] + 2.0 * here
            t = t + pltpu.roll(here, 1, axis=0) + pltpu.roll(here, band - 1, axis=0)
            t = t + pltpu.roll(here, 1, axis=1) + pltpu.roll(here, cols - 1, axis=1)
            done.append(t * 0.125)
            if len(done) == CHUNK:
                emit(z0 + i + 1 - CHUNK, done)
                done = []
        return carry

    in_groups(smooth_back, depth, group, 0, loop=band > 8)


def main_prepare_kernel(smooth, sig, smooth_tail, sig_tail, dxs, dys, rnorm, phis, edge, pixo, palette, par, *out):
    nz, rows, _ = dxs.shape
    nz = nz - 2
    smooth, sig = Joined(smooth, smooth_tail, nz), Joined(sig, sig_tail, nz - 1)
    prepare_block(rows, nz, GROUP_MAIN[2], smooth, dxs, dys, rnorm, phis, edge, sig, pixo, palette, par, *out)


def main_backward_kernel(smooth, smooth_tail, *refs):
    nz, rows = smooth.shape[0], refs[0].shape[1]
    backward_block(rows, nz, GROUP_MAIN[2], Joined(smooth, smooth_tail, nz), *refs)


def far_prepare_kernel(smooth, *refs):
    prepare_block(8, smooth.shape[0] - HALO, GROUP_FAR[2], smooth, *refs)


def main_result_kernel(grads, image, out, shown):
    nz, rows, _ = out.shape
    core, odd = where_am_i()
    shift = jnp.where(odd == 1, rows - 2, 2)
    for c in range(3):
        shown[c] = pltpu.roll(image[c], shift, axis=0)

    def emit(z0, values):
        values = [pltpu.roll(v, shift, axis=0) for v in values]
        for i, v in enumerate(values):
            out[local_plane(core, nz, z0 + i)] = v

    smooth_transpose(rows, nz, GROUP_MAIN[3], grads, emit)


def far_backward_kernel(*refs):
    res = refs[:13]
    near_grad, near_image, picture_h, out_h, image, grads, picture, out, sem = refs[13:]
    nz, rows, cols = out.shape
    size = CHUNK
    core, odd = where_am_i()
    shift = jnp.where(odd == 1, 2, rows - 2)
    row = lax.broadcasted_iota(jnp.int32, (rows, cols), 0)
    low = odd * (rows - 4)
    mask = (row >= low) & (row < low + 4)

    def emit(z0, values):
        for i in range(0, len(values), size):
            emit_chunk(z0 + i, values[i : i + size])

    def emit_chunk(z0, values):
        ats = [local_plane(core, nz, z0 + i) for i in range(len(values))]
        nears = [near_grad[at] for at in ats]
        both = [pltpu.roll(jnp.concatenate([v, v], axis=0), shift, axis=0) for v in values]
        both = [jnp.where(mask, b, v) for b, v in zip(both, nears)]
        for at, b in zip(ats, both):
            out[at] = b
        send(out, out_h, z0).start()

    def send(a, b, z0):
        at = pl.ds(jnp.where(core == 0, z0, nz - size - z0), size)
        return pltpu.make_async_copy(a.at[at], b.at[at], sem.at[z0 // size])

    backward_block(8, nz, GROUP_FAR[2], *res, image, grads)
    smooth_transpose(8, nz, GROUP_FAR[3], grads, emit)
    low = odd * (rows - 2)
    mask2 = (row >= low) & (row < low + 2)
    for c in range(3):
        both = pltpu.roll(jnp.concatenate([image[c], image[c]], axis=0), shift, axis=0)
        whole = jnp.where(mask2, both, near_image[c])
        picture[c] = jnp.where(core == 0, whole[:8], whole[8:])
    shown = pltpu.make_async_copy(picture, picture_h, sem.at[nz // size])
    shown.start()
    for z0 in range(0, nz, size):
        send(out, out_h, z0).wait()
    shown.wait()


def shards(density, absorption, view_dir, target_ids, palette, emission_coef, light):
    nz, rows, cols = density.shape
    tiles = lax.axis_size("tile")
    sds = resident
    dens = density

    zmsg, pix, pal, par = call(
        fetch_kernel,
        (sds(HALO, rows, cols), sds(PIX, rows, cols), sds(*palette.shape), sds(15, 8, 128)),
        (density, absorption, target_ids, view_dir, palette, emission_coef, light),
        [HBM] * 7,
        scratch=[
            pltpu.VMEM((rows, cols), jnp.int32),
            pltpu.SMEM(view_dir.shape, jnp.int32),
            pltpu.SMEM(emission_coef.shape, F32),
            pltpu.SMEM(light.shape, F32),
            pltpu.SemaphoreType.DMA((6 + HALO,)),
        ],
    )
    xmsg, lmsg = call(edges_kernel, (sds(nz + 2, HALO, cols), sds(nz + 2, HALO, cols)), (dens, pix), [VMEM] * 2)
    swap = [(0, 1), (1, 0)]
    near = [(i, i ^ 1) for i in range(tiles)]
    far = [(i, i + 1 if i % 2 else i - 1) for i in range(1, tiles - 1)]
    zrecv = lax.ppermute(zmsg, "depth", swap)
    xrecv = lax.ppermute(xmsg, "tile", near)
    lmsg = call(corner_kernel, sds(nz + 4, HALO, cols), (zrecv, lmsg), [VMEM, VMEM])
    lrecv = lax.ppermute(lmsg, "tile", far)
    xcorner = lax.ppermute(xrecv[:HALO], "depth", swap)

    def residuals(band):
        planes = nz + 2
        return (
            sds(nz + 4, band + 8, cols),
            *[sds(planes, band, cols)] * 4,
            sds(planes + 1, band, cols),
            sds(planes, band, cols),
            sds(4, band, cols),
            sds(PIX, band, cols),
        )

    parts = residuals(rows)
    smooth, taus, sig, pixo, total = call(
        main_smooth_kernel,
        (sds(nz, rows + 8, cols), sds(nz - 1, rows, cols), sds(nz - 1, rows, cols), parts[8], sds(rows, cols)),
        (dens, pix, xrecv),
        [VMEM] * 3,
    )
    xcorner, total = lax.optimization_barrier((xcorner, total))
    smooth_tail, sig_tail, dxs, dys, rnorm, phis, edge, mid = call(
        main_shade_kernel,
        (sds(4, rows + 8, cols), sds(3, rows, cols), *parts[1:6], parts[7]),
        (smooth, taus, sig, pixo, total, dens, pix, zrecv, xrecv, xcorner, par),
        [VMEM] * 11,
        scratch=[pltpu.VMEM((3, rows, cols), F32)],
    )
    theirs = lax.ppermute(mid, "depth", swap)

    def prepared(band):
        return (*[sds(nz + 2, band, cols)] * 5, sds(3, band, cols))

    ready = call(
        main_prepare_kernel,
        prepared(rows),
        (smooth, sig, smooth_tail, sig_tail, dxs, dys, rnorm, phis, edge, pixo, pal, par),
        [VMEM] * 12,
    )
    near_image, grads = call(
        main_backward_kernel,
        (sds(3, rows, cols), sds(nz + 2, rows, cols)),
        (smooth, smooth_tail, phis, edge, *ready, mid, pixo, theirs, par),
        [VMEM] * 14,
    )
    lrecv, near_image = lax.optimization_barrier((lrecv, near_image))
    smooth, dxs, dys, rnorm, phis, edge, sig, mid, pixo = call(
        far_forward_kernel,
        residuals(8),
        (dens, pix, zrecv, lrecv, par),
        [VMEM] * 5,
        scratch=[pltpu.VMEM((nz + 2, 8, cols), F32)],
    )
    theirs = lax.ppermute(mid, "depth", swap)
    near_image, pixo = lax.optimization_barrier((near_image, pixo))
    near_grad, near_image = call(main_result_kernel, (sds(nz, rows, cols), sds(3, rows, cols)), (grads, near_image), [VMEM] * 2)
    ready = call(
        far_prepare_kernel,
        prepared(8),
        (smooth, dxs, dys, rnorm, phis, edge, sig, pixo, pal, par),
        [VMEM] * 10,
    )
    picture, grad = call(
        far_backward_kernel,
        (jax.ShapeDtypeStruct((3, 8, cols), F32), jax.ShapeDtypeStruct((nz, rows, cols), F32)),
        (smooth, phis, edge, *ready, mid, pixo, theirs, par, near_grad, near_image),
        [VMEM] * 15,
        scratch=[
            pltpu.VMEM((3, 8, cols), F32),
            pltpu.VMEM((nz + 2, 8, cols), F32),
            pltpu.VMEM((3, 8, cols), F32),
            pltpu.VMEM((nz, rows, cols), F32),
            pltpu.SemaphoreType.DMA((nz // CHUNK + 1,)),
        ],
        out_specs=(HBM, HBM),
    )
    return picture, grad


def solution(mesh):
    placed = (P("depth", "tile", None), P("tile", None), P("tile"), P("tile", None), P(), P(), P())
    return jax.shard_map(
        shards,
        mesh=mesh,
        in_specs=placed,
        out_specs=(P(None, ("tile", "depth"), None), P("depth", "tile", None)),
        check_vma=False,
    )
```

```python
import jax
import jax.numpy as jnp
from jax import lax
from jax.experimental import pallas as pl
from jax.experimental.pallas import tpu as pltpu
from jax.sharding import PartitionSpec as P


F32 = jnp.float32
HALO = 4
PIX = 3
GROUP_MAIN = (10,16,17,16)
GROUP_FAR = (30,32,34,32)
CHUNK = 4
LATE = True
VMEM = pl.BlockSpec(memory_space=pltpu.VMEM)
HBM = pl.BlockSpec(memory_space=pl.ANY)


def call(kernel, outs, args, specs, scratch=(), cost=None, out_specs=None):
    args = [pltpu.with_memory_space_constraint(a, pltpu.VMEM if s is VMEM else pltpu.HBM) for a, s in zip(args, specs)]
    return pl.pallas_call(
        kernel,
        out_shape=outs,
        in_specs=specs,
        out_specs=out_specs or jax.tree.map(lambda _: VMEM, outs),
        scratch_shapes=scratch,
        cost_estimate=cost,
        compiler_params=pltpu.CompilerParams(vmem_limit_bytes=8 << 20),
    )(*args)


def resident(*shape):
    return pltpu.VMEM(shape, F32)


def where_am_i():
    return lax.axis_index("depth"), lax.rem(lax.axis_index("tile"), 2)


def local_plane(core, nz, z):
    return jnp.where(core == 0, z, nz - 1 - z)


def in_groups(body, count, group, carry, loop=False):
    full = count // group
    if loop:
        carry = lax.fori_loop(0, full, lambda i, c: body(i * group, group, c), carry)
    for i in range(0 if not loop else full, full):
        carry = body(i * group, group, carry)
    if count % group:
        carry = body(full * group, count % group, carry)
    return carry


class Joined:
    def __init__(self, head, tail, cut):
        self.head, self.tail, self.cut = head, tail, cut
        self.shape = (cut + tail.shape[0], *tail.shape[1:])

    def find(self, key):
        at, *rest = key if isinstance(key, tuple) else (key,)
        return (self.head, (at, *rest)) if at < self.cut else (self.tail, (at - self.cut, *rest))

    def __getitem__(self, key):
        ref, at = self.find(key)
        return ref[at]

    def __setitem__(self, key, value):
        ref, at = self.find(key)
        ref[at] = value


class Stores:
    def __init__(self):
        self.todo = []

    def put(self, ref, at, value):
        if LATE:
            self.todo.append((ref, at, value))
        else:
            ref[at] = value

    def flush(self):
        for ref, at, value in self.todo:
            ref[at] = value


def spread(par, i, rows, cols):
    t = par[i]
    t = jnp.concatenate([t] * (cols // t.shape[1]), axis=1)
    return jnp.concatenate([t] * (rows // t.shape[0]), axis=0)


def fetch_kernel(dens_h, absorb_h, ids_h, view_h, pal_h, coef_h, light_h, zmsg, pix, pal, par, ids, view, coef, light, sem):
    nz, rows, cols = dens_h.shape
    core, _ = where_am_i()
    seam = [(dens_h.at[local_plane(core, nz, nz - 1 - j)], zmsg.at[j]) for j in range(HALO)]
    pairs = (*seam, (view_h, view), (ids_h, ids), (absorb_h, pix.at[0]), (coef_h, coef), (light_h, light), (pal_h, pal))
    copies = [pltpu.make_async_copy(a, b, sem.at[i]) for i, (a, b) in enumerate(pairs)]
    for c in copies:
        c.start()
    for c in copies[HALO:]:
        c.wait()
    row = lax.broadcasted_iota(jnp.int32, (rows, cols), 0)
    seen = jnp.zeros((rows, cols), F32)
    for r in range(rows):
        seen = jnp.where(row == r, view[r].astype(F32), seen)
    pix[1] = ids[...].astype(F32)
    pix[2] = seen
    for i in range(3):
        for k in range(4):
            par[4 * i + k] = jnp.full(par.shape[1:], coef[i, k])
        value = light[i]
        if i == 0:
            value = jnp.where(core == 0, value, -value)
        par[12 + i] = jnp.full(par.shape[1:], value)
    for c in copies[:HALO]:
        c.wait()


def edges_kernel(dens, pix, xmsg, lmsg):
    nz, rows, _ = dens.shape
    core, odd = where_am_i()

    def edges(head, tail, to):
        xmsg[to] = jnp.where(odd == 1, head, tail)
        lmsg[to] = jnp.where(odd == 1, tail, head)

    a, ids, view = pix[0], pix[1], pix[2]
    edges(jnp.concatenate([a[:2], ids[:2]], axis=0), jnp.concatenate([ids[rows - 2 :], a[rows - 2 :]], axis=0), nz)
    edges(view[:HALO], view[rows - HALO :], nz + 1)
    for j in range(nz):
        plane = dens[local_plane(core, nz, nz - 1 - j)]
        edges(plane[:HALO], plane[rows - HALO :], j)


def corner_kernel(zrecv, early, lmsg):
    rows = zrecv.shape[1]
    _, odd = where_am_i()
    lmsg[2:] = early[...]
    one, two, three = zrecv[0], zrecv[1], zrecv[2]
    lmsg[1] = jnp.where(odd == 1, one[rows - HALO :], one[:HALO])
    tail = jnp.concatenate([three[rows - 1 :], two[rows - HALO + 1 :]], axis=0)
    head = jnp.concatenate([two[: HALO - 1], three[:1]], axis=0)
    lmsg[0] = jnp.where(odd == 1, tail, head)


def lookup(palette, ids):
    rows, cols = ids.shape
    entries = palette.shape[1]
    index = ids.astype(jnp.int32)
    parts = []
    for c in range(3):
        strips = []
        for r in range(0, rows, 8):
            strip = []
            for x in range(0, cols, entries):
                table = jnp.broadcast_to(palette[c : c + 1, :], (8, entries))
                strip.append(jnp.take_along_axis(table, index[r : r + 8, x : x + entries], axis=1))
            strips.append(jnp.concatenate(strip, axis=1))
        parts.append(jnp.concatenate(strips, axis=0))
    return parts


def pixel_rows(planes, z):
    if z == -1:
        return planes[0]
    if z == -2:
        return jnp.concatenate([planes[0][2:], planes[0][:2]], axis=0)
    return planes[1]


class Block:
    def __init__(self, band, shift, own, halo):
        self.band, self.shift, self.own, self.halo = band, shift, own, halo

    def plane(self, z):
        h = self.halo(z)
        return pltpu.roll(jnp.concatenate([self.own(z), h, h], axis=0), self.shift, axis=0)


def pixels(block, core):
    a, ids, view = [block.plane(-1 - j)[: block.band] for j in range(PIX)]
    back = jnp.where(core == 0, view, 1.0 - view)
    return a, ids, back


def smooth_planes(block, first, n, signed, depth, smooth, taus, softs, total, lead=None):
    band, wide = block.band, block.band + 8
    out = Stores()
    zs = [first - 1 + i for i in range(n + 2)]
    planes = [lead if i == 0 and lead is not None else block.plane(z) for i, z in enumerate(zs)]
    for i in range(n):
        here = planes[i + 1]
        cols = here.shape[1]
        t = planes[i] + planes[i + 2] + 2.0 * here
        t = t + pltpu.roll(here, 1, axis=0) + pltpu.roll(here, wide - 1, axis=0)
        t = t + pltpu.roll(here, 1, axis=1) + pltpu.roll(here, cols - 1, axis=1)
        s = t * 0.125
        out.put(smooth, zs[i + 1] + 1, s)
        static = isinstance(first, int)
        if not static or first + i < depth + 2:
            soft = jnp.log(1.0 + jnp.exp(s[:band]))
            tau = signed * soft
            out.put(taus, zs[i + 1], tau)
            out.put(softs, zs[i + 1], soft)
            if not static or first + i < depth:
                total = total + tau
    out.flush()
    return total


def smooth_slab(block, core, depth, group, smooth, taus, softs, pixo):
    a, ids, back = pixels(block, core)
    signed = a * (1.0 / (2 * depth)) * (1.0 - 2.0 * back)
    pixo[0], pixo[1], pixo[2] = a, ids, back
    face = block.plane(0)
    smooth[0] = face * 0.125
    zero = jnp.zeros_like(face)
    total = smooth_planes(block, 0, 1, signed, depth, smooth, taus, softs, jnp.zeros_like(a), lead=zero)

    def body(z, n, total):
        return smooth_planes(block, z + 1, n, signed, depth, smooth, taus, softs, total)

    return in_groups(body, depth - 2, group, total, loop=block.band > 8)


def smooth_seam(block, depth, smooth, taus, softs, pixo, total):
    a, back = pixo[0], pixo[2]
    signed = a * (1.0 / (2 * depth)) * (1.0 - 2.0 * back)
    return smooth_planes(block, depth - 1, 4, signed, depth, smooth, taus, softs, total)


def shade_slab(band, depth, group, total, par, smooth, taus, dxs, dys, rnorm, phis, edge, mid, pixo):
    wide, cols = band + 8, smooth.shape[2]
    back = pixo[2]
    sign = 1.0 - 2.0 * back
    lz, ly, lx = [spread(par, 12 + i, band, cols) for i in range(3)]
    start = jnp.where(back == 1.0, total, 0.0)
    opened = jnp.exp(start)
    edge[0] = opened

    def body(z0, n, carry):
        run, seen, m0, m1, m2, m3 = carry
        out = Stores()
        planes = [smooth[z0 + i] for i in range(n + 2)]
        absorbed = [taus[z0 + i] for i in range(n)]
        for i in range(n):
            here = planes[i + 1]
            s = here[:band]
            dz = planes[i + 2][:band] - planes[i][:band]
            dy = (pltpu.roll(here, wide - 1, axis=0) - pltpu.roll(here, 1, axis=0))[:band]
            dx = pltpu.roll(s, cols - 1, axis=1) - pltpu.roll(s, 1, axis=1)
            r = lax.rsqrt(4.0 + dz * dz + dy * dy + dx * dx)
            phi = (dz * lz + dy * ly + dx * lx) * r
            run = run - absorbed[i]
            nxt = jnp.exp(run)
            for ref, v in ((dxs, dx), (dys, dy), (rnorm, r), (phis, phi)):
                out.put(ref, z0 + i, v)
            out.put(edge, z0 + i + 1, nxt)
            b = (seen - nxt) * (1.0 + phi)
            m0 = m0 + b
            b = b * s
            m1 = m1 + b
            b = b * s
            m2 = m2 + b
            b = b * s
            m3 = m3 + b
            seen = nxt
        out.flush()
        return run, seen, m0, m1, m2, m3

    nil = jnp.zeros_like(back)
    carry = in_groups(body, depth, group, (start, opened, nil, nil, nil, nil))
    _, _, m0, m1, m2, m3 = carry
    half = 0.5 * sign
    mid[0] = sign * total
    for c in range(3):
        k0, k1, k2, k3 = [spread(par, 4 * c + k, band, cols) for k in range(4)]
        mid[1 + c] = half * (m0 * k0 + m1 * k1 + m2 * k2 + m3 * k3)
    body(depth, 2, carry)


def main_block(dens, pix, xrecv, zrecv=None, xcorner=None):
    nz, rows, _ = dens.shape
    core, odd = where_am_i()

    def own(z):
        if isinstance(z, int):
            if z < 0:
                return pix[-1 - z]
            if z >= nz:
                return zrecv[z - nz]
        return dens[local_plane(core, nz, z)]

    def halo(z):
        if isinstance(z, int):
            if z < 0:
                return pixel_rows((xrecv[nz], xrecv[nz + 1]), z)
            if z >= nz:
                return xcorner[z - nz]
        return xrecv[nz - 1 - z]

    return Block(rows, jnp.where(odd == 1, 2, rows + 8 - 2), own, halo)


def far_forward_kernel(dens, pix, zrecv, lrecv, par, smooth, dxs, dys, rnorm, phis, edge, softs, mid, pixo, taus):
    nz, rows, _ = dens.shape
    core, odd = where_am_i()
    at = pl.multiple_of(odd * (rows - 8), 8)

    def own(z):
        if isinstance(z, int):
            if z < 0:
                return pix[-1 - z, pl.ds(at, 8)]
            if z >= nz:
                return zrecv[z - nz, pl.ds(at, 8)]
        return dens[local_plane(core, nz, z), pl.ds(at, 8)]

    def halo(z):
        if isinstance(z, int):
            if z < 0:
                return pixel_rows((lrecv[nz + 2], lrecv[nz + 3]), z)
            if z == nz:
                return lrecv[1]
            if z > nz:
                plane = lrecv[0]
                if z != nz + 2:
                    return plane
                up = jnp.concatenate([plane[1:], plane[:1]], axis=0)
                return jnp.where(odd == 1, jnp.concatenate([plane[HALO - 1 :], plane[: HALO - 1]], axis=0), up)
        return lrecv[nz + 1 - z]

    block = Block(8, jnp.where(odd == 1, 16 - 2, 2), own, halo)
    total = smooth_slab(block, core, nz, GROUP_FAR[0], smooth, taus, softs, pixo)
    total = smooth_seam(block, nz, smooth, taus, softs, pixo, total)
    shade_slab(8, nz, GROUP_FAR[1], total, par, smooth, taus, dxs, dys, rnorm, phis, edge, mid, pixo)


def main_smooth_kernel(dens, pix, xrecv, smooth, taus, softs, pixo, total):
    core, _ = where_am_i()
    block = main_block(dens, pix, xrecv)
    total[...] = smooth_slab(block, core, dens.shape[0], GROUP_MAIN[0], smooth, taus, softs, pixo)


def main_shade_kernel(smooth, taus, softs, pixo, total, dens, pix, zrecv, xrecv, xcorner, par, smooth_tail, softs_tail, dxs, dys, rnorm, phis, edge, mid, taus_tail):
    nz, rows, _ = dens.shape
    block = main_block(dens, pix, xrecv, zrecv, xcorner)
    smooth, taus, softs = Joined(smooth, smooth_tail, nz), Joined(taus, taus_tail, nz - 1), Joined(softs, softs_tail, nz - 1)
    whole = smooth_seam(block, nz, smooth, taus, softs, pixo, total[...])
    shade_slab(rows, nz, GROUP_MAIN[1], whole, par, smooth, taus, dxs, dys, rnorm, phis, edge, mid, pixo)


def prepare_block(band, depth, group, smooth, dxs, dys, rnorm, phis, edge, softs, pixo, palette, par, bx, by, bz, gained, damped, targets):
    cols = smooth.shape[2]
    sign = 1.0 - 2.0 * pixo[2]
    weight = pixo[0] * (1.0 / (2 * depth))
    lz, ly, lx = [spread(par, 12 + i, band, cols) for i in range(3)]
    for c, t in enumerate(lookup(palette, pixo[1])):
        targets[c] = t

    def body(z0, n, carry):
        out = Stores()
        planes = [smooth[z0 + i, pl.ds(0, band)] for i in range(n + 2)]
        edges = [edge[z0 + i] for i in range(n + 1)]
        rest = [(phis[z0 + i], rnorm[z0 + i], softs[z0 + i], dys[z0 + i], dxs[z0 + i]) for i in range(n)]
        for i in range(n):
            phi, r, sg, dy, dx = rest[i]
            dz = planes[i + 2] - planes[i]
            w = sign * (edges[i] - edges[i + 1])
            p = w * r
            q = p * (phi * r)
            out.put(bx, z0 + i, p * lx - q * dx)
            out.put(by, z0 + i, p * ly - q * dy)
            out.put(bz, z0 + i, p * lz - q * dz)
            out.put(gained, z0 + i, w * (1.0 + phi))
            out.put(damped, z0 + i, weight - weight * jnp.exp(-sg))
        out.flush()
        return carry

    in_groups(body, depth + 2, group, 0)


def backward_block(band, depth, group, smooth, phis, edge, bx, by, bz, gained, damped, targets, mid, pixo, theirs, par, image, grads):
    cols = smooth.shape[2]
    back = pixo[2] == 1.0
    through_me, through_them = jnp.exp(-mid[0]), jnp.exp(-theirs[0])
    g, flow = [], jnp.zeros_like(through_me)
    for c in range(3):
        mine, other = mid[1 + c], theirs[1 + c]
        pic = jnp.where(back, other + through_them * mine, mine + through_me * other)
        image[c] = pic
        err = (pic - targets[c]) * (2.0 * depth)
        g.append(err)
        flow = flow + err * pic
    kappa = jnp.where(back, 0.5 * through_them, 0.5)
    g = [kappa * e for e in g]
    gam = []
    for k in range(4):
        k0, k1, k2 = [spread(par, 4 * c + k, band, cols) for c in range(3)]
        gam.append(g[0] * k0 + g[1] * k1 + g[2] * k2)
    queue = jnp.where(back, 0.0, -flow)

    def shade_back(z0, n, carry):
        run, part, last = carry
        out = Stores()
        rest = [[ref[z0 + i] for ref in (phis, bx, by, bz, gained, damped)] for i in range(n)]
        values = [smooth[z0 + i + 1, pl.ds(0, band)] for i in range(n)]
        edges = [edge[z0 + i] for i in range(n + 1)]
        for i in range(n):
            s = values[i]
            phi, dx, dy, dz, gain, damp = rest[i]
            near, far = edges[i], edges[i + 1]
            top = s * gam[3]
            inner = gam[2] + top
            outer = gam[1] + s * inner
            poly = gam[0] + s * outer
            slope = outer + s * (inner + top)
            h = poly + phi * poly
            mine = (near * h + run) * damp + gain * slope
            run = run + (near - far) * h
            az, ay, ax = dz * poly, dy * poly, dx * poly
            out.put(grads, z0 + i, part - az)
            part = mine + last
            part = part + (pltpu.roll(ay, 1, axis=0) - pltpu.roll(ay, band - 1, axis=0))
            part = part + (pltpu.roll(ax, 1, axis=1) - pltpu.roll(ax, cols - 1, axis=1))
            last = az
        out.flush()
        return run, part, last

    nil = jnp.zeros_like(through_me)
    in_groups(shade_back, depth + 2, group, (queue, nil, nil))


def smooth_transpose(band, depth, group, grads, emit):
    cols = grads.shape[2]

    def smooth_back(z0, n, carry):
        planes = [grads[z0 + i] for i in range(n + 2)]
        done = []
        for i in range(n):
            here = planes[i + 1]
            t = planes[i] + planes[i + 2] + 2.0 * here
            t = t + pltpu.roll(here, 1, axis=0) + pltpu.roll(here, band - 1, axis=0)
            t = t + pltpu.roll(here, 1, axis=1) + pltpu.roll(here, cols - 1, axis=1)
            done.append(t * 0.125)
            if len(done) == CHUNK:
                emit(z0 + i + 1 - CHUNK, done)
                done = []
        return carry

    in_groups(smooth_back, depth, group, 0, loop=band > 8)


def main_prepare_kernel(smooth, softs, smooth_tail, softs_tail, dxs, dys, rnorm, phis, edge, pixo, palette, par, *out):
    nz, rows, _ = dxs.shape
    nz = nz - 2
    smooth, softs = Joined(smooth, smooth_tail, nz), Joined(softs, softs_tail, nz - 1)
    prepare_block(rows, nz, GROUP_MAIN[2], smooth, dxs, dys, rnorm, phis, edge, softs, pixo, palette, par, *out)


def main_backward_kernel(smooth, smooth_tail, *refs):
    nz, rows = smooth.shape[0], refs[0].shape[1]
    backward_block(rows, nz, GROUP_MAIN[2], Joined(smooth, smooth_tail, nz), *refs)


def far_prepare_kernel(smooth, *refs):
    prepare_block(8, smooth.shape[0] - HALO, GROUP_FAR[2], smooth, *refs)


def main_result_kernel(grads, image, out, shown):
    nz, rows, _ = out.shape
    core, odd = where_am_i()
    shift = jnp.where(odd == 1, rows - 2, 2)
    for c in range(3):
        shown[c] = pltpu.roll(image[c], shift, axis=0)

    def emit(z0, values):
        values = [pltpu.roll(v, shift, axis=0) for v in values]
        for i, v in enumerate(values):
            out[local_plane(core, nz, z0 + i)] = v

    smooth_transpose(rows, nz, GROUP_MAIN[3], grads, emit)


def far_backward_kernel(*refs):
    res = refs[:13]
    near_grad, near_image, picture_h, out_h, image, grads, picture, out, sem = refs[13:]
    nz, rows, cols = out.shape
    size = CHUNK
    core, odd = where_am_i()
    shift = jnp.where(odd == 1, 2, rows - 2)
    row = lax.broadcasted_iota(jnp.int32, (rows, cols), 0)
    low = odd * (rows - 4)
    mask = (row >= low) & (row < low + 4)

    def emit(z0, values):
        for i in range(0, len(values), size):
            emit_chunk(z0 + i, values[i : i + size])

    def emit_chunk(z0, values):
        ats = [local_plane(core, nz, z0 + i) for i in range(len(values))]
        nears = [near_grad[at] for at in ats]
        both = [pltpu.roll(jnp.concatenate([v, v], axis=0), shift, axis=0) for v in values]
        both = [jnp.where(mask, b, v) for b, v in zip(both, nears)]
        for at, b in zip(ats, both):
            out[at] = b
        send(out, out_h, z0).start()

    def send(a, b, z0):
        at = pl.ds(jnp.where(core == 0, z0, nz - size - z0), size)
        return pltpu.make_async_copy(a.at[at], b.at[at], sem.at[z0 // size])

    backward_block(8, nz, GROUP_FAR[2], *res, image, grads)
    smooth_transpose(8, nz, GROUP_FAR[3], grads, emit)
    low = odd * (rows - 2)
    mask2 = (row >= low) & (row < low + 2)
    for c in range(3):
        both = pltpu.roll(jnp.concatenate([image[c], image[c]], axis=0), shift, axis=0)
        whole = jnp.where(mask2, both, near_image[c])
        picture[c] = jnp.where(core == 0, whole[:8], whole[8:])
    shown = pltpu.make_async_copy(picture, picture_h, sem.at[nz // size])
    shown.start()
    for z0 in range(0, nz, size):
        send(out, out_h, z0).wait()
    shown.wait()


def shards(density, absorption, view_dir, target_ids, palette, emission_coef, light):
    nz, rows, cols = density.shape
    tiles = lax.axis_size("tile")
    sds = resident
    dens = density

    zmsg, pix, pal, par = call(
        fetch_kernel,
        (sds(HALO, rows, cols), sds(PIX, rows, cols), sds(*palette.shape), sds(15, 8, 128)),
        (density, absorption, target_ids, view_dir, palette, emission_coef, light),
        [HBM] * 7,
        scratch=[
            pltpu.VMEM((rows, cols), jnp.int32),
            pltpu.SMEM(view_dir.shape, jnp.int32),
            pltpu.SMEM(emission_coef.shape, F32),
            pltpu.SMEM(light.shape, F32),
            pltpu.SemaphoreType.DMA((6 + HALO,)),
        ],
    )
    xmsg, lmsg = call(edges_kernel, (sds(nz + 2, HALO, cols), sds(nz + 2, HALO, cols)), (dens, pix), [VMEM] * 2)
    swap = [(0, 1), (1, 0)]
    near = [(i, i ^ 1) for i in range(tiles)]
    far = [(i, i + 1 if i % 2 else i - 1) for i in range(1, tiles - 1)]
    zrecv = lax.ppermute(zmsg, "depth", swap)
    xrecv = lax.ppermute(xmsg, "tile", near)
    lmsg = call(corner_kernel, sds(nz + 4, HALO, cols), (zrecv, lmsg), [VMEM, VMEM])
    lrecv = lax.ppermute(lmsg, "tile", far)
    xcorner = lax.ppermute(xrecv[:HALO], "depth", swap)

    def residuals(band):
        planes = nz + 2
        return (
            sds(nz + 4, band + 8, cols),
            *[sds(planes, band, cols)] * 4,
            sds(planes + 1, band, cols),
            sds(planes, band, cols),
            sds(4, band, cols),
            sds(PIX, band, cols),
        )

    parts = residuals(rows)
    smooth, taus, softs, pixo, total = call(
        main_smooth_kernel,
        (sds(nz, rows + 8, cols), sds(nz - 1, rows, cols), sds(nz - 1, rows, cols), parts[8], sds(rows, cols)),
        (dens, pix, xrecv),
        [VMEM] * 3,
    )
    xcorner, total = lax.optimization_barrier((xcorner, total))
    smooth_tail, softs_tail, dxs, dys, rnorm, phis, edge, mid = call(
        main_shade_kernel,
        (sds(4, rows + 8, cols), sds(3, rows, cols), *parts[1:6], parts[7]),
        (smooth, taus, softs, pixo, total, dens, pix, zrecv, xrecv, xcorner, par),
        [VMEM] * 11,
        scratch=[pltpu.VMEM((3, rows, cols), F32)],
    )
    theirs = lax.ppermute(mid, "depth", swap)

    def prepared(band):
        return (*[sds(nz + 2, band, cols)] * 5, sds(3, band, cols))

    ready = call(
        main_prepare_kernel,
        prepared(rows),
        (smooth, softs, smooth_tail, softs_tail, dxs, dys, rnorm, phis, edge, pixo, pal, par),
        [VMEM] * 12,
    )
    near_image, grads = call(
        main_backward_kernel,
        (sds(3, rows, cols), sds(nz + 2, rows, cols)),
        (smooth, smooth_tail, phis, edge, *ready, mid, pixo, theirs, par),
        [VMEM] * 14,
    )
    lrecv, near_image = lax.optimization_barrier((lrecv, near_image))
    smooth, dxs, dys, rnorm, phis, edge, softs, mid, pixo = call(
        far_forward_kernel,
        residuals(8),
        (dens, pix, zrecv, lrecv, par),
        [VMEM] * 5,
        scratch=[pltpu.VMEM((nz + 2, 8, cols), F32)],
    )
    theirs = lax.ppermute(mid, "depth", swap)
    near_image, pixo = lax.optimization_barrier((near_image, pixo))
    near_grad, near_image = call(main_result_kernel, (sds(nz, rows, cols), sds(3, rows, cols)), (grads, near_image), [VMEM] * 2)
    ready = call(
        far_prepare_kernel,
        prepared(8),
        (smooth, dxs, dys, rnorm, phis, edge, softs, pixo, pal, par),
        [VMEM] * 10,
    )
    picture, grad = call(
        far_backward_kernel,
        (jax.ShapeDtypeStruct((3, 8, cols), F32), jax.ShapeDtypeStruct((nz, rows, cols), F32)),
        (smooth, phis, edge, *ready, mid, pixo, theirs, par, near_grad, near_image),
        [VMEM] * 15,
        scratch=[
            pltpu.VMEM((3, 8, cols), F32),
            pltpu.VMEM((nz + 2, 8, cols), F32),
            pltpu.VMEM((3, 8, cols), F32),
            pltpu.VMEM((nz, rows, cols), F32),
            pltpu.SemaphoreType.DMA((nz // CHUNK + 1,)),
        ],
        out_specs=(HBM, HBM),
    )
    return picture, grad


def solution(mesh):
    placed = (P("depth", "tile", None), P("tile", None), P("tile"), P("tile", None), P(), P(), P())
    return jax.shard_map(
        shards,
        mesh=mesh,
        in_specs=placed,
        out_specs=(P(None, ("tile", "depth"), None), P("depth", "tile", None)),
        check_vma=False,
    )
```

```python
import jax
import jax.numpy as jnp
from jax import lax
from jax.experimental import pallas as pl
from jax.experimental.pallas import tpu as pltpu
from jax.sharding import PartitionSpec as P


F32 = jnp.float32
HALO = 4
PIX = 3
GROUP_MAIN = (10,16,17,16)
GROUP_FAR = (30,32,34,32)
CHUNK = 8
LATE = True
VMEM = pl.BlockSpec(memory_space=pltpu.VMEM)
HBM = pl.BlockSpec(memory_space=pl.ANY)


def call(kernel, outs, args, specs, scratch=(), cost=None, out_specs=None):
    args = [pltpu.with_memory_space_constraint(a, pltpu.VMEM if s is VMEM else pltpu.HBM) for a, s in zip(args, specs)]
    return pl.pallas_call(
        kernel,
        out_shape=outs,
        in_specs=specs,
        out_specs=out_specs or jax.tree.map(lambda _: VMEM, outs),
        scratch_shapes=scratch,
        cost_estimate=cost,
        compiler_params=pltpu.CompilerParams(vmem_limit_bytes=8 << 20),
    )(*args)


def resident(*shape):
    return pltpu.VMEM(shape, F32)


def where_am_i():
    return lax.axis_index("depth"), lax.rem(lax.axis_index("tile"), 2)


def local_plane(core, nz, z):
    return jnp.where(core == 0, z, nz - 1 - z)


def in_groups(body, count, group, carry, loop=False):
    full = count // group
    if loop:
        carry = lax.fori_loop(0, full, lambda i, c: body(i * group, group, c), carry)
    for i in range(0 if not loop else full, full):
        carry = body(i * group, group, carry)
    if count % group:
        carry = body(full * group, count % group, carry)
    return carry


class Joined:
    def __init__(self, head, tail, cut):
        self.head, self.tail, self.cut = head, tail, cut
        self.shape = (cut + tail.shape[0], *tail.shape[1:])

    def find(self, key):
        at, *rest = key if isinstance(key, tuple) else (key,)
        return (self.head, (at, *rest)) if at < self.cut else (self.tail, (at - self.cut, *rest))

    def __getitem__(self, key):
        ref, at = self.find(key)
        return ref[at]

    def __setitem__(self, key, value):
        ref, at = self.find(key)
        ref[at] = value


class Stores:
    def __init__(self):
        self.todo = []

    def put(self, ref, at, value):
        if LATE:
            self.todo.append((ref, at, value))
        else:
            ref[at] = value

    def flush(self):
        for ref, at, value in self.todo:
            ref[at] = value


def spread(par, i, rows, cols):
    t = par[i]
    t = jnp.concatenate([t] * (cols // t.shape[1]), axis=1)
    return jnp.concatenate([t] * (rows // t.shape[0]), axis=0)


def fetch_kernel(dens_h, absorb_h, ids_h, view_h, pal_h, coef_h, light_h, zmsg, pix, pal, par, ids, view, coef, light, sem):
    nz, rows, cols = dens_h.shape
    core, _ = where_am_i()
    seam = [(dens_h.at[local_plane(core, nz, nz - 1 - j)], zmsg.at[j]) for j in range(HALO)]
    pairs = (*seam, (view_h, view), (ids_h, ids), (absorb_h, pix.at[0]), (coef_h, coef), (light_h, light), (pal_h, pal))
    copies = [pltpu.make_async_copy(a, b, sem.at[i]) for i, (a, b) in enumerate(pairs)]
    for c in copies:
        c.start()
    for c in copies[HALO:]:
        c.wait()
    row = lax.broadcasted_iota(jnp.int32, (rows, cols), 0)
    seen = jnp.zeros((rows, cols), F32)
    for r in range(rows):
        seen = jnp.where(row == r, view[r].astype(F32), seen)
    pix[1] = ids[...].astype(F32)
    pix[2] = seen
    for i in range(3):
        for k in range(4):
            par[4 * i + k] = jnp.full(par.shape[1:], coef[i, k])
        value = light[i]
        if i == 0:
            value = jnp.where(core == 0, value, -value)
        par[12 + i] = jnp.full(par.shape[1:], value)
    for c in copies[:HALO]:
        c.wait()


def edges_kernel(dens, pix, xmsg, lmsg):
    nz, rows, _ = dens.shape
    core, odd = where_am_i()

    def edges(head, tail, to):
        xmsg[to] = jnp.where(odd == 1, head, tail)
        lmsg[to] = jnp.where(odd == 1, tail, head)

    a, ids, view = pix[0], pix[1], pix[2]
    edges(jnp.concatenate([a[:2], ids[:2]], axis=0), jnp.concatenate([ids[rows - 2 :], a[rows - 2 :]], axis=0), nz)
    edges(view[:HALO], view[rows - HALO :], nz + 1)
    for j in range(nz):
        plane = dens[local_plane(core, nz, nz - 1 - j)]
        edges(plane[:HALO], plane[rows - HALO :], j)


def corner_kernel(zrecv, early, lmsg):
    rows = zrecv.shape[1]
    _, odd = where_am_i()
    lmsg[2:] = early[...]
    one, two, three = zrecv[0], zrecv[1], zrecv[2]
    lmsg[1] = jnp.where(odd == 1, one[rows - HALO :], one[:HALO])
    tail = jnp.concatenate([three[rows - 1 :], two[rows - HALO + 1 :]], axis=0)
    head = jnp.concatenate([two[: HALO - 1], three[:1]], axis=0)
    lmsg[0] = jnp.where(odd == 1, tail, head)


def lookup(palette, ids):
    rows, cols = ids.shape
    entries = palette.shape[1]
    index = ids.astype(jnp.int32)
    parts = []
    for c in range(3):
        strips = []
        for r in range(0, rows, 8):
            strip = []
            for x in range(0, cols, entries):
                table = jnp.broadcast_to(palette[c : c + 1, :], (8, entries))
                strip.append(jnp.take_along_axis(table, index[r : r + 8, x : x + entries], axis=1))
            strips.append(jnp.concatenate(strip, axis=1))
        parts.append(jnp.concatenate(strips, axis=0))
    return parts


def pixel_rows(planes, z):
    if z == -1:
        return planes[0]
    if z == -2:
        return jnp.concatenate([planes[0][2:], planes[0][:2]], axis=0)
    return planes[1]


class Block:
    def __init__(self, band, shift, own, halo):
        self.band, self.shift, self.own, self.halo = band, shift, own, halo

    def plane(self, z):
        h = self.halo(z)
        return pltpu.roll(jnp.concatenate([self.own(z), h, h], axis=0), self.shift, axis=0)


def pixels(block, core):
    a, ids, view = [block.plane(-1 - j)[: block.band] for j in range(PIX)]
    back = jnp.where(core == 0, view, 1.0 - view)
    return a, ids, back


def smooth_planes(block, first, n, signed, depth, smooth, taus, sig, total, lead=None):
    band, wide = block.band, block.band + 8
    out = Stores()
    zs = [first - 1 + i for i in range(n + 2)]
    planes = [lead if i == 0 and lead is not None else block.plane(z) for i, z in enumerate(zs)]
    for i in range(n):
        here = planes[i + 1]
        cols = here.shape[1]
        t = planes[i] + planes[i + 2] + 2.0 * here
        t = t + pltpu.roll(here, 1, axis=0) + pltpu.roll(here, wide - 1, axis=0)
        t = t + pltpu.roll(here, 1, axis=1) + pltpu.roll(here, cols - 1, axis=1)
        s = t * 0.125
        out.put(smooth, zs[i + 1] + 1, s)
        static = isinstance(first, int)
        if not static or first + i < depth + 2:
            soft = jnp.log(1.0 + jnp.exp(s[:band]))
            tau = signed * soft
            out.put(taus, zs[i + 1], tau)
            out.put(sig, zs[i + 1], 1.0 - jnp.exp(-soft))
            if not static or first + i < depth:
                total = total + tau
    out.flush()
    return total


def smooth_slab(block, core, depth, group, smooth, taus, sig, pixo):
    a, ids, back = pixels(block, core)
    signed = a * (1.0 / (2 * depth)) * (1.0 - 2.0 * back)
    pixo[0], pixo[1], pixo[2] = a, ids, back
    face = block.plane(0)
    smooth[0] = face * 0.125
    zero = jnp.zeros_like(face)
    total = smooth_planes(block, 0, 1, signed, depth, smooth, taus, sig, jnp.zeros_like(a), lead=zero)

    def body(z, n, total):
        return smooth_planes(block, z + 1, n, signed, depth, smooth, taus, sig, total)

    return in_groups(body, depth - 2, group, total, loop=block.band > 8)


def smooth_seam(block, depth, smooth, taus, sig, pixo, total):
    a, back = pixo[0], pixo[2]
    signed = a * (1.0 / (2 * depth)) * (1.0 - 2.0 * back)
    return smooth_planes(block, depth - 1, 4, signed, depth, smooth, taus, sig, total)


def shade_slab(band, depth, group, total, par, smooth, taus, dxs, dys, rnorm, phis, edge, mid, pixo):
    wide, cols = band + 8, smooth.shape[2]
    back = pixo[2]
    sign = 1.0 - 2.0 * back
    lz, ly, lx = [spread(par, 12 + i, band, cols) for i in range(3)]
    start = jnp.where(back == 1.0, total, 0.0)
    opened = jnp.exp(start)
    edge[0] = opened

    def body(z0, n, carry):
        run, seen, m0, m1, m2, m3 = carry
        out = Stores()
        planes = [smooth[z0 + i] for i in range(n + 2)]
        absorbed = [taus[z0 + i] for i in range(n)]
        for i in range(n):
            here = planes[i + 1]
            s = here[:band]
            dz = planes[i + 2][:band] - planes[i][:band]
            dy = (pltpu.roll(here, wide - 1, axis=0) - pltpu.roll(here, 1, axis=0))[:band]
            dx = pltpu.roll(s, cols - 1, axis=1) - pltpu.roll(s, 1, axis=1)
            r = lax.rsqrt(4.0 + dz * dz + dy * dy + dx * dx)
            phi = (dz * lz + dy * ly + dx * lx) * r
            run = run - absorbed[i]
            nxt = jnp.exp(run)
            for ref, v in ((dxs, dx), (dys, dy), (rnorm, r), (phis, phi)):
                out.put(ref, z0 + i, v)
            out.put(edge, z0 + i + 1, nxt)
            b = (seen - nxt) * (1.0 + phi)
            m0 = m0 + b
            b = b * s
            m1 = m1 + b
            b = b * s
            m2 = m2 + b
            b = b * s
            m3 = m3 + b
            seen = nxt
        out.flush()
        return run, seen, m0, m1, m2, m3

    nil = jnp.zeros_like(back)
    carry = in_groups(body, depth, group, (start, opened, nil, nil, nil, nil))
    _, _, m0, m1, m2, m3 = carry
    half = 0.5 * sign
    mid[0] = sign * total
    for c in range(3):
        k0, k1, k2, k3 = [spread(par, 4 * c + k, band, cols) for k in range(4)]
        mid[1 + c] = half * (m0 * k0 + m1 * k1 + m2 * k2 + m3 * k3)
    body(depth, 2, carry)


def main_block(dens, pix, xrecv, zrecv=None, xcorner=None):
    nz, rows, _ = dens.shape
    core, odd = where_am_i()

    def own(z):
        if isinstance(z, int):
            if z < 0:
                return pix[-1 - z]
            if z >= nz:
                return zrecv[z - nz]
        return dens[local_plane(core, nz, z)]

    def halo(z):
        if isinstance(z, int):
            if z < 0:
                return pixel_rows((xrecv[nz], xrecv[nz + 1]), z)
            if z >= nz:
                return xcorner[z - nz]
        return xrecv[nz - 1 - z]

    return Block(rows, jnp.where(odd == 1, 2, rows + 8 - 2), own, halo)


def far_forward_kernel(dens, pix, zrecv, lrecv, par, smooth, dxs, dys, rnorm, phis, edge, sig, mid, pixo, taus):
    nz, rows, _ = dens.shape
    core, odd = where_am_i()
    at = pl.multiple_of(odd * (rows - 8), 8)

    def own(z):
        if isinstance(z, int):
            if z < 0:
                return pix[-1 - z, pl.ds(at, 8)]
            if z >= nz:
                return zrecv[z - nz, pl.ds(at, 8)]
        return dens[local_plane(core, nz, z), pl.ds(at, 8)]

    def halo(z):
        if isinstance(z, int):
            if z < 0:
                return pixel_rows((lrecv[nz + 2], lrecv[nz + 3]), z)
            if z == nz:
                return lrecv[1]
            if z > nz:
                plane = lrecv[0]
                if z != nz + 2:
                    return plane
                up = jnp.concatenate([plane[1:], plane[:1]], axis=0)
                return jnp.where(odd == 1, jnp.concatenate([plane[HALO - 1 :], plane[: HALO - 1]], axis=0), up)
        return lrecv[nz + 1 - z]

    block = Block(8, jnp.where(odd == 1, 16 - 2, 2), own, halo)
    total = smooth_slab(block, core, nz, GROUP_FAR[0], smooth, taus, sig, pixo)
    total = smooth_seam(block, nz, smooth, taus, sig, pixo, total)
    shade_slab(8, nz, GROUP_FAR[1], total, par, smooth, taus, dxs, dys, rnorm, phis, edge, mid, pixo)


def main_smooth_kernel(dens, pix, xrecv, smooth, taus, sig, pixo, total):
    core, _ = where_am_i()
    block = main_block(dens, pix, xrecv)
    total[...] = smooth_slab(block, core, dens.shape[0], GROUP_MAIN[0], smooth, taus, sig, pixo)


def main_shade_kernel(smooth, taus, sig, pixo, total, dens, pix, zrecv, xrecv, xcorner, par, smooth_tail, sig_tail, dxs, dys, rnorm, phis, edge, mid, taus_tail):
    nz, rows, _ = dens.shape
    block = main_block(dens, pix, xrecv, zrecv, xcorner)
    smooth, taus, sig = Joined(smooth, smooth_tail, nz), Joined(taus, taus_tail, nz - 1), Joined(sig, sig_tail, nz - 1)
    whole = smooth_seam(block, nz, smooth, taus, sig, pixo, total[...])
    shade_slab(rows, nz, GROUP_MAIN[1], whole, par, smooth, taus, dxs, dys, rnorm, phis, edge, mid, pixo)


def prepare_block(band, depth, group, smooth, dxs, dys, rnorm, phis, edge, sig, pixo, palette, par, bx, by, bz, gained, damped, targets):
    cols = smooth.shape[2]
    sign = 1.0 - 2.0 * pixo[2]
    weight = pixo[0] * (1.0 / (2 * depth))
    lz, ly, lx = [spread(par, 12 + i, band, cols) for i in range(3)]
    for c, t in enumerate(lookup(palette, pixo[1])):
        targets[c] = t

    def body(z0, n, carry):
        out = Stores()
        planes = [smooth[z0 + i, pl.ds(0, band)] for i in range(n + 2)]
        edges = [edge[z0 + i] for i in range(n + 1)]
        rest = [(phis[z0 + i], rnorm[z0 + i], sig[z0 + i], dys[z0 + i], dxs[z0 + i]) for i in range(n)]
        for i in range(n):
            phi, r, sg, dy, dx = rest[i]
            dz = planes[i + 2] - planes[i]
            w = sign * (edges[i] - edges[i + 1])
            p = w * r
            q = p * (phi * r)
            out.put(bx, z0 + i, p * lx - q * dx)
            out.put(by, z0 + i, p * ly - q * dy)
            out.put(bz, z0 + i, p * lz - q * dz)
            out.put(gained, z0 + i, w * (1.0 + phi))
            out.put(damped, z0 + i, weight * sg)
        out.flush()
        return carry

    in_groups(body, depth + 2, group, 0)


def combine(band, depth, targets, mid, pixo, theirs, par, image):
    cols = mid.shape[2]
    back = pixo[2] == 1.0
    through_me, through_them = jnp.exp(-mid[0]), jnp.exp(-theirs[0])
    g, flow = [], jnp.zeros_like(through_me)
    for c in range(3):
        mine, other = mid[1 + c], theirs[1 + c]
        pic = jnp.where(back, other + through_them * mine, mine + through_me * other)
        image[c] = pic
        err = (pic - targets[c]) * (2.0 * depth)
        g.append(err)
        flow = flow + err * pic
    kappa = jnp.where(back, 0.5 * through_them, 0.5)
    g = [kappa * e for e in g]
    gam = []
    for k in range(4):
        k0, k1, k2 = [spread(par, 4 * c + k, band, cols) for c in range(3)]
        gam.append(g[0] * k0 + g[1] * k1 + g[2] * k2)
    queue = jnp.where(back, 0.0, -flow)

    nil = jnp.zeros_like(through_me)
    return gam, (queue, nil, nil)


def shade_transpose(band, first, count, group, gam, carry, smooth, phis, edge, bx, by, bz, gained, damped, grads):
    cols = bx.shape[2]

    def shade_back(z0, n, carry):
        run, part, last = carry
        out = Stores()
        rest = [[ref[z0 + i] for ref in (phis, bx, by, bz, gained, damped)] for i in range(n)]
        values = [smooth[z0 + i + 1, pl.ds(0, band)] for i in range(n)]
        edges = [edge[z0 + i] for i in range(n + 1)]
        for i in range(n):
            s = values[i]
            phi, dx, dy, dz, gain, damp = rest[i]
            near, far = edges[i], edges[i + 1]
            top = s * gam[3]
            inner = gam[2] + top
            outer = gam[1] + s * inner
            poly = gam[0] + s * outer
            slope = outer + s * (inner + top)
            h = poly + phi * poly
            mine = (near * h + run) * damp + gain * slope
            run = run + (near - far) * h
            az, ay, ax = dz * poly, dy * poly, dx * poly
            out.put(grads, z0 + i, part - az)
            part = mine + last
            part = part + (pltpu.roll(ay, 1, axis=0) - pltpu.roll(ay, band - 1, axis=0))
            part = part + (pltpu.roll(ax, 1, axis=1) - pltpu.roll(ax, cols - 1, axis=1))
            last = az
        out.flush()
        return run, part, last

    def step(z0, n, carry):
        return shade_back(first + z0, n, carry)

    return in_groups(step, count, group, carry)


def smooth_transpose(band, depth, group, grads, emit):
    cols = grads.shape[2]

    def smooth_back(z0, n, carry):
        planes = [grads[z0 + i] for i in range(n + 2)]
        done = []
        for i in range(n):
            here = planes[i + 1]
            t = planes[i] + planes[i + 2] + 2.0 * here
            t = t + pltpu.roll(here, 1, axis=0) + pltpu.roll(here, band - 1, axis=0)
            t = t + pltpu.roll(here, 1, axis=1) + pltpu.roll(here, cols - 1, axis=1)
            done.append(t * 0.125)
            if len(done) == CHUNK:
                emit(z0 + i + 1 - CHUNK, done)
                done = []
        return carry

    in_groups(smooth_back, depth, group, 0)


def main_prepare_kernel(smooth, sig, smooth_tail, sig_tail, dxs, dys, rnorm, phis, edge, pixo, palette, par, *out):
    nz, rows, _ = dxs.shape
    nz = nz - 2
    smooth, sig = Joined(smooth, smooth_tail, nz), Joined(sig, sig_tail, nz - 1)
    prepare_block(rows, nz, GROUP_MAIN[2], smooth, dxs, dys, rnorm, phis, edge, sig, pixo, palette, par, *out)


def main_backward_kernel(smooth, phis, edge, bx, by, bz, gained, damped, targets, mid, pixo, theirs, par, image, grads, state):
    rows = image.shape[1]
    nz = phis.shape[0] - 2
    gam, carry = combine(rows, nz, targets, mid, pixo, theirs, par, image)
    carry = shade_transpose(rows, 0, grads.shape[0], grads.shape[0], gam, carry, smooth, phis, edge, bx, by, bz, gained, damped, grads)
    for i, v in enumerate((*gam, *carry)):
        state[i] = v


def far_prepare_kernel(smooth, *refs):
    prepare_block(8, smooth.shape[0] - HALO, GROUP_FAR[2], smooth, *refs)


def main_result_kernel(state, early, smooth, smooth_tail, phis, edge, bx, by, bz, gained, damped, image, out, shown, late):
    nz, rows, _ = out.shape
    core, odd = where_am_i()
    shift = jnp.where(odd == 1, rows - 2, 2)
    for c in range(3):
        shown[c] = pltpu.roll(image[c], shift, axis=0)

    def emit(z0, values):
        values = [pltpu.roll(v, shift, axis=0) for v in values]
        for i, v in enumerate(values):
            out[local_plane(core, nz, z0 + i)] = v

    first = early.shape[0]
    smooth = Joined(smooth, smooth_tail, nz)
    gam, carry = [state[i] for i in range(4)], tuple(state[4 + i] for i in range(3))
    grads = Joined(early, late, first)
    shade_transpose(rows, first, nz + 2 - first, nz + 2 - first, gam, carry, smooth, phis, edge, bx, by, bz, gained, damped, grads)
    smooth_transpose(rows, nz, GROUP_MAIN[3], grads, emit)


def far_backward_kernel(*refs):
    res = refs[:13]
    near_grad, near_image, picture_h, out_h, image, grads, picture, out, sem = refs[13:]
    nz, rows, cols = out.shape
    size = CHUNK
    core, odd = where_am_i()
    shift = jnp.where(odd == 1, 2, rows - 2)
    row = lax.broadcasted_iota(jnp.int32, (rows, cols), 0)
    low = odd * (rows - 4)
    mask = (row >= low) & (row < low + 4)

    def emit(z0, values):
        for i in range(0, len(values), size):
            emit_chunk(z0 + i, values[i : i + size])

    def emit_chunk(z0, values):
        ats = [local_plane(core, nz, z0 + i) for i in range(len(values))]
        nears = [near_grad[at] for at in ats]
        both = [pltpu.roll(jnp.concatenate([v, v], axis=0), shift, axis=0) for v in values]
        both = [jnp.where(mask, b, v) for b, v in zip(both, nears)]
        for at, b in zip(ats, both):
            out[at] = b
        send(out, out_h, z0).start()

    def send(a, b, z0):
        at = pl.ds(jnp.where(core == 0, z0, nz - size - z0), size)
        return pltpu.make_async_copy(a.at[at], b.at[at], sem.at[z0 // size])

    smooth, phis, edge, bx, by, bz, gained, damped, targets, mid, pixo, theirs, par = res
    gam, carry = combine(8, nz, targets, mid, pixo, theirs, par, image)
    shade_transpose(8, 0, nz + 2, GROUP_FAR[2], gam, carry, smooth, phis, edge, bx, by, bz, gained, damped, grads)
    smooth_transpose(8, nz, GROUP_FAR[3], grads, emit)
    low = odd * (rows - 2)
    mask2 = (row >= low) & (row < low + 2)
    for c in range(3):
        both = pltpu.roll(jnp.concatenate([image[c], image[c]], axis=0), shift, axis=0)
        whole = jnp.where(mask2, both, near_image[c])
        picture[c] = jnp.where(core == 0, whole[:8], whole[8:])
    shown = pltpu.make_async_copy(picture, picture_h, sem.at[nz // size])
    shown.start()
    for z0 in range(0, nz, size):
        send(out, out_h, z0).wait()
    shown.wait()


def shards(density, absorption, view_dir, target_ids, palette, emission_coef, light):
    nz, rows, cols = density.shape
    tiles = lax.axis_size("tile")
    sds = resident
    dens = density

    zmsg, pix, pal, par = call(
        fetch_kernel,
        (sds(HALO, rows, cols), sds(PIX, rows, cols), sds(*palette.shape), sds(15, 8, 128)),
        (density, absorption, target_ids, view_dir, palette, emission_coef, light),
        [HBM] * 7,
        scratch=[
            pltpu.VMEM((rows, cols), jnp.int32),
            pltpu.SMEM(view_dir.shape, jnp.int32),
            pltpu.SMEM(emission_coef.shape, F32),
            pltpu.SMEM(light.shape, F32),
            pltpu.SemaphoreType.DMA((6 + HALO,)),
        ],
    )
    xmsg, lmsg = call(edges_kernel, (sds(nz + 2, HALO, cols), sds(nz + 2, HALO, cols)), (dens, pix), [VMEM] * 2)
    swap = [(0, 1), (1, 0)]
    near = [(i, i ^ 1) for i in range(tiles)]
    far = [(i, i + 1 if i % 2 else i - 1) for i in range(1, tiles - 1)]
    zrecv = lax.ppermute(zmsg, "depth", swap)
    xrecv = lax.ppermute(xmsg, "tile", near)
    lmsg = call(corner_kernel, sds(nz + 4, HALO, cols), (zrecv, lmsg), [VMEM, VMEM])
    lrecv = lax.ppermute(lmsg, "tile", far)
    xcorner = lax.ppermute(xrecv[:HALO], "depth", swap)

    def residuals(band):
        planes = nz + 2
        return (
            sds(nz + 4, band + 8, cols),
            *[sds(planes, band, cols)] * 4,
            sds(planes + 1, band, cols),
            sds(planes, band, cols),
            sds(4, band, cols),
            sds(PIX, band, cols),
        )

    parts = residuals(rows)
    smooth, taus, sig, pixo, total = call(
        main_smooth_kernel,
        (sds(nz, rows + 8, cols), sds(nz - 1, rows, cols), sds(nz - 1, rows, cols), parts[8], sds(rows, cols)),
        (dens, pix, xrecv),
        [VMEM] * 3,
    )
    xcorner, total = lax.optimization_barrier((xcorner, total))
    smooth_tail, sig_tail, dxs, dys, rnorm, phis, edge, mid = call(
        main_shade_kernel,
        (sds(4, rows + 8, cols), sds(3, rows, cols), *parts[1:6], parts[7]),
        (smooth, taus, sig, pixo, total, dens, pix, zrecv, xrecv, xcorner, par),
        [VMEM] * 11,
        scratch=[pltpu.VMEM((3, rows, cols), F32)],
    )
    theirs = lax.ppermute(mid, "depth", swap)

    def prepared(band):
        return (*[sds(nz + 2, band, cols)] * 5, sds(3, band, cols))

    ready = call(
        main_prepare_kernel,
        prepared(rows),
        (smooth, sig, smooth_tail, sig_tail, dxs, dys, rnorm, phis, edge, pixo, pal, par),
        [VMEM] * 12,
    )
    half = nz // 2 + 1
    near_image, early, state = call(
        main_backward_kernel,
        (sds(3, rows, cols), sds(half, rows, cols), sds(7, rows, cols)),
        (smooth, phis, edge, *ready, mid, pixo, theirs, par),
        [VMEM] * 13,
    )
    main = (early, smooth, smooth_tail, phis, edge, *ready[:5])
    lrecv, near_image = lax.optimization_barrier((lrecv, near_image))
    smooth, dxs, dys, rnorm, phis, edge, sig, mid, pixo = call(
        far_forward_kernel,
        residuals(8),
        (dens, pix, zrecv, lrecv, par),
        [VMEM] * 5,
        scratch=[pltpu.VMEM((nz + 2, 8, cols), F32)],
    )
    theirs = lax.ppermute(mid, "depth", swap)
    near_image, state, pixo = lax.optimization_barrier((near_image, state, pixo))
    near_grad, near_image = call(
        main_result_kernel,
        (sds(nz, rows, cols), sds(3, rows, cols)),
        (state, *main, near_image),
        [VMEM] * 12,
        scratch=[pltpu.VMEM((nz + 2 - half, rows, cols), F32)],
    )
    ready = call(
        far_prepare_kernel,
        prepared(8),
        (smooth, dxs, dys, rnorm, phis, edge, sig, pixo, pal, par),
        [VMEM] * 10,
    )
    picture, grad = call(
        far_backward_kernel,
        (jax.ShapeDtypeStruct((3, 8, cols), F32), jax.ShapeDtypeStruct((nz, rows, cols), F32)),
        (smooth, phis, edge, *ready, mid, pixo, theirs, par, near_grad, near_image),
        [VMEM] * 15,
        scratch=[
            pltpu.VMEM((3, 8, cols), F32),
            pltpu.VMEM((nz + 2, 8, cols), F32),
            pltpu.VMEM((3, 8, cols), F32),
            pltpu.VMEM((nz, rows, cols), F32),
            pltpu.SemaphoreType.DMA((nz // CHUNK + 1,)),
        ],
        out_specs=(HBM, HBM),
    )
    return picture, grad


def solution(mesh):
    placed = (P("depth", "tile", None), P("tile", None), P("tile"), P("tile", None), P(), P(), P())
    return jax.shard_map(
        shards,
        mesh=mesh,
        in_specs=placed,
        out_specs=(P(None, ("tile", "depth"), None), P("depth", "tile", None)),
        check_vma=False,
    )
```
